32 devices in a mesh: dp: 8 (over y, x, core), seq: 4 (over z).
Axes of the slice: x: 2, y: 2, z: 4, core: 2. Of those that a mesh axis runs over, the one named last changes fastest.
Arguments:
- hidden_in: bfloat16 [2, 8, 512, 768], P(None, 'dp', 'seq'), may hold values from -6 to 6
- boxes: int32 [2, 2, 8, 512], P(None, None, 'dp', 'seq'), may hold values from 0 to 999
- lengths: int32 [2, 8], P(None, 'dp'), may hold values from 64 to 512, as said below
- w_query: bfloat16 [768, 768], replicated, may hold values from -0.21875 to 0.21875
- w_key: bfloat16 [768, 768], replicated, may hold values from -0.21875 to 0.21875
- w_value: bfloat16 [768, 768], replicated, may hold values from -0.21875 to 0.21875
- w_out: bfloat16 [768, 768], replicated, may hold values from -1.75 to 1.75
- w_rel: bfloat16 [768, 768], replicated, may hold values from -0.21875 to 0.21875
- w_up: bfloat16 [768, 3072], replicated, may hold values from -0.21875 to 0.21875
- b_up: bfloat16 [3072], replicated, may hold values from -3 to 3
- w_down: bfloat16 [3072, 768], replicated, may hold values from -0.109375 to 0.109375
- gain_attn: bfloat16 [768], replicated, may hold values from 0.5 to 1.5
- bias_attn: bfloat16 [768], replicated, may hold values from -2 to 2
- gain_ffn: bfloat16 [768], replicated, may hold values from 0.5 to 1.5
- bias_ffn: bfloat16 [768], replicated, may hold values from -2 to 2
- cotangent: bfloat16 [2, 8, 512, 768], P(None, 'dp', 'seq'), may hold values from -6 to 6
Outputs:
- hidden_out: bfloat16 [2, 8, 512, 768], P(None, 'dp', 'seq')
- input_grad: bfloat16 [2, 8, 512, 768], P(None, 'dp', 'seq')
- grad_w_query: float32 [768, 768], P('dp')
- grad_w_key: float32 [768, 768], P('dp')
- grad_w_value: float32 [768, 768], P('dp')
- grad_w_out: float32 [768, 768], P('dp')
- grad_w_rel: float32 [768, 768], P('dp')
- grad_w_up: float32 [768, 3072], P('dp')
- grad_b_up: float32 [3072], P('dp')
- grad_w_down: float32 [3072, 768], P('dp')
- grad_gain_attn: float32 [768], P('dp')
- grad_bias_attn: float32 [768], P('dp')
- grad_gain_ffn: float32 [768], P('dp')
- grad_bias_ffn: float32 [768], P('dp')
The draws below stay inside these ranges and needn't reach their ends.
Inputs may be any that keep to these rules, and one draw needn't show every extreme that they name: `lengths`: live tokens of each page; slots at or after it are padding; the first page of each micro-batch is full. `boxes`: quantized box centre coordinates.
All inputs are finite; a program needn't handle non-finite values.
Results may differ from the reference program's by a relative error of at most 0.018.
Values may be sent and summed in bfloat16 or wider, within the bound.
A program may use at most 192 MiB of HBM per device.

```python
import jax
import jax.numpy as jnp
from jax import lax

D = 768
HEADS = 12
FF = 3072
REL = 768
LEN = 512
MB = 2
PAGES = 8


def draw_lengths(key, part):
    raw_draw = jax.random.randint(key, (MB, PAGES), 0, LEN)
    cubed = raw_draw * raw_draw // LEN * raw_draw // LEN
    page_sizes = LEN - cubed * 7 // 8
    first_page = jnp.arange(PAGES)[None, :] == 0
    return jnp.where(first_page, LEN, page_sizes).astype(jnp.int32)


def place_ends(result, stream_key, least, largest):
    longest = result.shape.index(max(result.shape))
    spots = []
    for shift in (0, 1):
        where = [jax.random.randint(jax.random.fold_in(stream_key, axis), (), 0, length) for axis, length in enumerate(result.shape)]
        where[longest] = (where[longest] + shift) % result.shape[longest]
        spots.append(tuple(where))
    return result.at[spots[0]].set(least).at[spots[1]].set(largest)


def shard_levels(rng, shape, split, low, top_value):
    gain, own = 1.0, jax.random.fold_in(rng, 6)
    for dim, parts in split:
        heights = jnp.exp(jax.random.uniform(jax.random.fold_in(own, dim), (parts,), jnp.float32, low / len(split), top_value / len(split)))
        gain = gain * jnp.repeat(heights, shape[dim] // parts).reshape([-1 if axis == dim else 1 for axis in range(len(shape))])
    return gain


def noise(stream_key, extent, scale, limit, shards=(), kind=jnp.bfloat16):
    values = scale * jax.random.normal(stream_key, extent, jnp.float32)
    if shards:
        values = values * shard_levels(stream_key, extent, shards, -0.22, 0.18)
    return jnp.clip(values, -limit, limit).astype(kind)


def setup_inputs(seed: int = 0) -> dict:
    key_list = jax.random.split(jax.random.key(seed), 17)
    return {
        "hidden_in": noise(key_list[0], (MB, PAGES, LEN, D), 1.0, 6.0, ((1, 8), (2, 4))),
        "boxes": place_ends(jax.random.randint(key_list[1], (2, MB, PAGES, LEN), 0, 1000), jax.random.fold_in(key_list[1], 1), 0, 999).astype(jnp.int32),
        "lengths": draw_lengths(jax.random.fold_in(key_list[16], 71), 0),
        "w_query": noise(key_list[3], (D, D), D ** -0.5, 0.21875),
        "w_key": noise(key_list[4], (D, D), D ** -0.5, 0.21875),
        "w_value": noise(key_list[5], (D, D), D ** -0.5, 0.21875),
        "w_out": noise(key_list[6], (D, D), (D // 64) ** -0.5, 1.75),
        "w_rel": noise(key_list[7], (REL, D), D ** -0.5, 0.21875),
        "w_up": noise(key_list[8], (D, FF), D ** -0.5, 0.21875),
        "b_up": noise(key_list[9], (FF,), 0.5, 3.0),
        "w_down": noise(key_list[10], (FF, D), FF ** -0.5, 0.109375),
        "gain_attn": jnp.clip(1.0 + 0.1 * jax.random.normal(key_list[11], (D,), jnp.float32), 0.5, 1.5).astype(jnp.bfloat16),
        "bias_attn": noise(key_list[12], (D,), 0.3, 2.0),
        "gain_ffn": jnp.clip(1.0 + 0.1 * jax.random.normal(key_list[13], (D,), jnp.float32), 0.5, 1.5).astype(jnp.bfloat16),
        "bias_ffn": noise(key_list[14], (D,), 0.3, 2.0),
        "cotangent": noise(key_list[15], (MB, PAGES, LEN, D), 1.0, 6.0, ((1, 8), (2, 4))),
    }


highest = lax.Precision.HIGHEST
norm_epsilon = 1e-05

@jax.custom_vjp
def low(v):
    return lax.optimization_barrier(v.astype(jnp.bfloat16)).astype(jnp.float32)

@jax.custom_vjp
def low_back(v):
    return v

def low_keep(v):
    return (low(v), None)

def low_pass(kept, grad):
    return (grad,)

def back_keep(v):
    return (v, None)

def back_low(kept, grad):
    return (low(grad),)
low.defvjp(low_keep, low_pass)
low_back.defvjp(back_keep, back_low)

def layer_norm(row_block, gain_vec, shift_vec):
    center = row_block - lax.optimization_barrier(jnp.mean(row_block, axis=-1, keepdims=True))
    spread = lax.optimization_barrier(jnp.mean(center * center, axis=-1, keepdims=True))
    return center * lax.rsqrt(spread + norm_epsilon) * gain_vec + shift_vec

def sines(coords, freq_count):
    frequency = 10000.0 ** (-jnp.arange(freq_count, dtype=jnp.float32) / freq_count)
    angles = coords.astype(jnp.float32)[..., None] * frequency
    return (jnp.sin(angles), jnp.cos(angles))

def rotate(rel_in, sine_x, cosine_x, sine_y, cosine_y):
    quarter = sine_x.shape[-1]
    part_one = rel_in[..., 0:quarter]
    part_two = rel_in[..., quarter:2 * quarter]
    part_three = rel_in[..., 2 * quarter:3 * quarter]
    part_four = rel_in[..., 3 * quarter:4 * quarter]
    return jnp.concatenate([part_one * sine_x + part_two * cosine_x, part_two * sine_x - part_one * cosine_x, part_three * sine_y + part_four * cosine_y, part_four * sine_y - part_three * cosine_y], axis=-1)

def page_layer(params, page_x, page_box, page_len):
    query_weight, key_weight, value_weight, out_weight, rel_weight, up_weight, up_bias, down_weight, gain_one, bias_one, gain_two, bias_two = params
    seq_len, model_width = page_x.shape
    head_dim = model_width // HEADS
    query_rows = low(low_back(jnp.dot(page_x, query_weight, precision=highest)))
    key_rows = low(low_back(jnp.dot(page_x, key_weight, precision=highest)))
    value_rows = low(low_back(jnp.dot(page_x, value_weight, precision=highest)))
    query_heads = query_rows.reshape(seq_len, HEADS, head_dim)
    key_heads = key_rows.reshape(seq_len, HEADS, head_dim)
    value_heads = value_rows.reshape(seq_len, HEADS, head_dim)
    rel_heads = rel_weight.reshape(REL, HEADS, head_dim)
    rel_proj = low_back(jnp.einsum('ihe,che->ihc', query_heads, rel_heads, precision=highest))
    sine_x, cosine_x = sines(page_box[0], REL // 4)
    sine_y, cosine_y = sines(page_box[1], REL // 4)
    rel_query = low(rotate(rel_proj, sine_x[:, None, :], cosine_x[:, None, :], sine_y[:, None, :], cosine_y[:, None, :]))
    key_feat = low(jnp.concatenate([cosine_x, sine_x, cosine_y, sine_y], axis=-1))
    score_scale = head_dim ** (-0.5)
    logits = (jnp.einsum('ihe,jhe->hij', query_heads, key_heads, precision=highest) + jnp.einsum('ihc,jc->hij', rel_query, key_feat, precision=highest)) * score_scale
    live_keys = jnp.arange(seq_len) < page_len
    logits = low_back(jnp.where(live_keys[None, None, :], logits, -1e+30))
    attention_probs = jax.nn.softmax(logits, axis=-1)
    attended = jnp.einsum('hij,jhe->ihe', low(attention_probs), value_heads, precision=highest).reshape(seq_len, model_width)
    attended = low(low_back(attended))
    branch = low_back(jnp.dot(attended, out_weight, precision=highest))
    normed = layer_norm(page_x + branch, gain_one, bias_one)
    up_proj = low_back(jnp.dot(low(normed), up_weight, precision=highest) + up_bias)
    activated = low(jax.nn.gelu(up_proj, approximate=False))
    down_proj = low_back(jnp.dot(activated, down_weight, precision=highest))
    return layer_norm(normed + down_proj, gain_two, bias_two)

def reference(hidden_in, boxes, lengths, w_query, w_key, w_value, w_out, w_rel, w_up, b_up, w_down, gain_attn, bias_attn, gain_ffn, bias_ffn, cotangent):
    params = tuple((item.astype(jnp.float32) for item in (w_query, w_key, w_value, w_out, w_rel, w_up, b_up, w_down, gain_attn, bias_attn, gain_ffn, bias_ffn)))
    page_total = MB * PAGES
    page_inputs = hidden_in.astype(jnp.float32).reshape(page_total, LEN, D)
    page_boxes = jnp.moveaxis(boxes.reshape(2, page_total, LEN), 0, 1)
    page_lengths = lengths.reshape(page_total)

    def whole(weights_in, inputs_in):

        def page_step(page_item):
            return page_layer(weights_in, page_item[0], page_item[1], page_item[2])
        return lax.map(jax.checkpoint(page_step), (inputs_in, page_boxes, page_lengths))
    page_outputs, pull_back = jax.vjp(whole, params, page_inputs)
    weight_grads, input_grad = pull_back(cotangent.astype(jnp.float32).reshape(page_total, LEN, D))
    return (page_outputs.reshape(hidden_in.shape).astype(jnp.bfloat16), input_grad.reshape(hidden_in.shape).astype(jnp.bfloat16), weight_grads[0], weight_grads[1], weight_grads[2], weight_grads[3], weight_grads[4], weight_grads[5], weight_grads[6], weight_grads[7], weight_grads[8], weight_grads[9], weight_grads[10], weight_grads[11])
```

```python
import functools

import jax
import jax.numpy as jnp
import numpy as np
from jax import lax
from jax.experimental import pallas as pl
from jax.experimental.pallas import tpu as pltpu
from jax.sharding import PartitionSpec as P

HEADS = 12
EPS = 1e-05
BF = jnp.bfloat16
F32 = jnp.float32
PAIRS = HEADS // 2
VMEM_LIMIT = 67043328


def nn(a, b):
    return lax.dot_general(a, b, (((1,), (0,)), ((), ())), preferred_element_type=F32)


def nt(a, b):
    return lax.dot_general(a, b, (((1,), (1,)), ((), ())), preferred_element_type=F32)


def tn(a, b):
    return lax.dot_general(a, b, (((0,), (0,)), ((), ())), preferred_element_type=F32)


def trig_tables(quarter):
    freq = 10000.0 ** (-np.arange(quarter) / quarter)
    tables = []
    for step in (32.0, 1.0):
        angle = step * np.arange(32)[:, None] * freq[None, :]
        rest = np.concatenate([np.sin(angle), np.cos(angle)], axis=1).astype(np.float32)
        parts = []
        for _ in range(3):
            part = rest.astype(BF)
            parts.append(part)
            rest = rest - part.astype(np.float32)
        tables.append(np.concatenate(parts, axis=0))
    return tables


def features(bx_ref, hi_ref, lo_ref, sin_ref, cos_ref, feat_ref):
    quarter = hi_ref.shape[1] // 2
    half = 2 * quarter
    iota = lax.broadcasted_iota(jnp.int32, (32, 128), 0)
    hi_tab, lo_tab = hi_ref[...], lo_ref[...]
    for slot in range(4):
        sines, cosines = [], []
        for axis in range(2):
            where = bx_ref[slot, axis : axis + 1, :]
            pick_hi = (iota == lax.shift_right_logical(where, 5)).astype(F32).astype(BF)
            pick_lo = (iota == (where & 31)).astype(F32).astype(BF)
            hi = tn(jnp.concatenate([pick_hi] * 3, axis=0), hi_tab)
            lo = tn(jnp.concatenate([pick_lo] * 3, axis=0), lo_tab)
            sin_hi, cos_hi = hi[:, :quarter], hi[:, quarter:]
            sin_lo, cos_lo = lo[:, :quarter], lo[:, quarter:]
            sines.append(sin_hi * cos_lo + cos_hi * sin_lo)
            cosines.append(cos_hi * cos_lo - sin_hi * sin_lo)
        sine = jnp.concatenate(sines, axis=1)
        cosine = jnp.concatenate(cosines, axis=1)
        rows = pl.ds(128 * slot, 128)
        feat_ref[rows, 0:half] = cosine.astype(BF)
        feat_ref[rows, half : 2 * half] = sine.astype(BF)
        if slot < 2:
            sin_ref[rows, :] = sine
            cos_ref[rows, :] = cosine


def head_stack(pair):
    first = lax.broadcasted_iota(jnp.int32, pair.shape, 1) < 64
    zero = jnp.zeros_like(pair)
    return jnp.concatenate([jnp.where(first, pair, zero), jnp.where(first, zero, pair)], axis=0)


def head_join(stack):
    half = stack.shape[0] // 2
    first = lax.broadcasted_iota(jnp.int32, (half, 128), 1) < 64
    return jnp.where(first, stack[:half], stack[half:])


def attend_pair(pair, live, r):
    cols = pl.ds(pl.multiple_of(128 * pair, 128), 128)
    stack = head_stack(r.q[:, cols].astype(F32) * 0.125).astype(BF)
    sine, cosine = r.sine, r.cosine
    for head in range(2):
        rows = slice(256 * head, 256 * head + 256)
        left = nt(stack[rows], r.wr[0:384, cols])
        right = nt(stack[rows], r.wr[384:768, cols])
        sin, cos = sine[...], cosine[...]
        r.relq[rows, 0:384] = (left * sin + right * cos).astype(BF)
        r.relq[rows, 384:768] = (right * sin - left * cos).astype(BF)
    r.relq[:, 768:896] = stack
    r.feat[:, 768:896] = r.k[:, cols]
    r.score[...] = nt(r.relq[...], r.feat[...])

    for block in range(8):
        rows = pl.ds(64 * block, 64)
        score = jnp.where(live, r.score[rows, :], -1e30)
        top = jnp.max(score, axis=-1, keepdims=True)
        weight = jnp.exp(score - top)
        total = jnp.sum(weight, axis=-1, keepdims=True)
        r.probs[pair, rows, :] = (weight * (1.0 / total)).astype(BF)
    r.att[:, cols] = head_join(nn(r.probs[pair], r.v[:, cols])).astype(BF)


def attend_pair_back(pair, r):
    cols = pl.ds(pl.multiple_of(128 * pair, 128), 128)
    given = head_stack(r.datt[:, cols].astype(F32)).astype(BF)
    stack = head_stack(r.q[:, cols].astype(F32)).astype(BF)
    r.score[...] = nt(given, r.v[:, cols])

    for block in range(8):
        rows = pl.ds(64 * block, 64)
        prob = r.probs[pair, rows, :].astype(F32)
        push = prob * r.score[rows, :]
        mean = jnp.sum(push, axis=-1, keepdims=True)
        r.dlog[rows, :] = ((push - prob * mean) * 0.125).astype(BF)
    r.dv[:, cols] = tn(r.probs[pair], given).astype(BF)
    r.dk[:, cols] = tn(r.dlog[...], stack).astype(BF)
    r.feat[:, 768:896] = r.k[:, cols]
    for head in range(2):
        rows = slice(256 * head, 256 * head + 256)
        first = nn(r.dlog[rows, :], r.feat[:, 0:384])
        second = nn(r.dlog[rows, :], r.feat[:, 384:768])
        sin, cos = r.sine[...], r.cosine[...]
        r.relq[rows, 0:384] = (first * sin - second * cos).astype(BF)
        r.relq[rows, 384:768] = (first * cos + second * sin).astype(BF)
    dq = nn(r.dlog[...], r.feat[:, 768:896]) + nn(r.relq[:, 0:768], r.wr[:, cols])
    r.dq[:, cols] = head_join(dq).astype(BF)
    part = tn(r.relq[:, 0:768], stack).astype(BF)
    for piece, share in enumerate((0, 1, 4, 5, 2, 3, 6, 7)):
        r.g[share % 2, share // 2, 864:960, cols] = part[96 * piece : 96 * piece + 96]


def norm_back(given, hat, scale, gain):
    push = given * gain
    mean = jnp.mean(push, axis=-1, keepdims=True)
    lean = jnp.mean(push * hat, axis=-1, keepdims=True)
    return scale * (push - mean - hat * lean)


def put_shares(g_ref, base, cols, part):
    for share in range(8):
        g_ref[share % 2, share // 2, base : base + 96, cols] = part[
            96 * share : 96 * share + 96
        ].astype(BF)


class Refs:
    pass


def layer_kernel(names, *refs):
    r = Refs()
    for name, ref in zip(names, refs):
        setattr(r, name, ref)
    z = r.info[0]
    length = r.info[1]
    quarter = 192
    for dst, src in ((0, 0), (192, 384), (384, 192), (576, 576)):
        r.wr[dst : dst + 192, :] = r.w_rel[src : src + 192, :]
    features(r.bx, r.hi, r.lo, r.sine, r.cosine, r.feat)

    for tile in range(3):
        cols = slice(256 * tile, 256 * tile + 256)
        r.q[:, cols] = nn(r.x[0:256, :], r.w_query[:, cols]).astype(BF)
        r.k[:, cols] = nn(r.x[...], r.w_key[:, cols]).astype(BF)
        r.v[:, cols] = nn(r.x[...], r.w_value[:, cols]).astype(BF)

    lane = lax.broadcasted_iota(jnp.int32, (1, 128), 1)
    live = jnp.concatenate(
        [lane + 128 * block < length for block in (z, 3 - z, z + 1 - 2 * (z % 2), (z + 2) % 4)],
        axis=1,
    )

    def attend(pair, carry):
        attend_pair(pair, live, r)
        return carry

    lax.fori_loop(0, PAIRS, attend, 0)

    for tile in range(3):
        cols = slice(256 * tile, 256 * tile + 256)
        r.res[:, cols] = r.x[0:256, cols].astype(F32) + nn(r.att[...], r.w_out[:, cols])

    gain1, bias1 = r.gain_attn[...].astype(F32), r.bias_attn[...].astype(F32)
    gain2, bias2 = r.gain_ffn[...].astype(F32), r.bias_ffn[...].astype(F32)
    for block in range(4):
        rows = slice(64 * block, 64 * block + 64)
        res = r.res[rows, :]
        center = res - jnp.mean(res, axis=-1, keepdims=True)
        scale = lax.rsqrt(jnp.mean(center * center, axis=-1, keepdims=True) + EPS)
        hat = center * scale
        r.hat[rows, :] = hat
        r.scale[rows, :] = jnp.broadcast_to(scale, (64, 128))
        normed = hat * gain1 + bias1
        r.res[rows, :] = normed
        r.low[rows, :] = normed.astype(BF)

    def up(tile, carry):
        cols = pl.ds(pl.multiple_of(256 * tile, 256), 256)
        value = nn(r.low[...], r.w_up[:, cols]) + r.b_up[:, cols].astype(F32)
        below = 0.5 * (1.0 + lax.erf(value * np.float32(np.sqrt(0.5))))
        dense = jnp.exp(value * value * -0.5) * np.float32(1.0 / np.sqrt(2.0 * np.pi))
        r.act[:, cols] = (value * below).astype(BF)
        r.slope[:, cols] = below + value * dense
        return carry

    lax.fori_loop(0, 12, up, 0)
    for tile in range(3):
        cols = slice(256 * tile, 256 * tile + 256)
        r.res[:, cols] = r.res[:, cols] + nn(r.act[...], r.w_down[:, cols])

    sums = [jnp.zeros((1, 768), F32) for _ in range(4)]
    for block in range(4):
        rows = slice(64 * block, 64 * block + 64)
        res = r.res[rows, :]
        center = res - jnp.mean(res, axis=-1, keepdims=True)
        scale = lax.rsqrt(jnp.mean(center * center, axis=-1, keepdims=True) + EPS)
        hat = center * scale
        r.out[rows, :] = (hat * gain2 + bias2).astype(BF)
        given = r.cot[rows, :].astype(F32)
        sums[2] = sums[2] + jnp.sum(given * hat, axis=0, keepdims=True)
        sums[3] = sums[3] + jnp.sum(given, axis=0, keepdims=True)
        dres = norm_back(given, hat, scale, gain2)
        r.res[rows, :] = dres
        r.dlow[rows, :] = dres.astype(BF)

    def up_back(tile, carry):
        cols = pl.ds(pl.multiple_of(256 * tile, 256), 256)
        push = nt(r.dlow[...], r.w_down[cols, :]) * r.slope[:, cols]
        low = push.astype(BF)
        r.dup[:, cols] = low
        r.upsum[:, cols] = jnp.sum(low.astype(F32), axis=0, keepdims=True)
        return carry

    lax.fori_loop(0, 12, up_back, 0)
    for row in range(4):
        r.small[row : row + 1, :] = r.upsum[:, 768 * row : 768 * row + 768]

    def grad_down(share, carry):
        cols = pl.ds(pl.multiple_of(384 * share, 128), 384)
        r.g[share % 2, share // 2, 384:768, :] = tn(r.act[:, cols], r.dlow[...]).astype(BF)
        return carry

    lax.fori_loop(0, 8, grad_down, 0)

    def grad_up(tile, carry):
        cols = pl.ds(pl.multiple_of(256 * tile, 256), 256)
        part = tn(r.low[...], r.dup[:, cols])
        base = pl.multiple_of(96 * (tile // 3), 32)
        dest = pl.ds(pl.multiple_of(256 * (tile % 3), 256), 256)
        for share in range(8):
            r.g[share % 2, share // 2, pl.ds(base, 96), dest] = part[
                96 * share : 96 * share + 96
            ].astype(BF)
        return carry

    lax.fori_loop(0, 12, grad_up, 0)
    for tile in range(3):
        cols = slice(256 * tile, 256 * tile + 256)
        r.res[:, cols] = r.res[:, cols] + nt(r.dup[...], r.w_up[cols, :])
    for block in range(4):
        rows = slice(64 * block, 64 * block + 64)
        given, hat = r.res[rows, :], r.hat[rows, :]
        sums[0] = sums[0] + jnp.sum(given * hat, axis=0, keepdims=True)
        sums[1] = sums[1] + jnp.sum(given, axis=0, keepdims=True)
        dres = norm_back(given, hat, r.scale[rows, 0:1], gain1)
        r.res[rows, :] = dres
        r.dlow[rows, :] = dres.astype(BF)
    for row in range(4):
        r.small[4 + row : 5 + row, :] = sums[row]
    for tile in range(3):
        cols = slice(256 * tile, 256 * tile + 256)
        r.datt[:, cols] = nt(r.dlow[...], r.w_out[cols, :]).astype(BF)
        put_shares(r.g, 768, cols, tn(r.att[...], r.dlow[:, cols]))

    def attend_back(pair, carry):
        attend_pair_back(pair, r)
        return carry

    lax.fori_loop(0, PAIRS, attend_back, 0)

    for tile in range(3):
        cols = slice(256 * tile, 256 * tile + 256)
        tail = nt(r.dk[...], r.w_key[cols, :]) + nt(r.dv[...], r.w_value[cols, :])
        r.dx[256:512, cols] = tail[256:512].astype(BF)
        r.dx[0:256, cols] = (
            tail[0:256] + r.res[:, cols] + nt(r.dq[...], r.w_query[cols, :])
        ).astype(BF)
    for tile in range(3):
        cols = slice(256 * tile, 256 * tile + 256)
        put_shares(r.g, 960, cols, tn(r.x[0:256, :], r.dq[:, cols]))
        put_shares(r.g, 1056, cols, tn(r.x[...], r.dk[:, cols]))
        put_shares(r.g, 1152, cols, tn(r.x[...], r.dv[:, cols]))


G_ROWS = 1248

SCRATCH = (
    ("wr", (768, 768), BF),
    ("sine", (256, 384), F32),
    ("cosine", (256, 384), F32),
    ("feat", (512, 896), BF),
    ("q", (256, 768), BF),
    ("k", (512, 768), BF),
    ("v", (512, 768), BF),
    ("att", (256, 768), BF),
    ("relq", (512, 896), BF),
    ("score", (512, 512), F32),
    ("dlog", (512, 512), BF),
    ("probs", (PAIRS, 512, 512), BF),
    ("res", (256, 768), F32),
    ("hat", (256, 768), F32),
    ("scale", (256, 128), F32),
    ("low", (256, 768), BF),
    ("act", (256, 3072), BF),
    ("slope", (256, 3072), F32),
    ("dlow", (256, 768), BF),
    ("dup", (256, 3072), BF),
    ("upsum", (1, 3072), F32),
    ("datt", (256, 768), BF),
    ("dq", (256, 768), BF),
    ("dk", (512, 768), BF),
    ("dv", (512, 768), BF),
)

WEIGHTS = (
    "w_query",
    "w_key",
    "w_value",
    "w_out",
    "w_rel",
    "w_up",
    "b_up",
    "w_down",
    "gain_attn",
    "bias_attn",
    "gain_ffn",
    "bias_ffn",
)


def layer(info, x, bx, cot, weights):
    hi, lo = trig_tables(192)
    rows = [w if w.ndim == 2 else w.reshape(1, -1) for w in weights]
    names_in = ("info", "x", "bx", "cot", "hi", "lo") + WEIGHTS
    outs = (
        ("out", (256, 768), BF),
        ("dx", (512, 768), BF),
        ("g", (2, 4, G_ROWS, 768), BF),
        ("small", (8, 768), F32),
    )
    names = names_in + tuple(o[0] for o in outs) + tuple(s[0] for s in SCRATCH)
    vmem = pl.BlockSpec(memory_space=pltpu.VMEM)
    return pl.pallas_call(
        functools.partial(layer_kernel, names),
        out_shape=[jax.ShapeDtypeStruct(o[1], o[2]) for o in outs],
        in_specs=[pl.BlockSpec(memory_space=pltpu.SMEM)] + [vmem] * (len(names_in) - 1),
        out_specs=[vmem] * len(outs),
        scratch_shapes=[pltpu.VMEM(s[1], s[2]) for s in SCRATCH],
        compiler_params=pltpu.CompilerParams(vmem_limit_bytes=VMEM_LIMIT),
        name="layer",
    )(info, x, bx, cot, jnp.asarray(hi), jnp.asarray(lo), *rows)


def swap(value, axis, count, bit):
    return lax.ppermute(value, axis, [(i, i ^ bit) for i in range(count)])


def pick(stacked, index):
    return lax.dynamic_index_in_dim(stacked, index, 0, keepdims=False)


def reduce_grads(g, small):
    dp = lax.axis_index("dp")
    core, xbit, ybit = dp % 2, (dp // 2) % 2, dp // 4
    got = swap(pick(g, 1 - core), "dp", 8, 1)
    mine = (pick(g, core) + got).reshape(2, 2, G_ROWS, 768)
    cut = G_ROWS // 2
    a, b = mine[:, :, :cut], mine[:, :, cut:]
    a_x = jnp.swapaxes(a, 0, 1)
    got_a = swap(pick(a_x, 1 - xbit), "dp", 8, 2)
    got_b = swap(pick(b, 1 - ybit), "dp", 8, 4)
    a = pick(a_x, xbit) + got_a
    b = pick(b, ybit) + got_b
    got_a = swap(pick(a, 1 - ybit), "dp", 8, 4)
    got_b = swap(pick(b, 1 - xbit), "dp", 8, 2)
    share = jnp.concatenate([pick(a, ybit) + got_a, pick(b, xbit) + got_b], axis=0)
    z = lax.axis_index("seq")
    low = z % 2
    halves = share.reshape(2, cut, 768)
    part = pick(halves, low) + swap(pick(halves, 1 - low), "seq", 4, 1)
    part = part + swap(part, "seq", 4, 2)
    other = swap(part, "seq", 4, 1)
    share = jnp.where(low == 0, jnp.concatenate([part, other]), jnp.concatenate([other, part]))
    for axis, count, bit in (
        ("dp", 8, 1),
        ("dp", 8, 2),
        ("dp", 8, 4),
        ("seq", 4, 1),
        ("seq", 4, 2),
    ):
        small = small + swap(small, axis, count, bit)
    return share.astype(F32), small


def reduce_grads_any(g, small):
    order = g.transpose(1, 0, 2, 3).reshape(8, G_ROWS, 768)

    def weight(base):
        return order[:, base : base + 96].reshape(768, 768)

    up = jnp.concatenate([weight(96 * j) for j in range(4)], axis=1)
    down = order[:, 384:768].reshape(3072, 768)
    full = [weight(960), weight(1056), weight(1152), weight(768), weight(864), up, down]
    scattered = [
        lax.psum(lax.psum_scatter(w, "dp", scatter_dimension=0, tiled=True), "seq").astype(F32)
        for w in full
    ]
    return scattered, lax.psum(small, ("dp", "seq"))


def shards(hidden_in, boxes, lengths, *rest):
    weights, cotangent = rest[:-1], rest[-1]
    micro_count, _, rows, width = hidden_in.shape
    x, cot = hidden_in[:, 0], cotangent[:, 0]
    box = boxes[:, :, 0].transpose(1, 0, 2)
    z = lax.axis_index("seq")
    micro = z // 2
    got_x, got_box = [pick(x, micro)], [pick(box, micro)]
    for bit in (3, 1, 2):
        peer = (z ^ bit) // 2
        got_x.append(swap(pick(x, peer), "seq", 4, bit))
        got_box.append(swap(pick(box, peer), "seq", 4, bit))
    got_cot = [pick(cot, micro), swap(pick(cot, 1 - micro), "seq", 4, 3)]
    info = jnp.stack([z, pick(lengths[:, 0], micro)]).astype(jnp.int32)
    out, dx, g, small = layer(
        info, jnp.concatenate(got_x), jnp.stack(got_box), jnp.concatenate(got_cot), weights
    )
    other_out = swap(out[rows:], "seq", 4, 3)
    own_dx = dx[:rows].astype(F32) + swap(dx[2 * rows : 3 * rows], "seq", 4, 1).astype(F32)
    other_dx = swap(dx[rows : 2 * rows], "seq", 4, 3).astype(F32) + swap(
        dx[3 * rows :], "seq", 4, 2
    ).astype(F32)

    def by_micro(own, other):
        own, other = own.astype(BF), other.astype(BF)
        both = jnp.where(micro == 0, jnp.stack([own, other]), jnp.stack([other, own]))
        return both[:, None]

    hidden = by_micro(out[:rows], other_out)
    dinput = by_micro(own_dx, other_dx)
    dp_count = lax.axis_size("dp")
    if dp_count == 8:
        share, small = reduce_grads(g, small)
        up = jnp.concatenate([share[96 * j : 96 * j + 96] for j in range(4)], axis=1)
        grads = [
            share[960:1056],
            share[1056:1152],
            share[1152:1248],
            share[768:864],
            share[864:960],
            up,
            share[384:768],
        ]
    else:
        grads, small = reduce_grads_any(g, small)
    dp = lax.axis_index("dp")

    def own_part(vector):
        size = vector.shape[0] // dp_count
        return lax.dynamic_slice_in_dim(vector, dp * size, size)

    small = [own_part(small[0:4].reshape(-1))] + [own_part(small[4 + i]) for i in range(4)]
    return (hidden, dinput, *grads[:6], small[0], grads[6], *small[1:])


def solution(mesh):
    rows = P(None, "dp", "seq", None)
    placed = (rows, P(None, None, "dp", "seq"), P(None, "dp")) + (P(),) * 12 + (rows,)
    matrix, vector = P("dp", None), P("dp")
    return jax.shard_map(
        shards,
        mesh=mesh,
        in_specs=placed,
        out_specs=(rows, rows) + (matrix,) * 6 + (vector, matrix) + (vector,) * 4,
        check_vma=False,
    )
```

```python
import functools

import jax
import jax.numpy as jnp
import numpy as np
from jax import lax
from jax.experimental import pallas as pl
from jax.experimental.pallas import tpu as pltpu
from jax.sharding import PartitionSpec as P

HEADS = 12
EPS = 1e-05
BF = jnp.bfloat16
F32 = jnp.float32
PAIRS = HEADS // 2
VMEM_LIMIT = 67043328
QUARTER = 192


def nn(a, b):
    return lax.dot_general(a, b, (((1,), (0,)), ((), ())), preferred_element_type=F32)


def nt(a, b):
    return lax.dot_general(a, b, (((1,), (1,)), ((), ())), preferred_element_type=F32)


def tn(a, b):
    return lax.dot_general(a, b, (((0,), (0,)), ((), ())), preferred_element_type=F32)


def trig_tables(quarter):
    freq = 10000.0 ** (-np.arange(quarter) / quarter)
    tables = []
    for step in (32.0, 1.0):
        angle = step * np.arange(32)[:, None] * freq[None, :]
        rest = np.concatenate([np.sin(angle), np.cos(angle)], axis=1).astype(np.float32)
        parts = []
        for _ in range(3):
            part = rest.astype(BF)
            parts.append(part)
            rest = rest - part.astype(np.float32)
        tables.append(np.concatenate(parts, axis=0))
    return tables


def features(slot, r):
    half = 2 * QUARTER
    iota = lax.broadcasted_iota(jnp.int32, (32, 128), 0)
    hi_tab, lo_tab = r.hi[...], r.lo[...]
    sines, cosines = [], []
    for axis in range(2):
        where = r.bx[slot, axis : axis + 1, :]
        pick_hi = (iota == lax.shift_right_logical(where, 5)).astype(F32).astype(BF)
        pick_lo = (iota == (where & 31)).astype(F32).astype(BF)
        hi = tn(jnp.concatenate([pick_hi] * 3, axis=0), hi_tab)
        lo = tn(jnp.concatenate([pick_lo] * 3, axis=0), lo_tab)
        sin_hi, cos_hi = hi[:, :QUARTER], hi[:, QUARTER:]
        sin_lo, cos_lo = lo[:, :QUARTER], lo[:, QUARTER:]
        sines.append(sin_hi * cos_lo + cos_hi * sin_lo)
        cosines.append(cos_hi * cos_lo - sin_hi * sin_lo)
    sine = jnp.concatenate(sines, axis=1)
    cosine = jnp.concatenate(cosines, axis=1)
    rows = pl.ds(128 * slot, 128)
    r.feat[rows, 0:half] = cosine.astype(BF)
    r.feat[rows, half : 2 * half] = sine.astype(BF)
    if slot < 2:
        r.sine[rows, :] = sine
        r.cosine[rows, :] = cosine


def head_stack(pair):
    first = lax.broadcasted_iota(jnp.int32, pair.shape, 1) < 64
    zero = jnp.zeros_like(pair)
    return jnp.concatenate([jnp.where(first, pair, zero), jnp.where(first, zero, pair)], axis=0)


def head_join(stack):
    half = stack.shape[0] // 2
    first = lax.broadcasted_iota(jnp.int32, (half, 128), 1) < 64
    return jnp.where(first, stack[:half], stack[half:])


def attend_pair(pair, live, r):
    cols = pl.ds(pl.multiple_of(128 * pair, 128), 128)
    stack = head_stack(r.q[:, cols].astype(F32) * 0.125).astype(BF)
    for head in range(2):
        rows = slice(256 * head, 256 * head + 256)
        left = nt(stack[rows], r.wr[0:384, cols])
        right = nt(stack[rows], r.wr[384:768, cols])
        sin, cos = r.sine[...], r.cosine[...]
        r.relq[rows, 0:384] = (left * sin + right * cos).astype(BF)
        r.relq[rows, 384:768] = (right * sin - left * cos).astype(BF)
    r.relq[:, 768:896] = stack
    r.feat[:, 768:896] = r.k[:, cols]
    r.score[...] = nt(r.relq[...], r.feat[...])
    for block in range(8):
        rows = pl.ds(64 * block, 64)
        score = jnp.where(live, r.score[rows, :], -1e30)
        top = jnp.max(score, axis=-1, keepdims=True)
        weight = jnp.exp(score - top)
        total = jnp.sum(weight, axis=-1, keepdims=True)
        r.probs[pair, rows, :] = (weight * (1.0 / total)).astype(BF)
    r.att[:, cols] = head_join(nn(r.probs[pair], r.v[:, cols])).astype(BF)


def attend_pair_back(pair, r):
    cols = pl.ds(pl.multiple_of(128 * pair, 128), 128)
    given = head_stack(r.att[:, cols].astype(F32)).astype(BF)
    stack = head_stack(r.q[:, cols].astype(F32)).astype(BF)
    r.score[...] = nt(given, r.v[:, cols])
    for block in range(8):
        rows = pl.ds(64 * block, 64)
        prob = r.probs[pair, rows, :].astype(F32)
        push = prob * r.score[rows, :]
        mean = jnp.sum(push, axis=-1, keepdims=True)
        r.dlog[rows, :] = ((push - prob * mean) * 0.125).astype(BF)
    r.feat[:, 768:896] = r.k[:, cols]
    r.v[:, cols] = tn(r.probs[pair], given).astype(BF)
    r.k[:, cols] = tn(r.dlog[...], stack).astype(BF)
    for head in range(2):
        rows = slice(256 * head, 256 * head + 256)
        first = nn(r.dlog[rows, :], r.feat[:, 0:384])
        second = nn(r.dlog[rows, :], r.feat[:, 384:768])
        sin, cos = r.sine[...], r.cosine[...]
        r.relq[rows, 0:384] = (first * sin - second * cos).astype(BF)
        r.relq[rows, 384:768] = (first * cos + second * sin).astype(BF)
    dq = nn(r.dlog[...], r.feat[:, 768:896]) + nn(r.relq[:, 0:768], r.wr[:, cols])
    r.q[:, cols] = head_join(dq).astype(BF)
    part = tn(r.relq[:, 0:768], stack).astype(BF)
    for piece, share in enumerate((0, 1, 4, 5, 2, 3, 6, 7)):
        c, y, x = share % 2, share // 4, share // 2 % 2
        r.pool[c, y, x, 96:192, cols] = part[96 * piece : 96 * piece + 96]


def norm_back(given, hat, scale, gain):
    push = given * gain
    mean = jnp.mean(push, axis=-1, keepdims=True)
    lean = jnp.mean(push * hat, axis=-1, keepdims=True)
    return scale * (push - mean - hat * lean)


def put_shares(ref, base, cols, part):
    for share in range(8):
        c, y, x = share % 2, share // 4, share // 2 % 2
        ref[c, y, x, pl.ds(base, 96), cols] = part[96 * share : 96 * share + 96].astype(BF)


class Refs:
    pass


CHUNKS = (("g", 384, 384, 384), ("g", 0, 384, 0), ("pool", 0, 192, 768), ("pool", 192, 288, 960))
STAGES = ("core", "xa", "xb", "ya", "yb", "z1", "z2", "z3")
SENDS = ("x1", "x2", "x3", "b1", "b2", "b3", "cot", "out", "d1", "d2", "d3")
SENDS += tuple("s%d" % i for i in range(5))
SENDS += tuple("%s%d" % (s, u) for u in range(4) for s in STAGES)
LOADS = ("x", "cot", "key", "value", "query", "out")
LOADS += tuple("rel%d" % i for i in range(4)) + tuple("up%d" % i for i in range(4))
LOADS += tuple("down%d" % i for i in range(4))
STORES = ("hid0", "hid1", "din", "share", "small")


class Net:
    def __init__(self, r):
        self.r = r
        self.sent = []

    def start(self, name, src, dst, peer):
        i = SENDS.index(name)
        copy = pltpu.make_async_remote_copy(
            src_ref=src,
            dst_ref=dst,
            send_sem=self.r.send_sem.at[i],
            recv_sem=self.r.recv_sem.at[i],
            device_id=peer,
            device_id_type=pl.DeviceIdType.MESH,
        )
        copy.start()
        self.sent.append((name, src, dst, peer))

    def _of(self, name):
        for key, src, dst, peer in self.sent:
            if key == name:
                i = SENDS.index(name)
                return pltpu.make_async_remote_copy(
                    src_ref=src,
                    dst_ref=dst,
                    send_sem=self.r.send_sem.at[i],
                    recv_sem=self.r.recv_sem.at[i],
                    device_id=peer,
                    device_id_type=pl.DeviceIdType.MESH,
                )
        raise KeyError(name)

    def got(self, name):
        self._of(name).wait_recv()

    def finish(self):
        for name, *_ in self.sent:
            self._of(name).wait_send()


def add_rows(count, body):
    def step(i, carry):
        body(pl.multiple_of(48 * i, 16))
        return carry

    lax.fori_loop(0, count // 48, step, 0)


class Reduction:
    def __init__(self, r, net, dp, z):
        self.r, self.net = r, net
        self.c, self.x, self.y = dp % 2, dp // 2 % 2, dp // 4
        self.low = z % 2
        self.pc = (dp + 1 - 2 * self.c, z)
        self.px = (dp + 2 - 4 * self.x, z)
        self.py = (dp + 4 - 8 * self.y, z)
        self.pz1 = (dp, z + 1 - 2 * self.low)
        self.pz2 = (dp, (z + 2) % 4)

    def parts(self, u):
        name, base, rows, out = CHUNKS[u]
        return getattr(self.r, name), base, rows // 2, out, self.r.r1[u], out // 2

    def core(self, u):
        g, base, half, _, r1, _ = self.parts(u)
        rows = pl.ds(base, 2 * half)
        self.net.start("core%d" % u, g.at[1 - self.c, :, :, rows], r1, self.pc)

    def first(self, u):
        g, base, half, _, r1, at = self.parts(u)
        c, x, y = self.c, self.x, self.y
        self.net.got("core%d" % u)

        def add(i):
            for k in range(2):
                rows, own = pl.ds(base + i, 48), pl.ds(i, 48)
                g[c, k, 1 - x, rows] = (
                    g[c, k, 1 - x, rows].astype(F32) + r1[k, 1 - x, own].astype(F32)
                ).astype(BF)
                rows, own = pl.ds(base + half + i, 48), pl.ds(half + i, 48)
                g[c, 1 - y, k, rows] = (
                    g[c, 1 - y, k, rows].astype(F32) + r1[1 - y, k, own].astype(F32)
                ).astype(BF)

        add_rows(half, add)
        rows = pl.ds(at, half)
        self.net.start(
            "xa%d" % u, g.at[c, :, 1 - x, pl.ds(base, half)], self.r.ra.at[:, rows], self.px
        )
        self.net.start(
            "yb%d" % u, g.at[c, 1 - y, :, pl.ds(base + half, half)], self.r.rb.at[:, rows], self.py
        )

    def second(self, u):
        g, base, half, _, r1, at = self.parts(u)
        c, x, y = self.c, self.x, self.y
        self.net.got("xa%d" % u)
        self.net.got("yb%d" % u)

        def add(i):
            rows, own, came = pl.ds(base + i, 48), pl.ds(i, 48), pl.ds(at + i, 48)
            g[c, 1 - y, x, rows] = (
                g[c, 1 - y, x, rows].astype(F32)
                + r1[1 - y, x, own].astype(F32)
                + self.r.ra[1 - y, came].astype(F32)
            ).astype(BF)
            rows, own = pl.ds(base + half + i, 48), pl.ds(half + i, 48)
            g[c, y, 1 - x, rows] = (
                g[c, y, 1 - x, rows].astype(F32)
                + r1[y, 1 - x, own].astype(F32)
                + self.r.rb[1 - x, came].astype(F32)
            ).astype(BF)

        add_rows(half, add)
        rows = pl.ds(at, half)
        self.net.start(
            "ya%d" % u, g.at[c, 1 - y, x, pl.ds(base, half)], self.r.ra2.at[rows], self.py
        )
        self.net.start(
            "xb%d" % u, g.at[c, y, 1 - x, pl.ds(base + half, half)], self.r.rb2.at[rows], self.px
        )

    def third(self, u):
        g, base, half, _, r1, at = self.parts(u)
        c, x, y = self.c, self.x, self.y
        self.net.got("ya%d" % u)
        self.net.got("xb%d" % u)

        def add(i):
            came = pl.ds(at + i, 48)
            rows, own = pl.ds(base + i, 48), pl.ds(i, 48)
            g[c, y, x, rows] = (
                g[c, y, x, rows].astype(F32)
                + r1[y, x, own].astype(F32)
                + self.r.ra[y, came].astype(F32)
                + self.r.ra2[came].astype(F32)
            ).astype(BF)
            rows, own = pl.ds(base + half + i, 48), pl.ds(half + i, 48)
            g[c, y, x, rows] = (
                g[c, y, x, rows].astype(F32)
                + r1[y, x, own].astype(F32)
                + self.r.rb[x, came].astype(F32)
                + self.r.rb2[came].astype(F32)
            ).astype(BF)

        add_rows(half, add)
        start = pl.multiple_of(base + half * (1 - self.low), 16)
        self.net.start(
            "z1%d" % u, g.at[c, y, x, pl.ds(start, half)], self.r.rz1.at[pl.ds(at, half)], self.pz1
        )

    def fourth(self, u):
        g, base, half, _, _, at = self.parts(u)
        c, x, y = self.c, self.x, self.y
        self.net.got("z1%d" % u)
        start = pl.multiple_of(base + half * self.low, 16)

        def add(i):
            rows = pl.ds(pl.multiple_of(start + i, 16), 48)
            g[c, y, x, rows] = (
                g[c, y, x, rows].astype(F32) + self.r.rz1[pl.ds(at + i, 48)].astype(F32)
            ).astype(BF)

        add_rows(half, add)
        self.net.start(
            "z2%d" % u, g.at[c, y, x, pl.ds(start, half)], self.r.rz2.at[pl.ds(at, half)], self.pz2
        )

    def fifth(self, u):
        g, base, half, out, _, at = self.parts(u)
        c, x, y = self.c, self.x, self.y
        self.net.got("z2%d" % u)
        start = pl.multiple_of(base + half * self.low, 16)
        dest = pl.multiple_of(out + half * self.low, 16)

        def add(i):
            rows = pl.ds(pl.multiple_of(start + i, 16), 48)
            self.r.sums[pl.ds(pl.multiple_of(dest + i, 16), 48)] = (
                g[c, y, x, rows].astype(F32) + self.r.rz2[pl.ds(at + i, 48)].astype(F32)
            ).astype(BF)

        add_rows(half, add)
        rows = pl.ds(dest, half)
        self.net.start("z3%d" % u, self.r.sums.at[rows], self.r.sums.at[rows], self.pz1)

    def small(self, i):
        if i:
            self.net.got("s%d" % (i - 1))
            self.r.sm[i] = self.r.sm[i - 1] + self.r.smr[i - 1]
        if i < 5:
            peer = (self.pc, self.px, self.py, self.pz1, self.pz2)[i]
            self.net.start("s%d" % i, self.r.sm.at[i], self.r.smr.at[i], peer)


def layer_kernel(names, reduce, *refs):
    r = Refs()
    for name, ref in zip(names, refs):
        setattr(r, name, ref)
    r.r1 = (r.r1_0, r.r1_1, r.r1_2, r.r1_3) if reduce else None
    dp, z = lax.axis_index("dp"), lax.axis_index("seq")
    micro = z // 2
    peers = {1: (dp, 3 - z), 2: (dp, z + 1 - 2 * (z % 2)), 3: (dp, (z + 2) % 4)}
    net = Net(r)
    red = Reduction(r, net, dp, z) if reduce else None

    loads = {}

    def load(name, src, dst):
        loads[name] = pltpu.make_async_copy(src, dst, r.load_sem.at[LOADS.index(name)])
        loads[name].start()

    load("x", r.hidden_in.at[micro], r.x.at[0:128])
    load("key", r.w_key, r.wk)
    load("value", r.w_value, r.wv)
    load("query", r.w_query, r.wq)

    greet = list(peers.values()) + ([red.pc, red.px, red.py] if reduce else [])
    barrier = pltpu.get_barrier_semaphore()
    for peer in greet:
        pl.semaphore_signal(barrier, 1, device_id=peer, device_id_type=pl.DeviceIdType.MESH)
    pl.semaphore_wait(barrier, len(greet))
    for slot in (1, 3, 2):
        far = peers[slot][1] // 2
        net.start("b%d" % slot, r.boxes.at[far], r.bx.at[slot], peers[slot])
    for slot in (1, 3, 2):
        far = peers[slot][1] // 2
        rows = pl.ds(128 * slot, 128)
        net.start("x%d" % slot, r.hidden_in.at[far], r.x.at[rows], peers[slot])
    net.start("cot", r.cotangent.at[1 - micro], r.cot.at[128:256], peers[1])

    for i, (dst, src) in enumerate(((0, 0), (192, 384), (384, 192), (576, 576))):
        load("rel%d" % i, r.w_rel.at[src : src + 192], r.wr.at[dst : dst + 192])
    load("out", r.w_out, r.wo)
    for j in range(4):
        load("up%d" % j, r.w_up.at[:, 768 * j : 768 * j + 768], r.pool.at[0, j // 2, j % 2])
    for j in range(4):
        load("down%d" % j, r.w_down.at[768 * j : 768 * j + 768], r.pool.at[1, j // 2, j % 2])
    load("cot", r.cotangent.at[micro], r.cot.at[0:128])

    def project(slot):
        rows = slice(128 * slot, 128 * slot + 128)
        for tile in range(3):
            cols = slice(256 * tile, 256 * tile + 256)
            r.k[rows, cols] = nn(r.x[rows, :], r.wk[:, cols]).astype(BF)
            r.v[rows, cols] = nn(r.x[rows, :], r.wv[:, cols]).astype(BF)
            if slot < 2:
                r.q[rows, cols] = nn(r.x[rows, :], r.wq[:, cols]).astype(BF)

    r.bx[0] = r.boxes[micro]
    features(0, r)
    loads["x"].wait()
    loads["key"].wait()
    loads["value"].wait()
    loads["query"].wait()
    project(0)
    for slot in (1, 2, 3):
        net.got("b%d" % slot)
        features(slot, r)
    for i in range(4):
        loads["rel%d" % i].wait()
    for slot in (2, 1, 3):
        net.got("x%d" % slot)
        project(slot)

    lane = lax.broadcasted_iota(jnp.int32, (1, 128), 1)
    length = r.lengths[micro, 0]
    blocks = (z, peers[1][1], peers[2][1], peers[3][1])
    live = jnp.concatenate([lane + 128 * block < length for block in blocks], axis=1)

    def attend(pair, carry):
        attend_pair(pair, live, r)
        return carry

    lax.fori_loop(0, PAIRS, attend, 0)

    loads["out"].wait()
    for tile in range(3):
        cols = slice(256 * tile, 256 * tile + 256)
        r.res[:, cols] = r.x[0:256, cols].astype(F32) + nn(r.att[...], r.wo[:, cols])

    gain1, bias1, gain2, bias2 = [r.vectors[4 + i : 5 + i, :] for i in range(4)]
    for block in range(4):
        rows = slice(64 * block, 64 * block + 64)
        res = r.res[rows, :]
        center = res - jnp.mean(res, axis=-1, keepdims=True)
        scale = lax.rsqrt(jnp.mean(center * center, axis=-1, keepdims=True) + EPS)
        hat = center * scale
        r.hat[rows, :] = hat
        r.scale[rows, :] = jnp.broadcast_to(scale, (64, 128))
        normed = hat * gain1 + bias1
        r.res[rows, :] = normed
        r.low[rows, :] = normed.astype(BF)

    for j in range(4):
        loads["up%d" % j].wait()
    for j in range(4):
        loads["down%d" % j].wait()

    def up_tile(tile):
        j = tile // 3
        return j // 2, j % 2, pl.ds(pl.multiple_of(256 * (tile % 3), 256), 256)

    def up(tile, carry):
        cols = pl.ds(pl.multiple_of(256 * tile, 256), 256)
        y, x, part = up_tile(tile)
        bias = r.vectors[pl.ds(tile // 3, 1), part]
        value = nn(r.low[...], r.pool[0, y, x, :, part]) + bias
        below = 0.5 * (1.0 + lax.erf(value * np.float32(np.sqrt(0.5))))
        dense = jnp.exp(value * value * -0.5) * np.float32(1.0 / np.sqrt(2.0 * np.pi))
        r.act[:, cols] = (value * below).astype(BF)
        r.slope[:, cols] = below + value * dense
        return carry

    lax.fori_loop(0, 12, up, 0)
    for tile in range(3):
        cols = slice(256 * tile, 256 * tile + 256)
        r.res[:, cols] = r.res[:, cols] + sum(
            nn(r.act[:, 768 * j : 768 * j + 768], r.pool[1, j // 2, j % 2, :, cols])
            for j in range(4)
        )

    loads["cot"].wait()
    net.got("cot")
    sums = [jnp.zeros((1, 768), F32) for _ in range(4)]
    for block in range(4):
        rows = slice(64 * block, 64 * block + 64)
        res = r.res[rows, :]
        center = res - jnp.mean(res, axis=-1, keepdims=True)
        scale = lax.rsqrt(jnp.mean(center * center, axis=-1, keepdims=True) + EPS)
        hat = center * scale
        r.out[rows, :] = (hat * gain2 + bias2).astype(BF)
        given = r.cot[rows, :].astype(F32)
        sums[2] = sums[2] + jnp.sum(given * hat, axis=0, keepdims=True)
        sums[3] = sums[3] + jnp.sum(given, axis=0, keepdims=True)
        dres = norm_back(given, hat, scale, gain2)
        r.res[rows, :] = dres
        r.dlow[rows, :] = dres.astype(BF)

    def grad_down(share, carry):
        cols = pl.ds(pl.multiple_of(384 * share, 128), 384)
        r.g[share % 2, share // 4, share // 2 % 2, 384:768, :] = tn(
            r.act[:, cols], r.dlow[...]
        ).astype(BF)
        return carry

    lax.fori_loop(0, 8, grad_down, 0)
    stores = {}

    def store(name, src, dst):
        stores[name] = pltpu.make_async_copy(src, dst, r.store_sem.at[STORES.index(name)])
        stores[name].start()

    net.start("out", r.out.at[128:256], r.outr, peers[1])
    if reduce:
        red.core(0)

    def up_back(tile, carry):
        cols = pl.ds(pl.multiple_of(256 * tile, 256), 256)
        y, x, part = up_tile(tile)
        push = nt(r.dlow[...], r.pool[1, y, x, part, :]) * r.slope[:, cols]
        low = push.astype(BF)
        r.act[:, cols] = low
        r.sm[0, pl.ds(tile // 3, 1), part] = jnp.sum(low.astype(F32), axis=0, keepdims=True)
        return carry

    lax.fori_loop(0, 12, up_back, 0)

    def grad_up(tile, carry):
        cols = pl.ds(pl.multiple_of(256 * tile, 256), 256)
        _, _, dest = up_tile(tile)
        put_shares(r.g, pl.multiple_of(96 * (tile // 3), 32), dest, tn(r.low[...], r.act[:, cols]))
        return carry

    lax.fori_loop(0, 12, grad_up, 0)
    if reduce:
        red.core(1)
        red.first(0)
    for tile in range(3):
        cols = slice(256 * tile, 256 * tile + 256)
        r.res[:, cols] = r.res[:, cols] + sum(
            nt(r.act[:, 768 * j : 768 * j + 768], r.pool[0, j // 2, j % 2, cols, :])
            for j in range(4)
        )
    for block in range(4):
        rows = slice(64 * block, 64 * block + 64)
        given, hat = r.res[rows, :], r.hat[rows, :]
        sums[0] = sums[0] + jnp.sum(given * hat, axis=0, keepdims=True)
        sums[1] = sums[1] + jnp.sum(given, axis=0, keepdims=True)
        dres = norm_back(given, hat, r.scale[rows, 0:1], gain1)
        r.res[rows, :] = dres
        r.dlow[rows, :] = dres.astype(BF)
    for row in range(4):
        r.sm[0, 4 + row : 5 + row, :] = sums[row]
    if reduce:
        red.first(1)
    for tile in range(3):
        cols = slice(256 * tile, 256 * tile + 256)
        put_shares(r.pool, 0, cols, tn(r.att[...], r.dlow[:, cols]))
    for tile in range(3):
        cols = slice(256 * tile, 256 * tile + 256)
        r.att[:, cols] = nt(r.dlow[...], r.wo[cols, :]).astype(BF)
    if reduce:
        red.small(0)

    def attend_back(pair, carry):
        attend_pair_back(pair, r)
        return carry

    lax.fori_loop(0, 4, attend_back, 0)
    if reduce:
        red.second(0)
        red.small(1)
    lax.fori_loop(4, PAIRS, attend_back, 0)
    if reduce:
        red.core(2)

    for tile in range(3):
        cols = slice(256 * tile, 256 * tile + 256)
        tail = nt(r.k[...], r.wk[cols, :]) + nt(r.v[...], r.wv[cols, :])
        r.relq[256:512, cols] = tail[256:512].astype(BF)
        r.relq[0:256, cols] = (
            tail[0:256] + r.res[:, cols] + nt(r.q[...], r.wq[cols, :])
        ).astype(BF)
    for slot in (1, 3, 2):
        rows = pl.ds(128 * slot, 128)
        net.start("d%d" % slot, r.relq.at[rows, 0:768], r.dxr.at[slot - 1], peers[slot])
    if reduce:
        red.first(2)
        red.second(1)
        red.small(2)
    for tile in range(3):
        cols = slice(256 * tile, 256 * tile + 256)
        put_shares(r.pool, 192, cols, tn(r.x[0:256, :], r.q[:, cols]))
        put_shares(r.pool, 288, cols, tn(r.x[...], r.k[:, cols]))
        put_shares(r.pool, 384, cols, tn(r.x[...], r.v[:, cols]))
    if reduce:
        red.core(3)
        red.third(0)
        red.small(3)
        red.first(3)
    store("hid0", r.out.at[0:128], r.hidden_out.at[micro])
    net.got("out")
    store("hid1", r.outr, r.hidden_out.at[1 - micro])
    if reduce:
        red.second(2)
        red.fourth(0)
        red.third(1)
        red.small(4)
        red.second(3)
        red.fifth(0)
        red.fourth(1)
        red.third(2)
    for slot in (1, 2, 3):
        net.got("d%d" % slot)
    r.din[micro] = (r.relq[0:128, 0:768].astype(F32) + r.dxr[1].astype(F32)).astype(BF)
    r.din[1 - micro] = (r.dxr[0].astype(F32) + r.dxr[2].astype(F32)).astype(BF)
    store("din", r.din, r.input_grad)
    if reduce:
        red.fifth(1)
        red.fourth(2)
        red.third(3)
        red.small(5)
        store("small", r.sm.at[5], r.small)
        red.fifth(2)
        red.fourth(3)
        red.fifth(3)
        for u in range(4):
            net.got("z3%d" % u)
        store("share", r.sums, r.share)
    else:
        store("small", r.sm.at[0], r.small)
        store("share", r.g, r.share.at[0])
        last = pltpu.make_async_copy(r.pool, r.share.at[1], r.load_sem.at[0])
        last.start()
        last.wait()
    for copy in stores.values():
        copy.wait()
    net.finish()


def scratch(reduce):
    shapes = [
        ("x", (512, 768), BF),
        ("bx", (4, 2, 128), jnp.int32),
        ("cot", (256, 768), BF),
        ("wq", (768, 768), BF),
        ("wk", (768, 768), BF),
        ("wv", (768, 768), BF),
        ("wo", (768, 768), BF),
        ("wr", (768, 768), BF),
        ("pool", (2, 2, 2, 768, 768), BF),
        ("g", (2, 2, 2, 768, 768), BF),
        ("sine", (256, 384), F32),
        ("cosine", (256, 384), F32),
        ("feat", (512, 896), BF),
        ("q", (256, 768), BF),
        ("k", (512, 768), BF),
        ("v", (512, 768), BF),
        ("att", (256, 768), BF),
        ("relq", (512, 896), BF),
        ("score", (512, 512), F32),
        ("dlog", (512, 512), BF),
        ("probs", (PAIRS, 512, 512), BF),
        ("res", (256, 768), F32),
        ("hat", (256, 768), F32),
        ("scale", (256, 128), F32),
        ("low", (256, 768), BF),
        ("act", (256, 3072), BF),
        ("slope", (256, 3072), F32),
        ("dlow", (256, 768), BF),
        ("out", (256, 768), BF),
        ("outr", (128, 768), BF),
        ("dxr", (3, 128, 768), BF),
        ("din", (2, 128, 768), BF),
        ("sm", (6, 8, 768), F32),
    ]
    if reduce:
        shapes += [("r1_%d" % u, (2, 2, c[2], 768), BF) for u, c in enumerate(CHUNKS)]
        shapes += [
            ("ra", (2, 624, 768), BF),
            ("rb", (2, 624, 768), BF),
            ("ra2", (624, 768), BF),
            ("rb2", (624, 768), BF),
            ("rz1", (624, 768), BF),
            ("rz2", (624, 768), BF),
            ("sums", (1248, 768), BF),
            ("smr", (5, 8, 768), F32),
        ]
    return shapes


def layer(lengths, hidden_in, boxes, cotangent, vectors, weights, reduce):
    hi, lo = trig_tables(QUARTER)
    any_space = pl.BlockSpec(memory_space=pl.ANY)
    vmem = pl.BlockSpec(memory_space=pltpu.VMEM)
    ins = (
        ("lengths", lengths, pl.BlockSpec(memory_space=pltpu.SMEM)),
        ("hidden_in", hidden_in, any_space),
        ("cotangent", cotangent, any_space),
        ("boxes", boxes, vmem),
        ("vectors", vectors, vmem),
        ("hi", jnp.asarray(hi), vmem),
        ("lo", jnp.asarray(lo), vmem),
    ) + tuple((name, w, any_space) for name, w in weights)
    outs = (
        ("hidden_out", (2, 128, 768), BF),
        ("input_grad", (2, 128, 768), BF),
        ("share", (1248, 768) if reduce else (2, 2, 2, 2, 768, 768), BF),
        ("small", (8, 768), F32),
    )
    shapes = scratch(reduce)
    sems = ("send_sem", "recv_sem", "load_sem", "store_sem")
    names = tuple(i[0] for i in ins) + tuple(o[0] for o in outs)
    names += tuple(s[0] for s in shapes) + sems
    dma = pltpu.SemaphoreType.DMA
    return pl.pallas_call(
        functools.partial(layer_kernel, names, reduce),
        out_shape=[jax.ShapeDtypeStruct(o[1], o[2]) for o in outs],
        in_specs=[i[2] for i in ins],
        out_specs=[any_space] * len(outs),
        scratch_shapes=[pltpu.VMEM(s[1], s[2]) for s in shapes]
        + [dma((len(SENDS),)), dma((len(SENDS),)), dma((len(LOADS),)), dma((len(STORES),))],
        compiler_params=pltpu.CompilerParams(
            vmem_limit_bytes=VMEM_LIMIT, collective_id=0, has_side_effects=True
        ),
        name="layer",
    )(*[i[1] for i in ins])


def finish_kernel(share, small, dq, dk, dv, dout, drel, dup, dbup, ddown, *vectors):
    for j in range(4):
        dup[:, 768 * j : 768 * j + 768] = share[96 * j : 96 * j + 96, :].astype(F32)
    ddown[...] = share[384:768, :].astype(F32)
    for i, ref in enumerate((dout, drel, dq, dk, dv)):
        ref[...] = share[768 + 96 * i : 864 + 96 * i, :].astype(F32)
    dp = lax.axis_index("dp")
    row = small[pl.ds(dp // 2, 1), :]
    dbup[...] = jnp.where(dp % 2 == 0, row[:, 0:384], row[:, 384:768])
    turned = pltpu.roll(small[...], lax.rem(768 - 96 * dp, 768), 1)
    for i, ref in enumerate(vectors):
        ref[...] = turned[4 + i : 5 + i, 0:96]


def finish(share, small):
    shapes = [(96, 768)] * 5 + [(96, 3072), (1, 384), (384, 768)] + [(1, 96)] * 4
    outs = pl.pallas_call(
        finish_kernel,
        out_shape=[jax.ShapeDtypeStruct(s, F32) for s in shapes],
        name="finish",
    )(share, small)
    return [o.reshape(-1) if o.shape[0] == 1 else o for o in outs]


def finish_any(g, small):
    order = g.transpose(0, 2, 3, 1, 4, 5).reshape(2, 8, 768, 768)

    def weight(which, base):
        return order[which, :, base : base + 96].reshape(768, 768)

    up = jnp.concatenate([weight(0, 96 * j) for j in range(4)], axis=1)
    down = order[0, :, 384:768].reshape(3072, 768)
    full = [weight(1, base) for base in (192, 288, 384, 0, 96)] + [up, down]
    grads = [
        lax.psum(lax.psum_scatter(w, "dp", scatter_dimension=0, tiled=True), "seq").astype(F32)
        for w in full
    ]
    small = lax.psum(small, ("dp", "seq"))
    dp, count = lax.axis_index("dp"), lax.axis_size("dp")

    def own_part(vector):
        size = vector.shape[0] // count
        return lax.dynamic_slice_in_dim(vector, dp * size, size)

    parts = [own_part(small[4 + i]) for i in range(4)]
    return grads[:6] + [own_part(small[0:4].reshape(-1)), grads[6]] + parts


def shards(
    hidden_in,
    boxes,
    lengths,
    w_query,
    w_key,
    w_value,
    w_out,
    w_rel,
    w_up,
    b_up,
    w_down,
    gain_attn,
    bias_attn,
    gain_ffn,
    bias_ffn,
    cotangent,
):
    vectors = jnp.concatenate([b_up, gain_attn, bias_attn, gain_ffn, bias_ffn])
    weights = (
        ("w_query", w_query),
        ("w_key", w_key),
        ("w_value", w_value),
        ("w_out", w_out),
        ("w_rel", w_rel),
        ("w_up", w_up),
        ("w_down", w_down),
    )
    reduce = lax.axis_size("dp") == 8
    hidden, dinput, share, small = layer(
        lengths,
        hidden_in[:, 0],
        boxes[:, :, 0].transpose(1, 0, 2),
        cotangent[:, 0],
        vectors.astype(F32).reshape(8, 768),
        weights,
        reduce,
    )
    rest = finish(share, small) if reduce else finish_any(share, small)
    return (hidden[:, None], dinput[:, None], *rest)


def solution(mesh):
    rows = P(None, "dp", "seq", None)
    placed = (rows, P(None, None, "dp", "seq"), P(None, "dp")) + (P(),) * 12 + (rows,)
    matrix, vector = P("dp", None), P("dp")
    return jax.shard_map(
        shards,
        mesh=mesh,
        in_specs=placed,
        out_specs=(rows, rows) + (matrix,) * 6 + (vector, matrix) + (vector,) * 4,
        check_vma=False,
    )
```

```python
import functools

import jax
import jax.numpy as jnp
import numpy as np
from jax import lax
from jax.experimental import pallas as pl
from jax.experimental.pallas import tpu as pltpu
from jax.sharding import PartitionSpec as P

HEADS = 12
EPS = 1e-05
BF = jnp.bfloat16
F32 = jnp.float32
PAIRS = HEADS // 2
VMEM_LIMIT = 67043328
QUARTER = 192


def nn(a, b):
    return lax.dot_general(a, b, (((1,), (0,)), ((), ())), preferred_element_type=F32)


def nt(a, b):
    return lax.dot_general(a, b, (((1,), (1,)), ((), ())), preferred_element_type=F32)


def tn(a, b):
    return lax.dot_general(a, b, (((0,), (0,)), ((), ())), preferred_element_type=F32)


def trig_tables(quarter):
    freq = 10000.0 ** (-np.arange(quarter) / quarter)
    tables = []
    for step in (32.0, 1.0):
        angle = step * np.arange(32)[:, None] * freq[None, :]
        rest = np.concatenate([np.sin(angle), np.cos(angle)], axis=1).astype(np.float32)
        parts = []
        for _ in range(3):
            part = rest.astype(BF)
            parts.append(part)
            rest = rest - part.astype(np.float32)
        tables.append(np.concatenate(parts, axis=0))
    return tables


def features(slot, r):
    half = 2 * QUARTER
    iota = lax.broadcasted_iota(jnp.int32, (32, 128), 0)
    hi_tab, lo_tab = r.hi[...], r.lo[...]
    sines, cosines = [], []
    for axis in range(2):
        where = r.bx[slot, axis : axis + 1, :]
        pick_hi = (iota == lax.shift_right_logical(where, 5)).astype(F32).astype(BF)
        pick_lo = (iota == (where & 31)).astype(F32).astype(BF)
        hi = tn(jnp.concatenate([pick_hi] * 3, axis=0), hi_tab)
        lo = tn(jnp.concatenate([pick_lo] * 3, axis=0), lo_tab)
        sin_hi, cos_hi = hi[:, :QUARTER], hi[:, QUARTER:]
        sin_lo, cos_lo = lo[:, :QUARTER], lo[:, QUARTER:]
        sines.append(sin_hi * cos_lo + cos_hi * sin_lo)
        cosines.append(cos_hi * cos_lo - sin_hi * sin_lo)
    sine = jnp.concatenate(sines, axis=1)
    cosine = jnp.concatenate(cosines, axis=1)
    rows = pl.ds(128 * slot, 128)
    r.feat[rows, 0:half] = cosine.astype(BF)
    r.feat[rows, half : 2 * half] = sine.astype(BF)
    if slot < 2:
        r.sine[rows, :] = sine
        r.cosine[rows, :] = cosine


def head_stack(pair):
    first = lax.broadcasted_iota(jnp.int32, pair.shape, 1) < 64
    zero = jnp.zeros_like(pair)
    return jnp.concatenate([jnp.where(first, pair, zero), jnp.where(first, zero, pair)], axis=0)


def head_join(stack):
    half = stack.shape[0] // 2
    first = lax.broadcasted_iota(jnp.int32, (half, 128), 1) < 64
    return jnp.where(first, stack[:half], stack[half:])


def attend_pair(pair, live, r):
    cols = pl.ds(pl.multiple_of(128 * pair, 128), 128)
    stack = head_stack(r.q[:, cols].astype(F32) * 0.125).astype(BF)
    for head in range(2):
        rows = slice(256 * head, 256 * head + 256)
        left = nt(stack[rows], r.wr[0:384, cols])
        right = nt(stack[rows], r.wr[384:768, cols])
        sin, cos = r.sine[...], r.cosine[...]
        r.relq[rows, 0:384] = (left * sin + right * cos).astype(BF)
        r.relq[rows, 384:768] = (right * sin - left * cos).astype(BF)
    r.relq[:, 768:896] = stack
    r.feat[:, 768:896] = r.k[:, cols]
    r.score[...] = nt(r.relq[...], r.feat[...])
    for block in range(8):
        rows = pl.ds(64 * block, 64)
        score = jnp.where(live, r.score[rows, :], -1e30)
        top = jnp.max(score, axis=-1, keepdims=True)
        weight = jnp.exp(score - top)
        total = jnp.sum(weight, axis=-1, keepdims=True)
        r.probs[pair, rows, :] = (weight * (1.0 / total)).astype(BF)
    r.att[:, cols] = head_join(nn(r.probs[pair], r.v[:, cols])).astype(BF)


def attend_pair_back(pair, r):
    cols = pl.ds(pl.multiple_of(128 * pair, 128), 128)
    given = head_stack(r.att[:, cols].astype(F32)).astype(BF)
    stack = head_stack(r.q[:, cols].astype(F32)).astype(BF)
    r.score[...] = nt(given, r.v[:, cols])
    for block in range(8):
        rows = pl.ds(64 * block, 64)
        prob = r.probs[pair, rows, :].astype(F32)
        push = prob * r.score[rows, :]
        mean = jnp.sum(push, axis=-1, keepdims=True)
        r.dlog[rows, :] = ((push - prob * mean) * 0.125).astype(BF)
    r.feat[:, 768:896] = r.k[:, cols]
    r.v[:, cols] = tn(r.probs[pair], given).astype(BF)
    r.k[:, cols] = tn(r.dlog[...], stack).astype(BF)
    for head in range(2):
        rows = slice(256 * head, 256 * head + 256)
        first = nn(r.dlog[rows, :], r.feat[:, 0:384])
        second = nn(r.dlog[rows, :], r.feat[:, 384:768])
        sin, cos = r.sine[...], r.cosine[...]
        r.relq[rows, 0:384] = (first * sin - second * cos).astype(BF)
        r.relq[rows, 384:768] = (first * cos + second * sin).astype(BF)
    dq = nn(r.dlog[...], r.feat[:, 768:896]) + nn(r.relq[:, 0:768], r.wr[:, cols])
    r.q[:, cols] = head_join(dq).astype(BF)
    part = tn(r.relq[:, 0:768], stack).astype(BF)
    for piece, share in enumerate((0, 1, 4, 5, 2, 3, 6, 7)):
        c, y, x = share % 2, share // 4, share // 2 % 2
        r.pool[c, y, x, 96:192, cols] = part[96 * piece : 96 * piece + 96]


def norm_back(given, hat, scale, gain):
    push = given * gain
    mean = jnp.mean(push, axis=-1, keepdims=True)
    lean = jnp.mean(push * hat, axis=-1, keepdims=True)
    return scale * (push - mean - hat * lean)


def put_shares(ref, base, cols, part):
    for share in range(8):
        c, y, x = share % 2, share // 4, share // 2 % 2
        ref[c, y, x, pl.ds(base, 96), cols] = part[96 * share : 96 * share + 96].astype(BF)


class Refs:
    pass


CHUNKS = (
    ("g", 384, 128, 384),
    ("g", 512, 256, 512),
    ("g", 0, 192, 0),
    ("g", 192, 192, 192),
    ("pool", 0, 192, 768),
    ("pool", 192, 96, 960),
    ("pool", 288, 96, 1056),
    ("pool", 384, 96, 1152),
)
STAGES = ("core", "xa", "xb", "ya", "yb", "z1", "z2", "z3")
SENDS = tuple("t%d" % i for i in range(1, 8)) + ("b1", "b2", "b3", "cot", "out", "d1", "d2", "d3")
SENDS += tuple("s%d" % i for i in range(5))
SENDS += tuple("%s%d" % (s, u) for u in range(len(CHUNKS)) for s in STAGES)
LOADS = ("x", "cot", "key", "value", "query", "out")
LOADS += tuple("rel%d" % i for i in range(4)) + tuple("up%d" % i for i in range(4))
LOADS += tuple("down%d" % i for i in range(4))
STORES = ("hid0", "hid1", "din", "share", "small")


class Net:
    def __init__(self, r):
        self.r = r
        self.made = {}
        self.order = {"all": [], "end": [], "mid": []}

    def _of(self, name):
        i = SENDS.index(name)
        src, dst, peer = self.made[name]()
        return pltpu.make_async_remote_copy(
            src_ref=src,
            dst_ref=dst,
            send_sem=self.r.send_sem.at[i],
            recv_sem=self.r.recv_sem.at[i],
            device_id=peer,
            device_id_type=pl.DeviceIdType.MESH,
        )

    def start(self, name, make, role="all"):
        self.made[name] = make
        self._of(name).start()
        self.order[role].append(name)

    def got(self, name):
        self._of(name).wait_recv()

    def finish(self, role):
        for name in self.order[role]:
            self._of(name).wait_send()


def add_rows(count, body):
    size = 48 if count % 48 == 0 else 32

    def step(i, carry):
        body(pl.multiple_of(size * i, 16), size)
        return carry

    lax.fori_loop(0, count // size, step, 0)


def total(*terms):
    out = terms[0].astype(F32)
    for term in terms[1:]:
        out = out + term.astype(F32)
    return out.astype(BF)


class Reduction:
    def __init__(self, r, net, dp, z):
        self.r, self.net = r, net
        self.c, self.x, self.y = dp % 2, dp // 2 % 2, dp // 4
        self.pc = (dp + 1 - 2 * self.c, z)
        self.px = (dp + 2 - 4 * self.x, z)
        self.py = (dp + 4 - 8 * self.y, z)
        self.pz1 = (dp, z + 1 - 2 * (z % 2))
        self.pz2 = (dp, (z + 2) % 4)
        self.across = (dp, 3 - z)

    def parts(self, u):
        name, base, rows, out = CHUNKS[u]
        return getattr(self.r, name), base, rows // 2, out, self.r.r1[u], out // 2

    def core(self, u):
        g, base, half, _, r1, _ = self.parts(u)
        self.net.start(
            "core%d" % u, lambda: (g.at[1 - self.c, :, :, pl.ds(base, 2 * half)], r1, self.pc)
        )

    def first(self, u):
        g, base, half, _, r1, at = self.parts(u)
        c, x, y = self.c, self.x, self.y
        self.net.got("core%d" % u)

        def add(i, size):
            for k in range(2):
                rows, own = pl.ds(base + i, size), pl.ds(i, size)
                g[c, k, 1 - x, rows] = total(g[c, k, 1 - x, rows], r1[k, 1 - x, own])
                rows, own = pl.ds(base + half + i, size), pl.ds(half + i, size)
                g[c, 1 - y, k, rows] = total(g[c, 1 - y, k, rows], r1[1 - y, k, own])

        add_rows(half, add)
        a, b, to = pl.ds(base, half), pl.ds(base + half, half), pl.ds(at, half)
        self.net.start("xa%d" % u, lambda: (g.at[c, :, 1 - x, a], self.r.ra.at[:, to], self.px))
        self.net.start("yb%d" % u, lambda: (g.at[c, 1 - y, :, b], self.r.rb.at[:, to], self.py))

    def second(self, u):
        g, base, half, _, r1, at = self.parts(u)
        c, x, y = self.c, self.x, self.y
        ra, rb = self.r.ra, self.r.rb
        self.net.got("xa%d" % u)
        self.net.got("yb%d" % u)

        def add(i, size):
            came = pl.ds(at + i, size)
            rows, own = pl.ds(base + i, size), pl.ds(i, size)
            g[c, 1 - y, x, rows] = total(g[c, 1 - y, x, rows], r1[1 - y, x, own], ra[1 - y, came])
            rows, own = pl.ds(base + half + i, size), pl.ds(half + i, size)
            g[c, y, 1 - x, rows] = total(g[c, y, 1 - x, rows], r1[y, 1 - x, own], rb[1 - x, came])

        add_rows(half, add)
        a, b, to = pl.ds(base, half), pl.ds(base + half, half), pl.ds(at, half)
        self.net.start("ya%d" % u, lambda: (g.at[c, 1 - y, x, a], self.r.ra2.at[to], self.py))
        self.net.start("xb%d" % u, lambda: (g.at[c, y, 1 - x, b], self.r.rb2.at[to], self.px))

    def third(self, u, mid):
        g, base, half, out, r1, at = self.parts(u)
        c, x, y = self.c, self.x, self.y
        ra, rb, ra2, rb2, zr = self.r.ra, self.r.rb, self.r.ra2, self.r.rb2, self.r.zr
        self.net.got("ya%d" % u)
        self.net.got("xb%d" % u)
        if mid:
            self.net.got("z1%d" % u)

        def add(i, size):
            came = pl.ds(at + i, size)
            rows, own = pl.ds(base + i, size), pl.ds(i, size)
            more = (zr[pl.ds(out + i, size)],) if mid else ()
            g[c, y, x, rows] = total(
                g[c, y, x, rows], r1[y, x, own], ra[y, came], ra2[came], *more
            )
            rows, own = pl.ds(base + half + i, size), pl.ds(half + i, size)
            more = (zr[pl.ds(out + half + i, size)],) if mid else ()
            g[c, y, x, rows] = total(
                g[c, y, x, rows], r1[y, x, own], rb[x, came], rb2[came], *more
            )

        add_rows(half, add)
        rows, to = pl.ds(base, 2 * half), pl.ds(out, 2 * half)
        if mid:
            make = lambda: (g.at[c, y, x, rows], self.r.za.at[to], self.across)
            self.net.start("z2%d" % u, make, "mid")
        else:
            make = lambda: (g.at[c, y, x, rows], self.r.zr.at[to], self.pz1)
            self.net.start("z1%d" % u, make, "end")

    def fourth(self, u):
        g, base, half, out, _, _ = self.parts(u)
        c, x, y = self.c, self.x, self.y
        self.net.got("z2%d" % u)

        def add(i, size):
            rows, to = pl.ds(base + i, size), pl.ds(out + i, size)
            self.r.sums[to] = total(g[c, y, x, rows], self.r.za[to])

        add_rows(2 * half, add)
        to = pl.ds(out, 2 * half)
        self.net.start("z3%d" % u, lambda: (self.r.sums.at[to], self.r.sums.at[to], self.pz1), "mid")

    def small(self, i):
        if i:
            self.net.got("s%d" % (i - 1))
            self.r.sm[i] = self.r.sm[i - 1] + self.r.smr[i - 1]
        if i < 5:
            peer = (self.pc, self.px, self.py, self.pz1, self.pz2)[i]
            self.net.start("s%d" % i, lambda: (self.r.sm.at[i], self.r.smr.at[i], peer))


def layer_kernel(names, reduce, *refs):
    r = Refs()
    for name, ref in zip(names, refs):
        setattr(r, name, ref)
    dp, z = lax.axis_index("dp"), lax.axis_index("seq")
    micro = z // 2
    is_mid = lax.rem(z, 3) > 0
    is_end = lax.rem(z, 3) == 0
    peers = {1: (dp, 3 - z), 2: (dp, z + 1 - 2 * (z % 2)), 3: (dp, (z + 2) % 4)}
    net = Net(r)
    red = None
    if reduce:
        r.r1 = tuple(getattr(r, "r1_%d" % u) for u in range(len(CHUNKS)))
        red = Reduction(r, net, dp, z)

    def run(*steps):
        if not reduce:
            return
        for step in steps:
            kind, u = step[0], int(step[1:])
            if kind == "C":
                red.core(u)
            elif kind == "F":
                red.first(u)
            elif kind == "S":
                red.second(u)
            elif kind == "T":
                pl.when(is_end)(lambda: red.third(u, False))
            elif kind == "M":
                pl.when(is_mid)(lambda: red.third(u, True))
            elif kind == "N":
                pl.when(is_mid)(lambda: red.fourth(u))
            elif kind == "s":
                red.small(u)

    def run_at(index, plan):
        for at, steps in plan.items():
            pl.when(index == at)(functools.partial(run, *steps))

    loads = {}

    def load(name, src, dst):
        loads[name] = pltpu.make_async_copy(src, dst, r.load_sem.at[LOADS.index(name)])
        loads[name].start()

    load("x", r.hidden_in.at[micro], r.x.at[0:128])
    load("key", r.w_key, r.wk)
    load("value", r.w_value, r.wv)
    load("query", r.w_query, r.wq)

    greet = list(peers.values()) + ([red.pc, red.px, red.py] if reduce else [])
    barrier = pltpu.get_barrier_semaphore()
    for peer in greet:
        pl.semaphore_signal(barrier, 1, device_id=peer, device_id_type=pl.DeviceIdType.MESH)
    pl.semaphore_wait(barrier, len(greet))

    def slot_rows(slot):
        return r.x.at[128 * slot : 128 * slot + 128]

    @pl.when(is_end)
    def _():
        net.start("t1", lambda: (r.hidden_in.at[1 - micro], r.relay, peers[2]), "end")
        net.start("t2", lambda: (r.hidden_in.at[micro], slot_rows(2), peers[2]), "end")

    @pl.when(is_mid)
    def _():
        net.start("t4", lambda: (r.hidden_in.at[1 - micro], slot_rows(1), peers[1]), "mid")
        net.start("t3", lambda: (r.hidden_in.at[micro], slot_rows(2), peers[2]), "mid")

    for slot in (1, 3, 2):
        far = peers[slot][1] // 2
        net.start(
            "b%d" % slot,
            lambda slot=slot, far=far: (r.boxes.at[:, far], r.bx.at[slot], peers[slot]),
        )
    for i, (dst, src) in enumerate(((0, 0), (192, 384), (384, 192), (576, 576))):
        load("rel%d" % i, r.w_rel.at[src : src + 192], r.wr.at[dst : dst + 192])
    load("out", r.w_out, r.wo)
    for j in range(4):
        load("up%d" % j, r.w_up.at[:, 768 * j : 768 * j + 768], r.pool.at[0, j // 2, j % 2])
    for j in range(4):
        load("down%d" % j, r.w_down.at[768 * j : 768 * j + 768], r.pool.at[1, j // 2, j % 2])
    load("cot", r.cotangent.at[micro], r.cot.at[0:128])

    def project(slot):
        rows = slice(128 * slot, 128 * slot + 128)
        for tile in range(3):
            cols = slice(256 * tile, 256 * tile + 256)
            r.k[rows, cols] = nn(r.x[rows, :], r.wk[:, cols]).astype(BF)
            r.v[rows, cols] = nn(r.x[rows, :], r.wv[:, cols]).astype(BF)
            if slot < 2:
                r.q[rows, cols] = nn(r.x[rows, :], r.wq[:, cols]).astype(BF)

    for j in range(4):
        r.vectors[j : j + 1, :] = r.vector0[768 * j : 768 * j + 768].astype(F32).reshape(1, 768)
        row = getattr(r, "vector%d" % (j + 1))[...]
        r.vectors[4 + j : 5 + j, :] = row.astype(F32).reshape(1, 768)
    for axis in range(2):
        r.bx[0, axis : axis + 1, :] = r.boxes[axis, pl.ds(micro, 1), :]
    features(0, r)
    loads["x"].wait()
    loads["key"].wait()
    loads["value"].wait()
    loads["query"].wait()
    project(0)

    @pl.when(is_mid)
    def _():
        net.made["t1"] = lambda: (r.hidden_in.at[1 - micro], r.relay, peers[2])
        net.got("t1")
        net.start("t5", lambda: (r.relay, slot_rows(3), peers[1]), "mid")
        net.got("t4")
        net.start("t6", lambda: (slot_rows(1), slot_rows(3), peers[2]), "mid")

    for slot in (1, 2, 3):
        net.got("b%d" % slot)
        features(slot, r)
    for i in range(4):
        loads["rel%d" % i].wait()

    pl.when(is_mid)(lambda: net.got("t2"))
    pl.when(is_end)(lambda: net.got("t3"))
    project(2)

    @pl.when(is_mid)
    def _():
        net.got("t5")
        net.start("t7", lambda: (slot_rows(3), slot_rows(1), peers[2]), "mid")

    pl.when(is_end)(lambda: net.got("t6"))
    project(3)
    pl.when(is_end)(lambda: net.got("t7"))
    net.start("cot", lambda: (r.cotangent.at[1 - micro], r.cot.at[128:256], peers[1]))
    project(1)

    lane = lax.broadcasted_iota(jnp.int32, (1, 128), 1)
    length = r.lengths[micro]
    blocks = (z, peers[1][1], peers[2][1], peers[3][1])
    live = jnp.concatenate([lane + 128 * block < length for block in blocks], axis=1)

    def attend(pair, carry):
        attend_pair(pair, live, r)
        return carry

    lax.fori_loop(0, PAIRS, attend, 0)

    loads["out"].wait()
    for tile in range(3):
        cols = slice(256 * tile, 256 * tile + 256)
        r.res[:, cols] = r.x[0:256, cols].astype(F32) + nn(r.att[...], r.wo[:, cols])

    gain1, bias1, gain2, bias2 = [r.vectors[4 + i : 5 + i, :] for i in range(4)]
    for block in range(4):
        rows = slice(64 * block, 64 * block + 64)
        res = r.res[rows, :]
        center = res - jnp.mean(res, axis=-1, keepdims=True)
        scale = lax.rsqrt(jnp.mean(center * center, axis=-1, keepdims=True) + EPS)
        hat = center * scale
        r.hat[rows, :] = hat
        r.scale[rows, :] = jnp.broadcast_to(scale, (64, 128))
        normed = hat * gain1 + bias1
        r.res[rows, :] = normed
        r.low[rows, :] = normed.astype(BF)

    for j in range(4):
        loads["up%d" % j].wait()
    for j in range(4):
        loads["down%d" % j].wait()

    def up_tile(tile):
        j = tile // 3
        return j // 2, j % 2, pl.ds(pl.multiple_of(256 * (tile % 3), 256), 256)

    def up(tile, carry):
        cols = pl.ds(pl.multiple_of(256 * tile, 256), 256)
        y, x, part = up_tile(tile)
        bias = r.vectors[pl.ds(tile // 3, 1), part]
        value = nn(r.low[...], r.pool[0, y, x, :, part]) + bias
        below = 0.5 * (1.0 + lax.erf(value * np.float32(np.sqrt(0.5))))
        dense = jnp.exp(value * value * -0.5) * np.float32(1.0 / np.sqrt(2.0 * np.pi))
        r.act[:, cols] = (value * below).astype(BF)
        slope = below + value * dense
        top = slope.astype(BF)
        r.g[0, y, x, 0:256, part] = top
        r.g[1, y, x, 0:256, part] = (slope - top.astype(F32)).astype(BF)
        return carry

    lax.fori_loop(0, 12, up, 0)
    for tile in range(3):
        cols = slice(256 * tile, 256 * tile + 256)
        r.res[:, cols] = r.res[:, cols] + sum(
            nn(r.act[:, 768 * j : 768 * j + 768], r.pool[1, j // 2, j % 2, :, cols])
            for j in range(4)
        )

    loads["cot"].wait()
    net.got("cot")
    sums = [jnp.zeros((1, 768), F32) for _ in range(4)]
    for block in range(4):
        rows = slice(64 * block, 64 * block + 64)
        res = r.res[rows, :]
        center = res - jnp.mean(res, axis=-1, keepdims=True)
        scale = lax.rsqrt(jnp.mean(center * center, axis=-1, keepdims=True) + EPS)
        hat = center * scale
        r.out[rows, :] = (hat * gain2 + bias2).astype(BF)
        given = r.cot[rows, :].astype(F32)
        sums[2] = sums[2] + jnp.sum(given * hat, axis=0, keepdims=True)
        sums[3] = sums[3] + jnp.sum(given, axis=0, keepdims=True)
        dres = norm_back(given, hat, scale, gain2)
        r.res[rows, :] = dres
        r.dlow[rows, :] = dres.astype(BF)

    def grad_down(offset, size, share, carry):
        cols = pl.ds(pl.multiple_of(384 * share + offset, 128), size)
        r.g[share % 2, share // 4, share // 2 % 2, 384 + offset : 384 + offset + size, :] = tn(
            r.act[:, cols], r.dlow[...]
        ).astype(BF)
        return carry

    lax.fori_loop(0, 8, functools.partial(grad_down, 0, 128), 0)
    run("C0")
    lax.fori_loop(0, 8, functools.partial(grad_down, 128, 256), 0)
    run("C1")
    stores = {}

    def store(name, src, dst):
        stores[name] = pltpu.make_async_copy(src, dst, r.store_sem.at[STORES.index(name)])
        stores[name].start()

    net.start("out", lambda: (r.out.at[128:256], r.outr, peers[1]))

    def up_back(tile, carry):
        cols = pl.ds(pl.multiple_of(256 * tile, 256), 256)
        y, x, part = up_tile(tile)
        slope = r.g[0, y, x, 0:256, part].astype(F32) + r.g[1, y, x, 0:256, part].astype(F32)
        push = nt(r.dlow[...], r.pool[1, y, x, part, :]) * slope
        low = push.astype(BF)
        r.act[:, cols] = low
        r.sm[0, pl.ds(tile // 3, 1), part] = jnp.sum(low.astype(F32), axis=0, keepdims=True)
        run_at(tile, PLAN["up_back"])
        return carry

    lax.fori_loop(0, 12, up_back, 0)

    def grad_up(tile, carry):
        cols = pl.ds(pl.multiple_of(256 * tile, 256), 256)
        _, _, dest = up_tile(tile)
        put_shares(r.g, pl.multiple_of(96 * (tile // 3), 32), dest, tn(r.low[...], r.act[:, cols]))
        run_at(tile, PLAN["grad_up"])
        return carry

    lax.fori_loop(0, 12, grad_up, 0)
    for tile in range(3):
        cols = slice(256 * tile, 256 * tile + 256)
        r.res[:, cols] = r.res[:, cols] + sum(
            nt(r.act[:, 768 * j : 768 * j + 768], r.pool[0, j // 2, j % 2, cols, :])
            for j in range(4)
        )
    for block in range(4):
        rows = slice(64 * block, 64 * block + 64)
        given, hat = r.res[rows, :], r.hat[rows, :]
        sums[0] = sums[0] + jnp.sum(given * hat, axis=0, keepdims=True)
        sums[1] = sums[1] + jnp.sum(given, axis=0, keepdims=True)
        dres = norm_back(given, hat, r.scale[rows, 0:1], gain1)
        r.res[rows, :] = dres
        r.dlow[rows, :] = dres.astype(BF)
    for row in range(4):
        r.sm[0, 4 + row : 5 + row, :] = sums[row]
    run(*PLAN["norm"])
    for tile in range(3):
        cols = slice(256 * tile, 256 * tile + 256)
        put_shares(r.pool, 0, cols, tn(r.att[...], r.dlow[:, cols]))
    for tile in range(3):
        cols = slice(256 * tile, 256 * tile + 256)
        r.att[:, cols] = nt(r.dlow[...], r.wo[cols, :]).astype(BF)

    def attend_back(pair, carry):
        attend_pair_back(pair, r)
        run_at(pair, PLAN["pairs"])
        return carry

    lax.fori_loop(0, PAIRS, attend_back, 0)
    run("C4")
    for tile in range(3):
        cols = slice(256 * tile, 256 * tile + 256)
        put_shares(r.pool, 192, cols, tn(r.x[0:256, :], r.q[:, cols]))
    run("C5", *PLAN["query"])
    for tile in range(3):
        cols = slice(256 * tile, 256 * tile + 256)
        put_shares(r.pool, 288, cols, tn(r.x[...], r.k[:, cols]))
    run("C6", *PLAN["key"])
    for tile in range(3):
        cols = slice(256 * tile, 256 * tile + 256)
        put_shares(r.pool, 384, cols, tn(r.x[...], r.v[:, cols]))
    run("C7", *PLAN["value"])

    for tile in range(3):
        cols = slice(256 * tile, 256 * tile + 256)
        tail = nt(r.k[...], r.wk[cols, :]) + nt(r.v[...], r.wv[cols, :])
        r.relq[256:512, cols] = tail[256:512].astype(BF)
        r.relq[0:256, cols] = (
            tail[0:256] + r.res[:, cols] + nt(r.q[...], r.wq[cols, :])
        ).astype(BF)
    for slot in (1, 3, 2):
        rows = slice(128 * slot, 128 * slot + 128)
        net.start(
            "d%d" % slot,
            lambda slot=slot, rows=rows: (
                r.relq.at[rows, 0:768],
                r.dxr.at[slot - 1],
                peers[slot],
            ),
        )
    run(*PLAN["input"])
    store("hid0", r.out.at[0:128], r.hidden_out.at[micro])
    net.got("out")
    store("hid1", r.outr, r.hidden_out.at[1 - micro])
    run(*PLAN["tail"])
    for slot in (1, 2, 3):
        net.got("d%d" % slot)
    r.din[micro] = (r.relq[0:128, 0:768].astype(F32) + r.dxr[1].astype(F32)).astype(BF)
    r.din[1 - micro] = (r.dxr[0].astype(F32) + r.dxr[2].astype(F32)).astype(BF)
    store("din", r.din, r.input_grad)
    run(*PLAN["last"])
    if reduce:
        store("small", r.sm.at[5], r.small)

        @pl.when(is_end)
        def _():
            for u in range(len(CHUNKS)):
                net.got("z3%d" % u)

        store("share", r.sums, r.share)
    else:
        store("small", r.sm.at[0], r.small)
        store("share", r.g, r.share.at[0])
        last = pltpu.make_async_copy(r.pool, r.share.at[1], r.load_sem.at[0])
        last.start()
        last.wait()
    for copy in stores.values():
        copy.wait()
    net.finish("all")
    pl.when(is_end)(lambda: net.finish("end"))
    pl.when(is_mid)(lambda: net.finish("mid"))


PLAN = {
    "up_back": {4: ("F0",), 9: ("F1",)},
    "grad_up": {5: ("C2",), 11: ("C3",)},
    "norm": ("S0", "F2", "s0"),
    "pairs": {2: ("S1", "F3", "s1"), 3: ("T0",), 5: ("s2",)},
    "query": ("S2", "F4"),
    "key": ("M0", "T1"),
    "value": ("F5",),
    "input": ("s3",),
    "tail": ("M1", "T2", "S3", "N0", "F6", "M2", "N1", "S4", "F7", "s4", "T3", "N2", "S5", "M3"),
    "last": ("T4", "S6", "N3", "M4", "T5", "s5", "S7", "N4", "M5", "T6", "N5", "M6", "T7")
    + ("N6", "M7", "N7"),
}


def scratch(reduce):
    shapes = [
        ("x", (512, 768), BF),
        ("relay", (128, 768), BF),
        ("bx", (4, 2, 128), jnp.int32),
        ("cot", (256, 768), BF),
        ("vectors", (8, 768), F32),
        ("wq", (768, 768), BF),
        ("wk", (768, 768), BF),
        ("wv", (768, 768), BF),
        ("wo", (768, 768), BF),
        ("wr", (768, 768), BF),
        ("pool", (2, 2, 2, 768, 768), BF),
        ("g", (2, 2, 2, 768, 768), BF),
        ("sine", (256, 384), F32),
        ("cosine", (256, 384), F32),
        ("feat", (512, 896), BF),
        ("q", (256, 768), BF),
        ("k", (512, 768), BF),
        ("v", (512, 768), BF),
        ("att", (256, 768), BF),
        ("relq", (512, 896), BF),
        ("score", (512, 512), F32),
        ("dlog", (512, 512), BF),
        ("probs", (PAIRS, 512, 512), BF),
        ("res", (256, 768), F32),
        ("hat", (256, 768), F32),
        ("scale", (256, 128), F32),
        ("low", (256, 768), BF),
        ("act", (256, 3072), BF),
        ("dlow", (256, 768), BF),
        ("out", (256, 768), BF),
        ("outr", (128, 768), BF),
        ("dxr", (3, 128, 768), BF),
        ("din", (2, 128, 768), BF),
        ("sm", (6, 8, 768), F32),
    ]
    if reduce:
        shapes += [("r1_%d" % u, (2, 2, c[2], 768), BF) for u, c in enumerate(CHUNKS)]
        shapes += [
            ("ra", (2, 624, 768), BF),
            ("rb", (2, 624, 768), BF),
            ("ra2", (624, 768), BF),
            ("rb2", (624, 768), BF),
            ("zr", (1248, 768), BF),
            ("za", (1248, 768), BF),
            ("sums", (1248, 768), BF),
            ("smr", (5, 8, 768), F32),
        ]
    return shapes


def layer(lengths, hidden_in, boxes, cotangent, vectors, weights, reduce):
    hi, lo = trig_tables(QUARTER)
    any_space = pl.BlockSpec(memory_space=pl.ANY)
    vmem = pl.BlockSpec(memory_space=pltpu.VMEM)
    ins = (
        ("lengths", lengths.reshape(-1), pl.BlockSpec(memory_space=pltpu.SMEM)),
        ("hidden_in", hidden_in, any_space),
        ("cotangent", cotangent, any_space),
        ("boxes", boxes, vmem),
        ("hi", jnp.asarray(hi), vmem),
        ("lo", jnp.asarray(lo), vmem),
    )
    ins += tuple(("vector%d" % i, v, vmem) for i, v in enumerate(vectors))
    ins += tuple((name, w, any_space) for name, w in weights)
    outs = (
        ("hidden_out", (2, 128, 768), BF),
        ("input_grad", (2, 128, 768), BF),
        ("share", (1248, 768) if reduce else (2, 2, 2, 2, 768, 768), BF),
        ("small", (8, 768), F32),
    )
    shapes = scratch(reduce)
    sems = ("send_sem", "recv_sem", "load_sem", "store_sem")
    names = tuple(i[0] for i in ins) + tuple(o[0] for o in outs)
    names += tuple(s[0] for s in shapes) + sems
    dma = pltpu.SemaphoreType.DMA
    return pl.pallas_call(
        functools.partial(layer_kernel, names, reduce),
        out_shape=[jax.ShapeDtypeStruct(o[1], o[2]) for o in outs],
        in_specs=[i[2] for i in ins],
        out_specs=[any_space] * len(outs),
        scratch_shapes=[pltpu.VMEM(s[1], s[2]) for s in shapes]
        + [dma((len(SENDS),)), dma((len(SENDS),)), dma((len(LOADS),)), dma((len(STORES),))],
        compiler_params=pltpu.CompilerParams(
            vmem_limit_bytes=VMEM_LIMIT, collective_id=0, has_side_effects=True
        ),
        name="layer",
    )(*[i[1] for i in ins])


def finish_kernel(share, small, hid, din, hidden, dinput, dq, dk, dv, dout, drel, dup, *rest):
    dbup, ddown, vectors = rest[0], rest[1], rest[2:]
    hidden[...] = hid[...]
    dinput[...] = din[...]
    for j in range(4):
        dup[:, 768 * j : 768 * j + 768] = share[96 * j : 96 * j + 96, :].astype(F32)
    ddown[...] = share[384:768, :].astype(F32)
    for i, ref in enumerate((dout, drel, dq, dk, dv)):
        ref[...] = share[768 + 96 * i : 864 + 96 * i, :].astype(F32)
    dp = lax.axis_index("dp")
    row = small[pl.ds(dp // 2, 1), :]
    dbup[...] = jnp.where(dp % 2 == 0, row[:, 0:384], row[:, 384:768]).reshape(384)
    turned = pltpu.roll(small[...], lax.rem(768 - 96 * dp, 768), 1)
    for i, ref in enumerate(vectors):
        ref[...] = turned[4 + i : 5 + i, 0:96].reshape(96)


def finish(share, small, hidden, dinput):
    shapes = [(96, 768)] * 5 + [(96, 3072), (384,), (384, 768)] + [(96,)] * 4
    low = jax.ShapeDtypeStruct(hidden.shape, BF)
    return pl.pallas_call(
        finish_kernel,
        out_shape=[low, low] + [jax.ShapeDtypeStruct(s, F32) for s in shapes],
        name="finish",
    )(share, small, hidden, dinput)


def finish_any(g, small):
    order = g.transpose(0, 2, 3, 1, 4, 5).reshape(2, 8, 768, 768)

    def weight(which, base):
        return order[which, :, base : base + 96].reshape(768, 768)

    up = jnp.concatenate([weight(0, 96 * j) for j in range(4)], axis=1)
    down = order[0, :, 384:768].reshape(3072, 768)
    full = [weight(1, base) for base in (192, 288, 384, 0, 96)] + [up, down]
    grads = [
        lax.psum(lax.psum_scatter(w, "dp", scatter_dimension=0, tiled=True), "seq").astype(F32)
        for w in full
    ]
    small = lax.psum(small, ("dp", "seq"))
    dp, count = lax.axis_index("dp"), lax.axis_size("dp")

    def own_part(vector):
        size = vector.shape[0] // count
        return lax.dynamic_slice_in_dim(vector, dp * size, size)

    parts = [own_part(small[4 + i]) for i in range(4)]
    return grads[:6] + [own_part(small[0:4].reshape(-1)), grads[6]] + parts


def shards(
    hidden_in,
    boxes,
    lengths,
    w_query,
    w_key,
    w_value,
    w_out,
    w_rel,
    w_up,
    b_up,
    w_down,
    gain_attn,
    bias_attn,
    gain_ffn,
    bias_ffn,
    cotangent,
):
    vectors = (b_up, gain_attn, bias_attn, gain_ffn, bias_ffn)
    weights = (
        ("w_query", w_query),
        ("w_key", w_key),
        ("w_value", w_value),
        ("w_out", w_out),
        ("w_rel", w_rel),
        ("w_up", w_up),
        ("w_down", w_down),
    )
    reduce = lax.axis_size("dp") == 8
    hidden, dinput, share, small = layer(
        lengths,
        hidden_in[:, 0],
        boxes[:, :, 0],
        cotangent[:, 0],
        vectors,
        weights,
        reduce,
    )
    if reduce:
        hidden, dinput, *rest = finish(share, small, hidden, dinput)
    else:
        rest = finish_any(share, small)
    return (hidden[:, None], dinput[:, None], *rest)


def solution(mesh):
    rows = P(None, "dp", "seq", None)
    placed = (rows, P(None, None, "dp", "seq"), P(None, "dp")) + (P(),) * 12 + (rows,)
    matrix, vector = P("dp", None), P("dp")
    return jax.shard_map(
        shards,
        mesh=mesh,
        in_specs=placed,
        out_specs=(rows, rows) + (matrix,) * 6 + (vector, matrix) + (vector,) * 4,
        check_vma=False,
    )
```

```python
import functools

import jax
import jax.numpy as jnp
import numpy as np
from jax import lax
from jax.experimental import pallas as pl
from jax.experimental.pallas import tpu as pltpu
from jax.sharding import PartitionSpec as P

HEADS = 12
EPS = 1e-05
BF = jnp.bfloat16
F32 = jnp.float32
PAIRS = HEADS // 2
VMEM_LIMIT = 67043328
QUARTER = 192


def nn(a, b):
    return lax.dot_general(a, b, (((1,), (0,)), ((), ())), preferred_element_type=F32)


def nt(a, b):
    return lax.dot_general(a, b, (((1,), (1,)), ((), ())), preferred_element_type=F32)


def tn(a, b):
    return lax.dot_general(a, b, (((0,), (0,)), ((), ())), preferred_element_type=F32)


def trig_tables(quarter):
    freq = 10000.0 ** (-np.arange(quarter) / quarter)
    tables = []
    for step in (32.0, 1.0):
        angle = step * np.arange(32)[:, None] * freq[None, :]
        rest = np.concatenate([np.sin(angle), np.cos(angle)], axis=1).astype(np.float32)
        parts = []
        for _ in range(3):
            part = rest.astype(BF)
            parts.append(part)
            rest = rest - part.astype(np.float32)
        tables.append(np.concatenate(parts, axis=0))
    return tables


def features(slot, c, micro, r):
    half = 2 * QUARTER
    iota = lax.broadcasted_iota(jnp.int32, (32, 128), 0)
    hi_tab, lo_tab = r.hi[...], r.lo[...]
    block = pltpu.roll(r.meta[slot], 64 * c, 1)
    sines, cosines = [], []
    for axis in range(2):
        where = jnp.where(micro == 0, block[axis : axis + 1], block[2 + axis : 3 + axis])
        pick_hi = (iota == lax.shift_right_logical(where, 5)).astype(F32).astype(BF)
        pick_lo = (iota == (where & 31)).astype(F32).astype(BF)
        hi = tn(jnp.concatenate([pick_hi] * 3, axis=0), hi_tab)
        lo = tn(jnp.concatenate([pick_lo] * 3, axis=0), lo_tab)
        sin_hi, cos_hi = hi[:, :QUARTER], hi[:, QUARTER:]
        sin_lo, cos_lo = lo[:, :QUARTER], lo[:, QUARTER:]
        sines.append(sin_hi * cos_lo + cos_hi * sin_lo)
        cosines.append(cos_hi * cos_lo - sin_hi * sin_lo)
    sine = jnp.concatenate(sines, axis=1)
    cosine = jnp.concatenate(cosines, axis=1)
    for part in range(2):
        mine = slice(64 * part, 64 * part + 64)
        rows = pl.ds(256 * part + 64 * slot, 64)
        r.feat[rows, 0:half] = cosine[mine].astype(BF)
        r.feat[rows, half : 2 * half] = sine[mine].astype(BF)
    rows = pl.ds(64 * slot, 64)
    r.sine[rows, :] = sine[0:64]
    r.cosine[rows, :] = cosine[0:64]


def head_stack(pair):
    first = lax.broadcasted_iota(jnp.int32, pair.shape, 1) < 64
    zero = jnp.zeros_like(pair)
    return jnp.concatenate([jnp.where(first, pair, zero), jnp.where(first, zero, pair)], axis=0)


def head_join(stack):
    half = stack.shape[0] // 2
    first = lax.broadcasted_iota(jnp.int32, (half, 128), 1) < 64
    return jnp.where(first, stack[:half], stack[half:])


def attend_pair(pair, live, r):
    cols = pl.ds(pl.multiple_of(128 * pair, 128), 128)
    stack = head_stack(r.q[:, cols].astype(F32) * 0.125).astype(BF)
    for head in range(2):
        rows = slice(256 * head, 256 * head + 256)
        left = nt(stack[rows], r.wr[0:384, cols])
        right = nt(stack[rows], r.wr[384:768, cols])
        sin, cos = r.sine[...], r.cosine[...]
        r.relq[rows, 0:384] = (left * sin + right * cos).astype(BF)
        r.relq[rows, 384:768] = (right * sin - left * cos).astype(BF)
    r.relq[:, 768:896] = stack
    r.feat[:, 768:896] = r.k[:, cols]
    r.score[...] = nt(r.relq[...], r.feat[...])
    for block in range(8):
        rows = pl.ds(64 * block, 64)
        score = jnp.where(live, r.score[rows, :], -1e30)
        top = jnp.max(score, axis=-1, keepdims=True)
        weight = jnp.exp(score - top)
        total = jnp.sum(weight, axis=-1, keepdims=True)
        r.probs[pair, rows, :] = (weight * (1.0 / total)).astype(BF)
    r.att[:, cols] = head_join(nn(r.probs[pair], r.v[:, cols])).astype(BF)


def attend_pair_back(pair, r):
    cols = pl.ds(pl.multiple_of(128 * pair, 128), 128)
    given = head_stack(r.att[:, cols].astype(F32)).astype(BF)
    stack = head_stack(r.q[:, cols].astype(F32)).astype(BF)
    r.score[...] = nt(given, r.v[:, cols])
    for block in range(8):
        rows = pl.ds(64 * block, 64)
        prob = r.probs[pair, rows, :].astype(F32)
        push = prob * r.score[rows, :]
        mean = jnp.sum(push, axis=-1, keepdims=True)
        r.dlog[rows, :] = ((push - prob * mean) * 0.125).astype(BF)
    r.feat[:, 768:896] = r.k[:, cols]
    r.v[:, cols] = tn(r.probs[pair], given).astype(BF)
    r.k[:, cols] = tn(r.dlog[...], stack).astype(BF)
    for head in range(2):
        rows = slice(256 * head, 256 * head + 256)
        first = nn(r.dlog[rows, :], r.feat[:, 0:384])
        second = nn(r.dlog[rows, :], r.feat[:, 384:768])
        sin, cos = r.sine[...], r.cosine[...]
        r.relq[rows, 0:384] = (first * sin - second * cos).astype(BF)
        r.relq[rows, 384:768] = (first * cos + second * sin).astype(BF)
    dq = nn(r.dlog[...], r.feat[:, 768:896]) + nn(r.relq[:, 0:768], r.wr[:, cols])
    r.q[:, cols] = head_join(dq).astype(BF)
    part = tn(r.relq[:, 0:768], stack).astype(BF)
    for piece, share in enumerate((0, 1, 4, 5, 2, 3, 6, 7)):
        c, y, x = share % 2, share // 4, share // 2 % 2
        r.pool[c, y, x, 96:192, cols] = part[96 * piece : 96 * piece + 96]


def norm_back(given, hat, scale, gain):
    push = given * gain
    mean = jnp.mean(push, axis=-1, keepdims=True)
    lean = jnp.mean(push * hat, axis=-1, keepdims=True)
    return scale * (push - mean - hat * lean)


def put_shares(ref, base, cols, part):
    for share in range(8):
        c, y, x = share % 2, share // 4, share // 2 % 2
        ref[c, y, x, pl.ds(base, 96), cols] = part[96 * share : 96 * share + 96].astype(BF)


class Refs:
    pass


CHUNKS = (
    ("g", 384, 128, 384),
    ("g", 512, 256, 512),
    ("g", 0, 192, 0),
    ("g", 192, 192, 192),
    ("pool", 0, 192, 768),
    ("pool", 192, 96, 960),
    ("pool", 288, 96, 1056),
    ("pool", 384, 96, 1152),
)
STAGES = ("core", "xa", "xb", "ya", "yb", "z1", "z2", "z3")
BLOCKS = ("x", "m", "c", "f", "o", "d")
SENDS = tuple(k + str(i) for k in BLOCKS for i in range(4)) + ("dx0",)
SENDS += tuple("s%d" % i for i in range(5))
SENDS += tuple("%s%d" % (s, u) for u in range(len(CHUNKS)) for s in STAGES)
LOADS = ("x", "x2", "cot", "key", "value", "query", "out")
LOADS += tuple("rel%d" % i for i in range(4)) + tuple("up%d" % i for i in range(4))
LOADS += tuple("down%d" % i for i in range(4))
STORES = ("hid", "din", "share", "small")
POSTS = tuple(k + i for k in "xmc" for i in ("a0", "a1", "b0", "b1", "p"))
POSTS += tuple(k + str(i) for k in "fod" for i in range(4)) + ("dx",)


class Net:
    def __init__(self, r):
        self.r = r
        self.made = {}
        self.order = {"all": [], "end": [], "mid": []}
        self.posts = {"all": [], "own": [], "far": []}

    def _of(self, name):
        i = SENDS.index(name)
        src, dst, peer = self.made[name]()
        return pltpu.make_async_remote_copy(
            src_ref=src,
            dst_ref=dst,
            send_sem=self.r.send_sem.at[i],
            recv_sem=self.r.recv_sem.at[i],
            device_id=peer,
            device_id_type=pl.DeviceIdType.MESH,
        )

    def start(self, name, make, role="all"):
        self.made[name] = make
        self._of(name).start()
        self.order[role].append(name)

    def got(self, name):
        self._of(name).wait_recv()

    def _post(self, name, src, dst, at, peer):
        return pltpu.make_async_remote_copy(
            src_ref=src,
            dst_ref=dst,
            send_sem=self.r.post_sem.at[POSTS.index(name)],
            recv_sem=self.r.recv_sem.at[at],
            device_id=peer,
            device_id_type=pl.DeviceIdType.MESH,
        )

    def post(self, name, kind, index, make, role="all"):
        src, dst, peer = make()
        self._post(name, src, dst, SENDS.index(kind + "0") + index, peer).start()
        self.posts[role].append((name, kind, index, make))

    def came(self, kind, index, make):
        src, dst, peer = make()
        self._post(POSTS[0], src, dst, SENDS.index(kind + "0") + index, peer).wait_recv()

    def finish(self, role):
        for name in self.order[role]:
            self._of(name).wait_send()

    def posted(self, role):
        for name, kind, index, make in self.posts[role]:
            src, dst, peer = make()
            self._post(name, src, dst, SENDS.index(kind + "0") + index, peer).wait_send()


def add_rows(count, body):
    size = 48 if count % 48 == 0 else 32

    def step(i, carry):
        body(pl.multiple_of(size * i, 16), size)
        return carry

    lax.fori_loop(0, count // size, step, 0)


def total(*terms):
    out = terms[0].astype(F32)
    for term in terms[1:]:
        out = out + term.astype(F32)
    return out.astype(BF)


class Reduction:
    def __init__(self, r, net, dp, z):
        self.r, self.net = r, net
        self.c, self.x, self.y = dp % 2, dp // 2 % 2, dp // 4
        self.pc = (dp + 1 - 2 * self.c, z)
        self.px = (dp + 2 - 4 * self.x, z)
        self.py = (dp + 4 - 8 * self.y, z)
        self.pz1 = (dp, z + 1 - 2 * (z % 2))
        self.pz2 = (dp, (z + 2) % 4)
        self.across = (dp, 3 - z)

    def parts(self, u):
        name, base, rows, out = CHUNKS[u]
        return getattr(self.r, name), base, rows // 2, out, self.r.r1[u], out // 2

    def core(self, u):
        g, base, half, _, r1, _ = self.parts(u)
        self.net.start(
            "core%d" % u, lambda: (g.at[1 - self.c, :, :, pl.ds(base, 2 * half)], r1, self.pc)
        )

    def first(self, u):
        g, base, half, _, r1, at = self.parts(u)
        c, x, y = self.c, self.x, self.y
        self.net.got("core%d" % u)

        def add(i, size):
            for k in range(2):
                rows, own = pl.ds(base + i, size), pl.ds(i, size)
                g[c, k, 1 - x, rows] = total(g[c, k, 1 - x, rows], r1[k, 1 - x, own])
                rows, own = pl.ds(base + half + i, size), pl.ds(half + i, size)
                g[c, 1 - y, k, rows] = total(g[c, 1 - y, k, rows], r1[1 - y, k, own])

        add_rows(half, add)
        a, b, to = pl.ds(base, half), pl.ds(base + half, half), pl.ds(at, half)
        self.net.start("xa%d" % u, lambda: (g.at[c, :, 1 - x, a], self.r.ra.at[:, to], self.px))
        self.net.start("yb%d" % u, lambda: (g.at[c, 1 - y, :, b], self.r.rb.at[:, to], self.py))

    def second(self, u):
        g, base, half, _, r1, at = self.parts(u)
        c, x, y = self.c, self.x, self.y
        ra, rb = self.r.ra, self.r.rb
        self.net.got("xa%d" % u)
        self.net.got("yb%d" % u)

        def add(i, size):
            came = pl.ds(at + i, size)
            rows, own = pl.ds(base + i, size), pl.ds(i, size)
            g[c, 1 - y, x, rows] = total(g[c, 1 - y, x, rows], r1[1 - y, x, own], ra[1 - y, came])
            rows, own = pl.ds(base + half + i, size), pl.ds(half + i, size)
            g[c, y, 1 - x, rows] = total(g[c, y, 1 - x, rows], r1[y, 1 - x, own], rb[1 - x, came])

        add_rows(half, add)
        a, b, to = pl.ds(base, half), pl.ds(base + half, half), pl.ds(at, half)
        self.net.start("ya%d" % u, lambda: (g.at[c, 1 - y, x, a], self.r.ra2.at[to], self.py))
        self.net.start("xb%d" % u, lambda: (g.at[c, y, 1 - x, b], self.r.rb2.at[to], self.px))

    def third(self, u, mid):
        g, base, half, out, r1, at = self.parts(u)
        c, x, y = self.c, self.x, self.y
        ra, rb, ra2, rb2, zr = self.r.ra, self.r.rb, self.r.ra2, self.r.rb2, self.r.zr
        self.net.got("ya%d" % u)
        self.net.got("xb%d" % u)
        if mid:
            self.net.got("z1%d" % u)

        def add(i, size):
            came = pl.ds(at + i, size)
            rows, own = pl.ds(base + i, size), pl.ds(i, size)
            more = (zr[pl.ds(out + i, size)],) if mid else ()
            g[c, y, x, rows] = total(
                g[c, y, x, rows], r1[y, x, own], ra[y, came], ra2[came], *more
            )
            rows, own = pl.ds(base + half + i, size), pl.ds(half + i, size)
            more = (zr[pl.ds(out + half + i, size)],) if mid else ()
            g[c, y, x, rows] = total(
                g[c, y, x, rows], r1[y, x, own], rb[x, came], rb2[came], *more
            )

        add_rows(half, add)
        rows, to = pl.ds(base, 2 * half), pl.ds(out, 2 * half)
        if mid:
            make = lambda: (g.at[c, y, x, rows], self.r.za.at[to], self.across)
            self.net.start("z2%d" % u, make, "mid")
        else:
            make = lambda: (g.at[c, y, x, rows], self.r.zr.at[to], self.pz1)
            self.net.start("z1%d" % u, make, "end")

    def fourth(self, u):
        g, base, half, out, _, _ = self.parts(u)
        c, x, y = self.c, self.x, self.y
        self.net.got("z2%d" % u)

        def add(i, size):
            rows, to = pl.ds(base + i, size), pl.ds(out + i, size)
            self.r.sums[to] = total(g[c, y, x, rows], self.r.za[to])

        add_rows(2 * half, add)
        to = pl.ds(out, 2 * half)
        self.net.start("z3%d" % u, lambda: (self.r.sums.at[to], self.r.sums.at[to], self.pz1), "mid")

    def small(self, i):
        if i:
            self.net.got("s%d" % (i - 1))
            self.r.sm[i] = self.r.sm[i - 1] + self.r.smr[i - 1]
        if i < 5:
            peer = (self.pc, self.px, self.py, self.pz1, self.pz2)[i]
            self.net.start("s%d" % i, lambda: (self.r.sm.at[i], self.r.smr.at[i], peer))


def layer_kernel(names, reduce, *refs):
    r = Refs()
    for name, ref in zip(names, refs):
        setattr(r, name, ref)
    dp, z = lax.axis_index("dp"), lax.axis_index("seq")
    micro, c = z // 2, dp % 2
    is_mid = lax.rem(z, 3) > 0
    is_end = lax.rem(z, 3) == 0
    own = c == z % 2
    far = c != z % 2
    base = jnp.where(own, 0, 1)
    column = dp - c
    source = column + z % 2
    pair = (dp + 1 - 2 * c, z)
    half = pl.ds(pl.multiple_of(64 * c, 64), 64)
    other = pl.ds(pl.multiple_of(64 - 64 * c, 64), 64)
    net = Net(r)
    red = None
    if reduce:
        r.r1 = tuple(getattr(r, "r1_%d" % u) for u in range(len(CHUNKS)))
        red = Reduction(r, net, dp, z)

    def run(*steps):
        if not reduce:
            return
        for step in steps:
            kind, u = step[0], int(step[1:])
            if kind == "C":
                red.core(u)
            elif kind == "F":
                red.first(u)
            elif kind == "S":
                red.second(u)
            elif kind == "T":
                pl.when(is_end)(lambda: red.third(u, False))
            elif kind == "M":
                pl.when(is_mid)(lambda: red.third(u, True))
            elif kind == "N":
                pl.when(is_mid)(lambda: red.fourth(u))
            elif kind == "s":
                red.small(u)

    def run_at(index, plan):
        for at, steps in plan.items():
            pl.when(index == at)(functools.partial(run, *steps))

    loads = {}

    def load(name, src, dst):
        loads[name] = lambda: (src(), dst(), r.load_sem.at[LOADS.index(name)])
        pltpu.make_async_copy(*loads[name]()).start()

    def loaded(name):
        pltpu.make_async_copy(*loads[name]()).wait()

    load("key", lambda: r.w_key, lambda: r.wk)
    load("value", lambda: r.w_value, lambda: r.wv)
    load("query", lambda: r.w_query, lambda: r.wq)

    greet = [pair] + [(column + h, (z + i) % 4) for i in range(1, 4) for h in range(2)]
    greet += [red.px, red.py] if reduce else []
    line = lax.broadcasted_iota(jnp.int32, (8, 128), 0)
    wide = [r.boxes[axis, m : m + 1, :] for m in range(2) for axis in range(2)]
    wide = jnp.concatenate(wide * 2, axis=0)
    wide = jnp.where(line == 4, r.lengths[0], jnp.where(line == 5, r.lengths[1], wide))
    r.facts[...] = wide
    barrier = pltpu.get_barrier_semaphore()
    for peer in greet:
        pl.semaphore_signal(barrier, 1, device_id=peer, device_id_type=pl.DeviceIdType.MESH)
    pl.semaphore_wait(barrier, len(greet))

    def spread(kind, src, dst):
        for first in (False, True):
            step = base if first else base + 2
            to = (z + 4 - step) % 4
            rows = pl.ds(pl.multiple_of(64 * step, 64), 64)
            for h in range(2):
                def make(h=h, to=to, rows=rows, step=step):
                    return src(to // 2, pl.ds(64 * h, 64)), dst(step, rows), (column + h, to)

                name = kind + ("a" if first else "b") + str(h)
                if first:
                    pl.when(far)(functools.partial(net.post, name, kind, step, make, "far"))
                else:
                    net.post(name, kind, step, make)

    def here(kind, src, dst):
        make = lambda: (src(micro, other), dst(0, pl.ds(0, 64)), pair)
        net.post(kind + "p", kind, 0, make, "own")

    hidden = lambda m, rows: r.hidden_in.at[m, rows]
    grads = lambda m, rows: r.cotangent.at[m, rows]

    x_to = lambda step, rows: r.x.at[rows]
    m_to = lambda step, rows: r.meta.at[step]
    c_to = lambda step, rows: r.cot.at[rows]
    spread("m", lambda m, rows: r.facts, m_to)
    spread("x", hidden, x_to)

    @pl.when(own)
    def _():
        here("m", lambda m, rows: r.facts, m_to)
        here("x", hidden, x_to)
        make = lambda: (hidden(micro, half), r.x.at[256:320], pair)
        net.post("f0", "f", 0, make, "own")
        load("x", lambda: hidden(micro, half), lambda: r.x.at[0:64])
        load("x2", lambda: hidden(micro, other), lambda: r.x.at[256:320])
        r.meta[0] = r.facts[...]

    for i, (dst, src) in enumerate(((0, 0), (192, 384), (384, 192), (576, 576))):
        load("rel%d" % i, lambda src=src, dst=dst: r.w_rel.at[src : src + 192], lambda src=src, dst=dst: r.wr.at[dst : dst + 192])
    load("out", lambda: r.w_out, lambda: r.wo)
    for j in range(4):
        load("up%d" % j, lambda j=j: r.w_up.at[:, 768 * j : 768 * j + 768], lambda j=j: r.pool.at[0, j // 2, j % 2])
    for j in range(4):
        load("down%d" % j, lambda j=j: r.w_down.at[768 * j : 768 * j + 768], lambda j=j: r.pool.at[1, j // 2, j % 2])
    pl.when(own)(lambda: load("cot", lambda: grads(micro, half), lambda: r.cot.at[0:64]))

    def project(start, stop):
        rows = slice(start, stop)
        for tile in range(3):
            cols = slice(256 * tile, 256 * tile + 256)
            r.k[rows, cols] = nn(r.x[rows, :], r.wk[:, cols]).astype(BF)
            r.v[rows, cols] = nn(r.x[rows, :], r.wv[:, cols]).astype(BF)
            if stop <= 256:
                r.q[rows, cols] = nn(r.x[rows, :], r.wq[:, cols]).astype(BF)

    for j in range(4):
        r.vectors[j : j + 1, :] = r.vector0[768 * j : 768 * j + 768].astype(F32).reshape(1, 768)
        row = getattr(r, "vector%d" % (j + 1))[...]
        r.vectors[4 + j : 5 + j, :] = row.astype(F32).reshape(1, 768)
    x_size = lambda: (hidden(0, pl.ds(0, 64)), r.x.at[0:64], pair)
    m_size = lambda: (r.facts, r.meta.at[0], pair)
    pl.when(far)(lambda: net.came("m", 0, m_size))
    features(0, c, micro, r)
    for slot in (1, 3, 2):
        net.came("m", slot, m_size)
        features(slot, c, micro, r)
    loaded("key")
    loaded("value")
    loaded("query")

    @pl.when(own)
    def _():
        loaded("x")
        loaded("x2")

    @pl.when(far)
    def _():
        net.came("x", 0, x_size)
        net.came("f", 0, x_size)

    project(0, 64)
    project(256, 320)
    for i in range(4):
        loaded("rel%d" % i)
    for slot in (1, 3, 2):
        net.came("x", slot, x_size)
        mine, theirs = slice(64 * slot, 64 * slot + 64), slice(256 + 64 * slot, 320 + 64 * slot)
        make = lambda mine=mine, theirs=theirs: (r.x.at[mine], r.x.at[theirs], pair)
        net.post("f%d" % slot, "f", slot, make)
    spread("c", grads, c_to)
    pl.when(own)(lambda: here("c", grads, c_to))
    project(64, 256)
    for slot in (1, 3, 2):
        net.came("f", slot, x_size)
    project(320, 512)

    place = lax.broadcasted_iota(jnp.int32, (1, 512), 1)
    turn = lax.shift_right_logical(place, 8)
    token = 128 * ((z + (lax.shift_right_logical(place, 6) & 3)) & 3) + (place & 63)
    token = token + 64 * ((c + turn) & 1)
    known = r.meta[1]
    length = jnp.where(micro == 0, known[4:5], known[5:6])
    live = token < jnp.concatenate([length] * 4, axis=1)

    def attend(pair, carry):
        attend_pair(pair, live, r)
        return carry

    lax.fori_loop(0, PAIRS, attend, 0)

    loaded("out")
    for tile in range(3):
        cols = slice(256 * tile, 256 * tile + 256)
        r.res[:, cols] = r.x[0:256, cols].astype(F32) + nn(r.att[...], r.wo[:, cols])

    gain1, bias1, gain2, bias2 = [r.vectors[4 + i : 5 + i, :] for i in range(4)]
    for block in range(4):
        rows = slice(64 * block, 64 * block + 64)
        res = r.res[rows, :]
        center = res - jnp.mean(res, axis=-1, keepdims=True)
        scale = lax.rsqrt(jnp.mean(center * center, axis=-1, keepdims=True) + EPS)
        hat = center * scale
        r.hat[rows, :] = hat
        r.scale[rows, :] = jnp.broadcast_to(scale, (64, 128))
        normed = hat * gain1 + bias1
        r.res[rows, :] = normed
        r.low[rows, :] = normed.astype(BF)

    for j in range(4):
        loaded("up%d" % j)
    for j in range(4):
        loaded("down%d" % j)

    def up_tile(tile):
        j = tile // 3
        return j // 2, j % 2, pl.ds(pl.multiple_of(256 * (tile % 3), 256), 256)

    def up(tile, carry):
        cols = pl.ds(pl.multiple_of(256 * tile, 256), 256)
        y, x, part = up_tile(tile)
        bias = r.vectors[pl.ds(tile // 3, 1), part]
        value = nn(r.low[...], r.pool[0, y, x, :, part]) + bias
        below = 0.5 * (1.0 + lax.erf(value * np.float32(np.sqrt(0.5))))
        dense = jnp.exp(value * value * -0.5) * np.float32(1.0 / np.sqrt(2.0 * np.pi))
        r.act[:, cols] = (value * below).astype(BF)
        slope = below + value * dense
        top = slope.astype(BF)
        r.g[0, y, x, 0:256, part] = top
        r.g[1, y, x, 0:256, part] = (slope - top.astype(F32)).astype(BF)
        return carry

    lax.fori_loop(0, 12, up, 0)
    for tile in range(3):
        cols = slice(256 * tile, 256 * tile + 256)
        r.res[:, cols] = r.res[:, cols] + sum(
            nn(r.act[:, 768 * j : 768 * j + 768], r.pool[1, j // 2, j % 2, :, cols])
            for j in range(4)
        )

    c_size = lambda: (grads(0, pl.ds(0, 64)), r.cot.at[0:64], pair)
    pl.when(own)(lambda: loaded("cot"))
    pl.when(far)(lambda: net.came("c", 0, c_size))
    for slot in (1, 2, 3):
        net.came("c", slot, c_size)
    sums = [jnp.zeros((1, 768), F32) for _ in range(4)]
    for block in range(4):
        rows = slice(64 * block, 64 * block + 64)
        res = r.res[rows, :]
        center = res - jnp.mean(res, axis=-1, keepdims=True)
        scale = lax.rsqrt(jnp.mean(center * center, axis=-1, keepdims=True) + EPS)
        hat = center * scale
        r.out[rows, :] = (hat * gain2 + bias2).astype(BF)
        given = r.cot[rows, :].astype(F32)
        sums[2] = sums[2] + jnp.sum(given * hat, axis=0, keepdims=True)
        sums[3] = sums[3] + jnp.sum(given, axis=0, keepdims=True)
        dres = norm_back(given, hat, scale, gain2)
        r.res[rows, :] = dres
        r.dlow[rows, :] = dres.astype(BF)

    def grad_down(offset, size, share, carry):
        cols = pl.ds(pl.multiple_of(384 * share + offset, 128), size)
        r.g[share % 2, share // 4, share // 2 % 2, 384 + offset : 384 + offset + size, :] = tn(
            r.act[:, cols], r.dlow[...]
        ).astype(BF)
        return carry

    lax.fori_loop(0, 8, functools.partial(grad_down, 0, 128), 0)
    run("C0")
    lax.fori_loop(0, 8, functools.partial(grad_down, 128, 256), 0)
    run("C1")
    stores = {}

    def store(name, src, dst):
        stores[name] = lambda: (src(), dst(), r.store_sem.at[STORES.index(name)])
        pltpu.make_async_copy(*stores[name]()).start()

    def stored(name):
        pltpu.make_async_copy(*stores[name]()).wait()

    def give_back(kind, src, dst):
        for slot in (3, 1, 2, 0):
            rows = slice(64 * slot, 64 * slot + 64)
            to = (source, (z + slot) % 4)
            make = lambda rows=rows, to=to: (src.at[rows], dst.at[micro, half], to)
            role = "all" if slot else "far"
            post = functools.partial(net.post, kind + str(slot), kind, 2 * micro + c, make, role)
            if slot:
                post()
            else:
                pl.when(far)(post)

    def given_back(kind, dst):
        size = lambda: (r.out.at[0:64], dst.at[0, 0:64], pair)
        for m in range(2):
            for h in range(2):
                local = own & (micro == m) & (c == h)
                pl.when(jnp.logical_not(local))(functools.partial(net.came, kind, 2 * m + h, size))

    give_back("o", r.out, r.hidden_out)
    pl.when(own)(lambda: store("hid", lambda: r.out.at[0:64], lambda: r.hidden_out.at[micro, half]))

    def up_back(tile, carry):
        cols = pl.ds(pl.multiple_of(256 * tile, 256), 256)
        y, x, part = up_tile(tile)
        slope = r.g[0, y, x, 0:256, part].astype(F32) + r.g[1, y, x, 0:256, part].astype(F32)
        push = nt(r.dlow[...], r.pool[1, y, x, part, :]) * slope
        low = push.astype(BF)
        r.act[:, cols] = low
        r.sm[0, pl.ds(tile // 3, 1), part] = jnp.sum(low.astype(F32), axis=0, keepdims=True)
        run_at(tile, PLAN["up_back"])
        return carry

    lax.fori_loop(0, 12, up_back, 0)

    def grad_up(tile, carry):
        cols = pl.ds(pl.multiple_of(256 * tile, 256), 256)
        _, _, dest = up_tile(tile)
        put_shares(r.g, pl.multiple_of(96 * (tile // 3), 32), dest, tn(r.low[...], r.act[:, cols]))
        run_at(tile, PLAN["grad_up"])
        return carry

    lax.fori_loop(0, 12, grad_up, 0)
    for tile in range(3):
        cols = slice(256 * tile, 256 * tile + 256)
        r.res[:, cols] = r.res[:, cols] + sum(
            nt(r.act[:, 768 * j : 768 * j + 768], r.pool[0, j // 2, j % 2, cols, :])
            for j in range(4)
        )
    for block in range(4):
        rows = slice(64 * block, 64 * block + 64)
        given, hat = r.res[rows, :], r.hat[rows, :]
        sums[0] = sums[0] + jnp.sum(given * hat, axis=0, keepdims=True)
        sums[1] = sums[1] + jnp.sum(given, axis=0, keepdims=True)
        dres = norm_back(given, hat, r.scale[rows, 0:1], gain1)
        r.res[rows, :] = dres
        r.dlow[rows, :] = dres.astype(BF)
    for row in range(4):
        r.sm[0, 4 + row : 5 + row, :] = sums[row]
    run(*PLAN["norm"])
    for tile in range(3):
        cols = slice(256 * tile, 256 * tile + 256)
        put_shares(r.pool, 0, cols, tn(r.att[...], r.dlow[:, cols]))
    for tile in range(3):
        cols = slice(256 * tile, 256 * tile + 256)
        r.att[:, cols] = nt(r.dlow[...], r.wo[cols, :]).astype(BF)

    def attend_back(pair, carry):
        attend_pair_back(pair, r)
        run_at(pair, PLAN["pairs"])
        return carry

    lax.fori_loop(0, PAIRS, attend_back, 0)
    run("C4")
    for tile in range(3):
        cols = slice(256 * tile, 256 * tile + 256)
        put_shares(r.pool, 192, cols, tn(r.x[0:256, :], r.q[:, cols]))
    run("C5", *PLAN["query"])
    for tile in range(3):
        cols = slice(256 * tile, 256 * tile + 256)
        put_shares(r.pool, 288, cols, tn(r.x[...], r.k[:, cols]))
    run("C6", *PLAN["key"])
    for tile in range(3):
        cols = slice(256 * tile, 256 * tile + 256)
        put_shares(r.pool, 384, cols, tn(r.x[...], r.v[:, cols]))
    run("C7", *PLAN["value"])

    for tile in range(3):
        cols = slice(256 * tile, 256 * tile + 256)
        tail = nt(r.k[...], r.wk[cols, :]) + nt(r.v[...], r.wv[cols, :])
        r.relq[256:512, cols] = tail[256:512].astype(BF)
        r.relq[0:256, cols] = (
            tail[0:256] + r.res[:, cols] + nt(r.q[...], r.wq[cols, :])
        ).astype(BF)
    net.post("dx", "dx", 0, lambda: (r.relq.at[256:512, 0:768], r.dxr, pair))
    run(*PLAN["input"])
    net.came("dx", 0, lambda: (r.relq.at[256:512, 0:768], r.dxr, pair))
    r.din[...] = (r.relq[0:256, 0:768].astype(F32) + r.dxr[...].astype(F32)).astype(BF)
    give_back("d", r.din, r.input_grad)
    pl.when(own)(lambda: store("din", lambda: r.din.at[0:64], lambda: r.input_grad.at[micro, half]))
    run(*PLAN["tail"])
    run(*PLAN["last"])
    if reduce:
        store("small", lambda: r.sm.at[5], lambda: r.small)

        @pl.when(is_end)
        def _():
            for u in range(len(CHUNKS)):
                net.got("z3%d" % u)

        store("share", lambda: r.sums, lambda: r.share)
    else:
        store("small", lambda: r.sm.at[0], lambda: r.small)
        store("share", lambda: r.g, lambda: r.share.at[0])
        last = pltpu.make_async_copy(r.pool, r.share.at[1], r.load_sem.at[0])
        last.start()
        last.wait()
    given_back("o", r.hidden_out)
    given_back("d", r.input_grad)
    stored("small")
    stored("share")

    @pl.when(own)
    def _():
        stored("hid")
        stored("din")
        net.posted("own")

    pl.when(far)(lambda: net.posted("far"))
    net.posted("all")
    net.finish("all")
    pl.when(is_end)(lambda: net.finish("end"))
    pl.when(is_mid)(lambda: net.finish("mid"))


PLAN = {
    "up_back": {4: ("F0",), 9: ("F1",)},
    "grad_up": {5: ("C2",), 11: ("C3",)},
    "norm": ("S0", "F2", "s0"),
    "pairs": {2: ("S1", "F3", "s1"), 3: ("T0",), 5: ("s2",)},
    "query": ("S2", "F4"),
    "key": ("M0", "T1"),
    "value": ("F5",),
    "input": ("s3",),
    "tail": ("M1", "T2", "S3", "N0", "F6", "M2", "N1", "S4", "F7", "s4", "T3", "N2", "S5", "M3"),
    "last": ("T4", "S6", "N3", "M4", "T5", "s5", "S7", "N4", "M5", "T6", "N5", "M6", "T7")
    + ("N6", "M7", "N7"),
}


def scratch(reduce):
    shapes = [
        ("x", (512, 768), BF),
        ("facts", (8, 128), jnp.int32),
        ("meta", (4, 8, 128), jnp.int32),
        ("cot", (256, 768), BF),
        ("vectors", (8, 768), F32),
        ("wq", (768, 768), BF),
        ("wk", (768, 768), BF),
        ("wv", (768, 768), BF),
        ("wo", (768, 768), BF),
        ("wr", (768, 768), BF),
        ("pool", (2, 2, 2, 768, 768), BF),
        ("g", (2, 2, 2, 768, 768), BF),
        ("sine", (256, 384), F32),
        ("cosine", (256, 384), F32),
        ("feat", (512, 896), BF),
        ("q", (256, 768), BF),
        ("k", (512, 768), BF),
        ("v", (512, 768), BF),
        ("att", (256, 768), BF),
        ("relq", (512, 896), BF),
        ("score", (512, 512), F32),
        ("dlog", (512, 512), BF),
        ("probs", (PAIRS, 512, 512), BF),
        ("res", (256, 768), F32),
        ("hat", (256, 768), F32),
        ("scale", (256, 128), F32),
        ("low", (256, 768), BF),
        ("act", (256, 3072), BF),
        ("dlow", (256, 768), BF),
        ("out", (256, 768), BF),
        ("dxr", (256, 768), BF),
        ("din", (256, 768), BF),
        ("sm", (6, 8, 768), F32),
    ]
    if reduce:
        shapes += [("r1_%d" % u, (2, 2, c[2], 768), BF) for u, c in enumerate(CHUNKS)]
        shapes += [
            ("ra", (2, 624, 768), BF),
            ("rb", (2, 624, 768), BF),
            ("ra2", (624, 768), BF),
            ("rb2", (624, 768), BF),
            ("zr", (1248, 768), BF),
            ("za", (1248, 768), BF),
            ("sums", (1248, 768), BF),
            ("smr", (5, 8, 768), F32),
        ]
    return shapes


def layer(lengths, hidden_in, boxes, cotangent, vectors, weights, reduce):
    hi, lo = trig_tables(QUARTER)
    any_space = pl.BlockSpec(memory_space=pl.ANY)
    vmem = pl.BlockSpec(memory_space=pltpu.VMEM)
    ins = (
        ("lengths", lengths.reshape(-1), pl.BlockSpec(memory_space=pltpu.SMEM)),
        ("hidden_in", hidden_in, any_space),
        ("cotangent", cotangent, any_space),
        ("boxes", boxes, vmem),
        ("hi", jnp.asarray(hi), vmem),
        ("lo", jnp.asarray(lo), vmem),
    )
    ins += tuple(("vector%d" % i, v, vmem) for i, v in enumerate(vectors))
    ins += tuple((name, w, any_space) for name, w in weights)
    outs = (
        ("hidden_out", (2, 128, 768), BF),
        ("input_grad", (2, 128, 768), BF),
        ("share", (1248, 768) if reduce else (2, 2, 2, 2, 768, 768), BF),
        ("small", (8, 768), F32),
    )
    shapes = scratch(reduce)
    sems = ("send_sem", "recv_sem", "post_sem", "load_sem", "store_sem")
    names = tuple(i[0] for i in ins) + tuple(o[0] for o in outs)
    names += tuple(s[0] for s in shapes) + sems
    dma = pltpu.SemaphoreType.DMA
    return pl.pallas_call(
        functools.partial(layer_kernel, names, reduce),
        out_shape=[jax.ShapeDtypeStruct(o[1], o[2]) for o in outs],
        in_specs=[i[2] for i in ins],
        out_specs=[any_space] * len(outs),
        scratch_shapes=[pltpu.VMEM(s[1], s[2]) for s in shapes]
        + [dma((len(i),)) for i in (SENDS, SENDS, POSTS, LOADS, STORES)],
        compiler_params=pltpu.CompilerParams(
            vmem_limit_bytes=VMEM_LIMIT, collective_id=0, has_side_effects=True
        ),
        name="layer",
    )(*[i[1] for i in ins])


def finish_kernel(share, small, hid, din, hidden, dinput, dq, dk, dv, dout, drel, dup, *rest):
    dbup, ddown, vectors = rest[0], rest[1], rest[2:]
    hidden[...] = hid[...]
    dinput[...] = din[...]
    for j in range(4):
        dup[:, 768 * j : 768 * j + 768] = share[96 * j : 96 * j + 96, :].astype(F32)
    ddown[...] = share[384:768, :].astype(F32)
    for i, ref in enumerate((dout, drel, dq, dk, dv)):
        ref[...] = share[768 + 96 * i : 864 + 96 * i, :].astype(F32)
    dp = lax.axis_index("dp")
    row = small[pl.ds(dp // 2, 1), :]
    dbup[...] = jnp.where(dp % 2 == 0, row[:, 0:384], row[:, 384:768]).reshape(384)
    turned = pltpu.roll(small[...], lax.rem(768 - 96 * dp, 768), 1)
    for i, ref in enumerate(vectors):
        ref[...] = turned[4 + i : 5 + i, 0:96].reshape(96)


def finish(share, small, hidden, dinput):
    shapes = [(96, 768)] * 5 + [(96, 3072), (384,), (384, 768)] + [(96,)] * 4
    low = jax.ShapeDtypeStruct(hidden.shape, BF)
    return pl.pallas_call(
        finish_kernel,
        out_shape=[low, low] + [jax.ShapeDtypeStruct(s, F32) for s in shapes],
        name="finish",
    )(share, small, hidden, dinput)


def finish_any(g, small):
    order = g.transpose(0, 2, 3, 1, 4, 5).reshape(2, 8, 768, 768)

    def weight(which, base):
        return order[which, :, base : base + 96].reshape(768, 768)

    up = jnp.concatenate([weight(0, 96 * j) for j in range(4)], axis=1)
    down = order[0, :, 384:768].reshape(3072, 768)
    full = [weight(1, base) for base in (192, 288, 384, 0, 96)] + [up, down]
    grads = [
        lax.psum(lax.psum_scatter(w, "dp", scatter_dimension=0, tiled=True), "seq").astype(F32)
        for w in full
    ]
    small = lax.psum(small, ("dp", "seq"))
    dp, count = lax.axis_index("dp"), lax.axis_size("dp")

    def own_part(vector):
        size = vector.shape[0] // count
        return lax.dynamic_slice_in_dim(vector, dp * size, size)

    parts = [own_part(small[4 + i]) for i in range(4)]
    return grads[:6] + [own_part(small[0:4].reshape(-1)), grads[6]] + parts


def shards(
    hidden_in,
    boxes,
    lengths,
    w_query,
    w_key,
    w_value,
    w_out,
    w_rel,
    w_up,
    b_up,
    w_down,
    gain_attn,
    bias_attn,
    gain_ffn,
    bias_ffn,
    cotangent,
):
    vectors = (b_up, gain_attn, bias_attn, gain_ffn, bias_ffn)
    weights = (
        ("w_query", w_query),
        ("w_key", w_key),
        ("w_value", w_value),
        ("w_out", w_out),
        ("w_rel", w_rel),
        ("w_up", w_up),
        ("w_down", w_down),
    )
    reduce = lax.axis_size("dp") == 8
    hidden, dinput, share, small = layer(
        lengths,
        hidden_in[:, 0],
        boxes[:, :, 0],
        cotangent[:, 0],
        vectors,
        weights,
        reduce,
    )
    if reduce:
        hidden, dinput, *rest = finish(share, small, hidden, dinput)
    else:
        rest = finish_any(share, small)
    return (hidden[:, None], dinput[:, None], *rest)


def solution(mesh):
    rows = P(None, "dp", "seq", None)
    placed = (rows, P(None, None, "dp", "seq"), P(None, "dp")) + (P(),) * 12 + (rows,)
    matrix, vector = P("dp", None), P("dp")
    return jax.shard_map(
        shards,
        mesh=mesh,
        in_specs=placed,
        out_specs=(rows, rows) + (matrix,) * 6 + (vector, matrix) + (vector,) * 4,
        check_vma=False,
    )
```

```python
import functools

import jax
import jax.numpy as jnp
import numpy as np
from jax import lax
from jax.experimental import pallas as pl
from jax.experimental.pallas import tpu as pltpu
from jax.sharding import PartitionSpec as P

HEADS = 12
EPS = 1e-05
BF = jnp.bfloat16
F32 = jnp.float32
PAIRS = HEADS // 2
VMEM_LIMIT = 67043328
QUARTER = 192


def nn(a, b):
    return lax.dot_general(a, b, (((1,), (0,)), ((), ())), preferred_element_type=F32)


def nt(a, b):
    return lax.dot_general(a, b, (((1,), (1,)), ((), ())), preferred_element_type=F32)


def tn(a, b):
    return lax.dot_general(a, b, (((0,), (0,)), ((), ())), preferred_element_type=F32)


def trig_tables(quarter):
    freq = 10000.0 ** (-np.arange(quarter) / quarter)
    tables = []
    for step in (32.0, 1.0):
        angle = step * np.arange(32)[:, None] * freq[None, :]
        rest = np.concatenate([np.sin(angle), np.cos(angle)], axis=1).astype(np.float32)
        parts = []
        for _ in range(3):
            part = rest.astype(BF)
            parts.append(part)
            rest = rest - part.astype(np.float32)
        tables.append(np.concatenate(parts, axis=0))
    return tables


def features(slot, c, micro, r):
    half = 2 * QUARTER
    iota = lax.broadcasted_iota(jnp.int32, (32, 128), 0)
    hi_tab, lo_tab = r.hi[...], r.lo[...]
    block = pltpu.roll(r.meta[slot], 64 * c, 1)
    sines, cosines = [], []
    for axis in range(2):
        where = jnp.where(micro == 0, block[axis : axis + 1], block[2 + axis : 3 + axis])
        pick_hi = (iota == lax.shift_right_logical(where, 5)).astype(F32).astype(BF)
        pick_lo = (iota == (where & 31)).astype(F32).astype(BF)
        hi = tn(jnp.concatenate([pick_hi] * 3, axis=0), hi_tab)
        lo = tn(jnp.concatenate([pick_lo] * 3, axis=0), lo_tab)
        sin_hi, cos_hi = hi[:, :QUARTER], hi[:, QUARTER:]
        sin_lo, cos_lo = lo[:, :QUARTER], lo[:, QUARTER:]
        sines.append(sin_hi * cos_lo + cos_hi * sin_lo)
        cosines.append(cos_hi * cos_lo - sin_hi * sin_lo)
    sine = jnp.concatenate(sines, axis=1)
    cosine = jnp.concatenate(cosines, axis=1)
    for part in range(2):
        mine = slice(64 * part, 64 * part + 64)
        rows = pl.ds(256 * part + 64 * slot, 64)
        r.feat[rows, 0:half] = cosine[mine].astype(BF)
        r.feat[rows, half : 2 * half] = sine[mine].astype(BF)
    rows = pl.ds(64 * slot, 64)
    r.sine[rows, :] = sine[0:64]
    r.cosine[rows, :] = cosine[0:64]


def head_stack(pair):
    first = lax.broadcasted_iota(jnp.int32, pair.shape, 1) < 64
    zero = jnp.zeros_like(pair)
    return jnp.concatenate([jnp.where(first, pair, zero), jnp.where(first, zero, pair)], axis=0)


def head_join(stack):
    half = stack.shape[0] // 2
    first = lax.broadcasted_iota(jnp.int32, (half, 128), 1) < 64
    return jnp.where(first, stack[:half], stack[half:])


def attend_pair(pair, live, r):
    cols = pl.ds(pl.multiple_of(128 * pair, 128), 128)
    stack = head_stack(r.q[:, cols].astype(F32) * 0.125).astype(BF)
    for head in range(2):
        rows = slice(256 * head, 256 * head + 256)
        left = nt(stack[rows], r.wr[0:384, cols])
        right = nt(stack[rows], r.wr[384:768, cols])
        sin, cos = r.sine[...], r.cosine[...]
        r.relq[rows, 0:384] = (left * sin + right * cos).astype(BF)
        r.relq[rows, 384:768] = (right * sin - left * cos).astype(BF)
    r.relq[:, 768:896] = stack
    r.feat[:, 768:896] = r.k[:, cols]
    r.score[...] = nt(r.relq[...], r.feat[...])
    for block in range(8):
        rows = pl.ds(64 * block, 64)
        score = jnp.where(live, r.score[rows, :], -1e30)
        top = jnp.max(score, axis=-1, keepdims=True)
        weight = jnp.exp(score - top)
        total = jnp.sum(weight, axis=-1, keepdims=True)
        r.probs[pair, rows, :] = (weight * (1.0 / total)).astype(BF)
    r.att[:, cols] = head_join(nn(r.probs[pair], r.v[:, cols])).astype(BF)


def attend_pair_back(pair, r):
    cols = pl.ds(pl.multiple_of(128 * pair, 128), 128)
    given = head_stack(r.att[:, cols].astype(F32)).astype(BF)
    stack = head_stack(r.q[:, cols].astype(F32)).astype(BF)
    r.score[...] = nt(given, r.v[:, cols])
    for block in range(8):
        rows = pl.ds(64 * block, 64)
        prob = r.probs[pair, rows, :].astype(F32)
        push = prob * r.score[rows, :]
        mean = jnp.sum(push, axis=-1, keepdims=True)
        r.dlog[rows, :] = ((push - prob * mean) * 0.125).astype(BF)
    r.feat[:, 768:896] = r.k[:, cols]
    r.v[:, cols] = tn(r.probs[pair], given).astype(BF)
    r.k[:, cols] = tn(r.dlog[...], stack).astype(BF)
    for head in range(2):
        rows = slice(256 * head, 256 * head + 256)
        first = nn(r.dlog[rows, :], r.feat[:, 0:384])
        second = nn(r.dlog[rows, :], r.feat[:, 384:768])
        sin, cos = r.sine[...], r.cosine[...]
        r.relq[rows, 0:384] = (first * sin - second * cos).astype(BF)
        r.relq[rows, 384:768] = (first * cos + second * sin).astype(BF)
    dq = nn(r.dlog[...], r.feat[:, 768:896]) + nn(r.relq[:, 0:768], r.wr[:, cols])
    r.q[:, cols] = head_join(dq).astype(BF)
    part = tn(r.relq[:, 0:768], stack).astype(BF)
    for piece, share in enumerate((0, 1, 4, 5, 2, 3, 6, 7)):
        c, y, x = share % 2, share // 4, share // 2 % 2
        r.pool[c, y, x, 96:192, cols] = part[96 * piece : 96 * piece + 96]


def norm_back(given, hat, scale, gain):
    push = given * gain
    mean = jnp.mean(push, axis=-1, keepdims=True)
    lean = jnp.mean(push * hat, axis=-1, keepdims=True)
    return scale * (push - mean - hat * lean)


def put_shares(ref, base, cols, part):
    for share in range(8):
        c, y, x = share % 2, share // 4, share // 2 % 2
        ref[c, y, x, pl.ds(base, 96), cols] = part[96 * share : 96 * share + 96].astype(BF)


class Refs:
    pass


CHUNKS = (
    ("g", 384, 128, 384),
    ("g", 512, 128, 512),
    ("g", 640, 128, 640),
    ("g", 0, 96, 0),
    ("g", 96, 96, 96),
    ("g", 192, 96, 192),
    ("g", 288, 96, 288),
    ("pool", 0, 96, 768),
    ("pool", 96, 96, 864),
    ("pool", 192, 96, 960),
    ("pool", 288, 96, 1056),
    ("pool", 384, 64, 1152),
    ("pool", 448, 32, 1216),
)
C, F, S, T, M, N, V = range(7)
STAGES = ("core", "xa", "xb", "ya", "yb", "z1", "z2", "z3")
BLOCKS = ("x", "m", "c", "f", "o", "d")
SENDS = tuple(k + str(i) for k in BLOCKS for i in range(4)) + ("dx0",)
SENDS += tuple("s%d" % i for i in range(5))
SENDS += tuple("%s%d" % (s, u) for u in range(len(CHUNKS)) for s in STAGES)
LOADS = ("x", "x2", "cot", "key", "value", "query", "out")
LOADS += tuple("rel%d" % i for i in range(4)) + tuple("up%d" % i for i in range(4))
LOADS += tuple("down%d" % i for i in range(4))
STORES = ("hid", "din", "share", "small")
POSTS = tuple(k + i for k in "xmc" for i in ("a0", "a1", "b0", "b1", "p"))
POSTS += tuple(k + str(i) for k in "fod" for i in range(4)) + ("dx",)


class Net:
    def __init__(self, r):
        self.r = r
        self.made = {}
        self.order = {"all": [], "end": [], "mid": []}
        self.posts = {"all": [], "own": [], "far": []}

    def _of(self, name):
        i = SENDS.index(name)
        src, dst, peer = self.made[name]()
        return pltpu.make_async_remote_copy(
            src_ref=src,
            dst_ref=dst,
            send_sem=self.r.send_sem.at[i],
            recv_sem=self.r.recv_sem.at[i],
            device_id=peer,
            device_id_type=pl.DeviceIdType.MESH,
        )

    def start(self, name, make, role="all"):
        self.made[name] = make
        self._of(name).start()
        self.order[role].append(name)

    def got(self, name):
        self._of(name).wait_recv()

    def _post(self, name, src, dst, at, peer):
        return pltpu.make_async_remote_copy(
            src_ref=src,
            dst_ref=dst,
            send_sem=self.r.post_sem.at[POSTS.index(name)],
            recv_sem=self.r.recv_sem.at[at],
            device_id=peer,
            device_id_type=pl.DeviceIdType.MESH,
        )

    def post(self, name, kind, index, make, role="all"):
        src, dst, peer = make()
        self._post(name, src, dst, SENDS.index(kind + "0") + index, peer).start()
        self.posts[role].append((name, kind, index, make))

    def came(self, kind, index, make):
        src, dst, peer = make()
        self._post(POSTS[0], src, dst, SENDS.index(kind + "0") + index, peer).wait_recv()

    def finish(self, role):
        for name in self.order[role]:
            self._of(name).wait_send()

    def posted(self, role):
        for name, kind, index, make in self.posts[role]:
            src, dst, peer = make()
            self._post(name, src, dst, SENDS.index(kind + "0") + index, peer).wait_send()


def add_rows(count, body):
    size = 48 if count % 48 == 0 else 32 if count % 32 == 0 else 16

    def step(i, carry):
        body(pl.multiple_of(size * i, 16), size)
        return carry

    lax.fori_loop(0, count // size, step, 0)


def total(*terms):
    out = terms[0].astype(F32)
    for term in terms[1:]:
        out = out + term.astype(F32)
    return out.astype(BF)


class Reduction:
    def __init__(self, r, net, dp, z):
        self.r, self.net = r, net
        self.c, self.x, self.y = dp % 2, dp // 2 % 2, dp // 4
        self.pc = (dp + 1 - 2 * self.c, z)
        self.px = (dp + 2 - 4 * self.x, z)
        self.py = (dp + 4 - 8 * self.y, z)
        self.pz1 = (dp, z + 1 - 2 * (z % 2))
        self.pz2 = (dp, (z + 2) % 4)
        self.across = (dp, 3 - z)

    def parts(self, u):
        name, base, rows, out = CHUNKS[u]
        return getattr(self.r, name), base, rows // 2, out, self.r.r1[u], out // 2

    def core(self, u):
        g, base, half, _, r1, _ = self.parts(u)
        self.net.start(
            "core%d" % u, lambda: (g.at[1 - self.c, :, :, pl.ds(base, 2 * half)], r1, self.pc)
        )

    def first(self, u):
        g, base, half, _, r1, at = self.parts(u)
        c, x, y = self.c, self.x, self.y
        self.net.got("core%d" % u)

        def add(i, size):
            for k in range(2):
                rows, own = pl.ds(base + i, size), pl.ds(i, size)
                g[c, k, 1 - x, rows] = total(g[c, k, 1 - x, rows], r1[k, 1 - x, own])
                rows, own = pl.ds(base + half + i, size), pl.ds(half + i, size)
                g[c, 1 - y, k, rows] = total(g[c, 1 - y, k, rows], r1[1 - y, k, own])

        add_rows(half, add)
        a, b, to = pl.ds(base, half), pl.ds(base + half, half), pl.ds(at, half)
        self.net.start("xa%d" % u, lambda: (g.at[c, :, 1 - x, a], self.r.ra.at[:, to], self.px))
        self.net.start("yb%d" % u, lambda: (g.at[c, 1 - y, :, b], self.r.rb.at[:, to], self.py))

    def second(self, u):
        g, base, half, _, r1, at = self.parts(u)
        c, x, y = self.c, self.x, self.y
        ra, rb = self.r.ra, self.r.rb
        self.net.got("xa%d" % u)
        self.net.got("yb%d" % u)

        def add(i, size):
            came = pl.ds(at + i, size)
            rows, own = pl.ds(base + i, size), pl.ds(i, size)
            g[c, 1 - y, x, rows] = total(g[c, 1 - y, x, rows], r1[1 - y, x, own], ra[1 - y, came])
            rows, own = pl.ds(base + half + i, size), pl.ds(half + i, size)
            g[c, y, 1 - x, rows] = total(g[c, y, 1 - x, rows], r1[y, 1 - x, own], rb[1 - x, came])

        add_rows(half, add)
        a, b, to = pl.ds(base, half), pl.ds(base + half, half), pl.ds(at, half)
        self.net.start("ya%d" % u, lambda: (g.at[c, 1 - y, x, a], self.r.ra2.at[to], self.py))
        self.net.start("xb%d" % u, lambda: (g.at[c, y, 1 - x, b], self.r.rb2.at[to], self.px))

    def third(self, u, mid):
        g, base, half, out, r1, at = self.parts(u)
        c, x, y = self.c, self.x, self.y
        ra, rb, ra2, rb2, zr = self.r.ra, self.r.rb, self.r.ra2, self.r.rb2, self.r.zr
        self.net.got("ya%d" % u)
        self.net.got("xb%d" % u)
        if mid:
            self.net.got("z1%d" % u)

        def add(i, size):
            came = pl.ds(at + i, size)
            rows, own = pl.ds(base + i, size), pl.ds(i, size)
            more = (zr[pl.ds(out + i, size)],) if mid else ()
            g[c, y, x, rows] = total(
                g[c, y, x, rows], r1[y, x, own], ra[y, came], ra2[came], *more
            )
            rows, own = pl.ds(base + half + i, size), pl.ds(half + i, size)
            more = (zr[pl.ds(out + half + i, size)],) if mid else ()
            g[c, y, x, rows] = total(
                g[c, y, x, rows], r1[y, x, own], rb[x, came], rb2[came], *more
            )

        add_rows(half, add)
        rows, to = pl.ds(base, 2 * half), pl.ds(out, 2 * half)
        if mid:
            make = lambda: (g.at[c, y, x, rows], self.r.za.at[to], self.across)
            self.net.start("z2%d" % u, make, "mid")
        else:
            make = lambda: (g.at[c, y, x, rows], self.r.zr.at[to], self.pz1)
            self.net.start("z1%d" % u, make, "end")

    def fourth(self, u):
        g, base, half, out, _, _ = self.parts(u)
        c, x, y = self.c, self.x, self.y
        self.net.got("z2%d" % u)

        def add(i, size):
            rows, to = pl.ds(base + i, size), pl.ds(out + i, size)
            self.r.sums[to] = total(g[c, y, x, rows], self.r.za[to])

        add_rows(2 * half, add)
        to = pl.ds(out, 2 * half)
        self.net.start("z3%d" % u, lambda: (self.r.sums.at[to], self.r.sums.at[to], self.pz1), "mid")

    def small(self, i):
        if i:
            self.net.got("s%d" % (i - 1))
            self.r.sm[i] = self.r.sm[i - 1] + self.r.smr[i - 1]
        if i < 5:
            peer = (self.pc, self.px, self.py, self.pz1, self.pz2)[i]
            self.net.start("s%d" % i, lambda: (self.r.sm.at[i], self.r.smr.at[i], peer))


def layer_kernel(names, reduce, *refs):
    r = Refs()
    for name, ref in zip(names, refs):
        setattr(r, name, ref)
    dp, z = lax.axis_index("dp"), lax.axis_index("seq")
    micro, c = z // 2, dp % 2
    is_mid = lax.rem(z, 3) > 0
    is_end = lax.rem(z, 3) == 0
    own = c == z % 2
    far = c != z % 2
    base = jnp.where(own, 0, 1)
    column = dp - c
    source = column + z % 2
    pair = (dp + 1 - 2 * c, z)
    half = pl.ds(pl.multiple_of(64 * c, 64), 64)
    other = pl.ds(pl.multiple_of(64 - 64 * c, 64), 64)
    net = Net(r)
    red = None
    if reduce:
        r.r1 = tuple(getattr(r, "r1_%d" % u) for u in range(len(CHUNKS)))
        red = Reduction(r, net, dp, z)

    def run(*steps):
        if not reduce:
            return
        for kind, u in steps:
            if kind == C:
                red.core(u)
            elif kind == F:
                red.first(u)
            elif kind == S:
                red.second(u)
            elif kind == T:
                pl.when(is_end)(functools.partial(red.third, u, False))
            elif kind == M:
                pl.when(is_mid)(functools.partial(red.third, u, True))
            elif kind == N:
                pl.when(is_mid)(functools.partial(red.fourth, u))
            else:
                red.small(u)

    def run_plan(place):
        run(*PLAN.get(place, ()))

    def run_at(index, place):
        for at, steps in PLAN[place].items():
            pl.when(index == at)(functools.partial(run, *steps))

    loads = {}

    def load(name, src, dst):
        loads[name] = lambda: (src(), dst(), r.load_sem.at[LOADS.index(name)])
        pltpu.make_async_copy(*loads[name]()).start()

    def loaded(name):
        pltpu.make_async_copy(*loads[name]()).wait()

    load("key", lambda: r.w_key, lambda: r.wk)
    load("value", lambda: r.w_value, lambda: r.wv)
    load("query", lambda: r.w_query, lambda: r.wq)

    greet = [pair] + [(column + h, (z + i) % 4) for i in range(1, 4) for h in range(2)]
    greet += [red.px, red.py] if reduce else []
    line = lax.broadcasted_iota(jnp.int32, (8, 128), 0)
    wide = [r.boxes[axis, m : m + 1, :] for m in range(2) for axis in range(2)]
    wide = jnp.concatenate(wide * 2, axis=0)
    wide = jnp.where(line == 4, r.lengths[0], jnp.where(line == 5, r.lengths[1], wide))
    r.facts[...] = wide
    barrier = pltpu.get_barrier_semaphore()
    for peer in greet:
        pl.semaphore_signal(barrier, 1, device_id=peer, device_id_type=pl.DeviceIdType.MESH)
    pl.semaphore_wait(barrier, len(greet))

    def spread(kind, src, dst):
        for first in (False, True):
            step = base if first else base + 2
            to = (z + 4 - step) % 4
            rows = pl.ds(pl.multiple_of(64 * step, 64), 64)
            for h in range(2):
                def make(h=h, to=to, rows=rows, step=step):
                    return src(to // 2, pl.ds(64 * h, 64)), dst(step, rows), (column + h, to)

                name = kind + ("a" if first else "b") + str(h)
                if first:
                    pl.when(far)(functools.partial(net.post, name, kind, step, make, "far"))
                else:
                    net.post(name, kind, step, make)

    def here(kind, src, dst):
        make = lambda: (src(micro, other), dst(0, pl.ds(0, 64)), pair)
        net.post(kind + "p", kind, 0, make, "own")

    hidden = lambda m, rows: r.hidden_in.at[m, rows]
    grads = lambda m, rows: r.cotangent.at[m, rows]

    x_to = lambda step, rows: r.x.at[rows]
    m_to = lambda step, rows: r.meta.at[step]
    c_to = lambda step, rows: r.cot.at[rows]
    spread("m", lambda m, rows: r.facts, m_to)
    spread("x", hidden, x_to)

    @pl.when(own)
    def _():
        here("m", lambda m, rows: r.facts, m_to)
        here("x", hidden, x_to)
        make = lambda: (hidden(micro, half), r.x.at[256:320], pair)
        net.post("f0", "f", 0, make, "own")
        load("x", lambda: hidden(micro, half), lambda: r.x.at[0:64])
        load("x2", lambda: hidden(micro, other), lambda: r.x.at[256:320])
        r.meta[0] = r.facts[...]

    for i, (dst, src) in enumerate(((0, 0), (192, 384), (384, 192), (576, 576))):
        load("rel%d" % i, lambda src=src, dst=dst: r.w_rel.at[src : src + 192], lambda src=src, dst=dst: r.wr.at[dst : dst + 192])
    load("out", lambda: r.w_out, lambda: r.wo)
    for j in range(4):
        load("up%d" % j, lambda j=j: r.w_up.at[:, 768 * j : 768 * j + 768], lambda j=j: r.pool.at[0, j // 2, j % 2])
    for j in range(4):
        load("down%d" % j, lambda j=j: r.w_down.at[768 * j : 768 * j + 768], lambda j=j: r.pool.at[1, j // 2, j % 2])
    pl.when(own)(lambda: load("cot", lambda: grads(micro, half), lambda: r.cot.at[0:64]))

    def project(start, stop):
        rows = slice(start, stop)
        for tile in range(3):
            cols = slice(256 * tile, 256 * tile + 256)
            r.k[rows, cols] = nn(r.x[rows, :], r.wk[:, cols]).astype(BF)
            r.v[rows, cols] = nn(r.x[rows, :], r.wv[:, cols]).astype(BF)
            if stop <= 256:
                r.q[rows, cols] = nn(r.x[rows, :], r.wq[:, cols]).astype(BF)

    for j in range(4):
        r.vectors[j : j + 1, :] = r.vector0[768 * j : 768 * j + 768].astype(F32).reshape(1, 768)
        row = getattr(r, "vector%d" % (j + 1))[...]
        r.vectors[4 + j : 5 + j, :] = row.astype(F32).reshape(1, 768)
    x_size = lambda: (hidden(0, pl.ds(0, 64)), r.x.at[0:64], pair)
    m_size = lambda: (r.facts, r.meta.at[0], pair)
    pl.when(far)(lambda: net.came("m", 0, m_size))
    features(0, c, micro, r)
    for slot in (1, 3, 2):
        net.came("m", slot, m_size)
        features(slot, c, micro, r)
    loaded("key")
    loaded("value")
    loaded("query")

    @pl.when(own)
    def _():
        loaded("x")
        loaded("x2")

    @pl.when(far)
    def _():
        net.came("x", 0, x_size)
        net.came("f", 0, x_size)

    project(0, 64)
    project(256, 320)
    for i in range(4):
        loaded("rel%d" % i)
    for slot in (1, 3, 2):
        net.came("x", slot, x_size)
        mine, theirs = slice(64 * slot, 64 * slot + 64), slice(256 + 64 * slot, 320 + 64 * slot)
        make = lambda mine=mine, theirs=theirs: (r.x.at[mine], r.x.at[theirs], pair)
        net.post("f%d" % slot, "f", slot, make)
    spread("c", grads, c_to)
    pl.when(own)(lambda: here("c", grads, c_to))
    project(64, 256)
    for slot in (1, 3, 2):
        net.came("f", slot, x_size)
    project(320, 512)

    place = lax.broadcasted_iota(jnp.int32, (1, 512), 1)
    turn = lax.shift_right_logical(place, 8)
    token = 128 * ((z + (lax.shift_right_logical(place, 6) & 3)) & 3) + (place & 63)
    token = token + 64 * ((c + turn) & 1)
    known = r.meta[1]
    length = jnp.where(micro == 0, known[4:5], known[5:6])
    live = token < jnp.concatenate([length] * 4, axis=1)

    def attend(pair, carry):
        attend_pair(pair, live, r)
        return carry

    lax.fori_loop(0, PAIRS, attend, 0)

    loaded("out")
    for tile in range(3):
        cols = slice(256 * tile, 256 * tile + 256)
        r.res[:, cols] = r.x[0:256, cols].astype(F32) + nn(r.att[...], r.wo[:, cols])

    gain1, bias1, gain2, bias2 = [r.vectors[4 + i : 5 + i, :] for i in range(4)]
    for block in range(4):
        rows = slice(64 * block, 64 * block + 64)
        res = r.res[rows, :]
        center = res - jnp.mean(res, axis=-1, keepdims=True)
        scale = lax.rsqrt(jnp.mean(center * center, axis=-1, keepdims=True) + EPS)
        hat = center * scale
        r.hat[rows, :] = hat
        r.scale[rows, :] = jnp.broadcast_to(scale, (64, 128))
        normed = hat * gain1 + bias1
        r.res[rows, :] = normed
        r.low[rows, :] = normed.astype(BF)

    for j in range(4):
        loaded("up%d" % j)
    for j in range(4):
        loaded("down%d" % j)

    def up_tile(tile):
        j = tile // 3
        return j // 2, j % 2, pl.ds(pl.multiple_of(256 * (tile % 3), 256), 256)

    def up(tile, carry):
        cols = pl.ds(pl.multiple_of(256 * tile, 256), 256)
        y, x, part = up_tile(tile)
        bias = r.vectors[pl.ds(tile // 3, 1), part]
        value = nn(r.low[...], r.pool[0, y, x, :, part]) + bias
        below = 0.5 * (1.0 + lax.erf(value * np.float32(np.sqrt(0.5))))
        dense = jnp.exp(value * value * -0.5) * np.float32(1.0 / np.sqrt(2.0 * np.pi))
        r.act[:, cols] = (value * below).astype(BF)
        slope = below + value * dense
        top = slope.astype(BF)
        r.g[0, y, x, 0:256, part] = top
        r.g[1, y, x, 0:256, part] = (slope - top.astype(F32)).astype(BF)
        return carry

    lax.fori_loop(0, 12, up, 0)
    for tile in range(3):
        cols = slice(256 * tile, 256 * tile + 256)
        r.res[:, cols] = r.res[:, cols] + sum(
            nn(r.act[:, 768 * j : 768 * j + 768], r.pool[1, j // 2, j % 2, :, cols])
            for j in range(4)
        )

    c_size = lambda: (grads(0, pl.ds(0, 64)), r.cot.at[0:64], pair)
    pl.when(own)(lambda: loaded("cot"))
    pl.when(far)(lambda: net.came("c", 0, c_size))
    for slot in (1, 2, 3):
        net.came("c", slot, c_size)
    sums = [jnp.zeros((1, 768), F32) for _ in range(4)]
    for block in range(4):
        rows = slice(64 * block, 64 * block + 64)
        res = r.res[rows, :]
        center = res - jnp.mean(res, axis=-1, keepdims=True)
        scale = lax.rsqrt(jnp.mean(center * center, axis=-1, keepdims=True) + EPS)
        hat = center * scale
        r.out[rows, :] = (hat * gain2 + bias2).astype(BF)
        given = r.cot[rows, :].astype(F32)
        sums[2] = sums[2] + jnp.sum(given * hat, axis=0, keepdims=True)
        sums[3] = sums[3] + jnp.sum(given, axis=0, keepdims=True)
        dres = norm_back(given, hat, scale, gain2)
        r.res[rows, :] = dres
        r.dlow[rows, :] = dres.astype(BF)

    def grad_down(offset, size, share, carry):
        cols = pl.ds(pl.multiple_of(384 * share + offset, 128), size)
        r.g[share % 2, share // 4, share // 2 % 2, 384 + offset : 384 + offset + size, :] = tn(
            r.act[:, cols], r.dlow[...]
        ).astype(BF)
        return carry

    for third in range(3):
        lax.fori_loop(0, 8, functools.partial(grad_down, 128 * third, 128), 0)
        run_plan("down%d" % third)
    stores = {}

    def store(name, src, dst):
        stores[name] = lambda: (src(), dst(), r.store_sem.at[STORES.index(name)])
        pltpu.make_async_copy(*stores[name]()).start()

    def stored(name):
        pltpu.make_async_copy(*stores[name]()).wait()

    def give_back(kind, src, dst):
        for slot in (3, 1, 2, 0):
            rows = slice(64 * slot, 64 * slot + 64)
            to = (source, (z + slot) % 4)
            make = lambda rows=rows, to=to: (src.at[rows], dst.at[micro, half], to)
            role = "all" if slot else "far"
            post = functools.partial(net.post, kind + str(slot), kind, 2 * micro + c, make, role)
            if slot:
                post()
            else:
                pl.when(far)(post)

    def given_back(kind, dst):
        size = lambda: (r.out.at[0:64], dst.at[0, 0:64], pair)
        for m in range(2):
            for h in range(2):
                local = own & (micro == m) & (c == h)
                pl.when(jnp.logical_not(local))(functools.partial(net.came, kind, 2 * m + h, size))

    give_back("o", r.out, r.hidden_out)
    pl.when(own)(lambda: store("hid", lambda: r.out.at[0:64], lambda: r.hidden_out.at[micro, half]))

    def up_back(tile, carry):
        cols = pl.ds(pl.multiple_of(256 * tile, 256), 256)
        y, x, part = up_tile(tile)
        slope = r.g[0, y, x, 0:256, part].astype(F32) + r.g[1, y, x, 0:256, part].astype(F32)
        push = nt(r.dlow[...], r.pool[1, y, x, part, :]) * slope
        low = push.astype(BF)
        r.act[:, cols] = low
        r.sm[0, pl.ds(tile // 3, 1), part] = jnp.sum(low.astype(F32), axis=0, keepdims=True)
        run_at(tile, "up_back")
        return carry

    lax.fori_loop(0, 12, up_back, 0)

    def grad_up(tile, carry):
        cols = pl.ds(pl.multiple_of(256 * tile, 256), 256)
        _, _, dest = up_tile(tile)
        put_shares(r.g, pl.multiple_of(96 * (tile // 3), 32), dest, tn(r.low[...], r.act[:, cols]))
        run_at(tile, "grad_up")
        return carry

    lax.fori_loop(0, 12, grad_up, 0)
    for tile in range(3):
        cols = slice(256 * tile, 256 * tile + 256)
        r.res[:, cols] = r.res[:, cols] + sum(
            nt(r.act[:, 768 * j : 768 * j + 768], r.pool[0, j // 2, j % 2, cols, :])
            for j in range(4)
        )
    for block in range(4):
        rows = slice(64 * block, 64 * block + 64)
        given, hat = r.res[rows, :], r.hat[rows, :]
        sums[0] = sums[0] + jnp.sum(given * hat, axis=0, keepdims=True)
        sums[1] = sums[1] + jnp.sum(given, axis=0, keepdims=True)
        dres = norm_back(given, hat, r.scale[rows, 0:1], gain1)
        r.res[rows, :] = dres
        r.dlow[rows, :] = dres.astype(BF)
    for row in range(4):
        r.sm[0, 4 + row : 5 + row, :] = sums[row]
    run_plan("norm")
    for tile in range(3):
        cols = slice(256 * tile, 256 * tile + 256)
        put_shares(r.pool, 0, cols, tn(r.att[...], r.dlow[:, cols]))
    run_plan("out")
    for tile in range(3):
        cols = slice(256 * tile, 256 * tile + 256)
        r.att[:, cols] = nt(r.dlow[...], r.wo[cols, :]).astype(BF)
    run_plan("datt")

    def attend_back(pair, carry):
        attend_pair_back(pair, r)
        run_at(pair, "pairs")
        return carry

    lax.fori_loop(0, PAIRS, attend_back, 0)
    for tile in range(3):
        cols = slice(256 * tile, 256 * tile + 256)
        put_shares(r.pool, 192, cols, tn(r.x[0:256, :], r.q[:, cols]))
    run_plan("query")
    for tile in range(3):
        cols = slice(256 * tile, 256 * tile + 256)
        put_shares(r.pool, 288, cols, tn(r.x[...], r.k[:, cols]))
    run_plan("key")
    for tile in range(3):
        cols = slice(256 * tile, 256 * tile + 256)
        put_shares(r.pool, 384, cols, tn(r.x[...], r.v[:, cols]))
    run_plan("value")

    for tile in range(3):
        cols = slice(256 * tile, 256 * tile + 256)
        tail = nt(r.k[...], r.wk[cols, :]) + nt(r.v[...], r.wv[cols, :])
        r.relq[256:512, cols] = tail[256:512].astype(BF)
        r.relq[0:256, cols] = (
            tail[0:256] + r.res[:, cols] + nt(r.q[...], r.wq[cols, :])
        ).astype(BF)
    net.post("dx", "dx", 0, lambda: (r.relq.at[256:512, 0:768], r.dxr, pair))
    run_plan("input")
    net.came("dx", 0, lambda: (r.relq.at[256:512, 0:768], r.dxr, pair))
    r.din[...] = (r.relq[0:256, 0:768].astype(F32) + r.dxr[...].astype(F32)).astype(BF)
    give_back("d", r.din, r.input_grad)
    pl.when(own)(lambda: store("din", lambda: r.din.at[0:64], lambda: r.input_grad.at[micro, half]))
    run_plan("dxdone")
    run_plan("tail")
    if reduce:
        store("small", lambda: r.sm.at[5], lambda: r.small)

        @pl.when(is_end)
        def _():
            for u in range(len(CHUNKS)):
                net.got("z3%d" % u)

        store("share", lambda: r.sums, lambda: r.share)
    else:
        store("small", lambda: r.sm.at[0], lambda: r.small)
        store("share", lambda: r.g, lambda: r.share.at[0])
        last = pltpu.make_async_copy(r.pool, r.share.at[1], r.load_sem.at[0])
        last.start()
        last.wait()
    given_back("o", r.hidden_out)
    given_back("d", r.input_grad)
    stored("small")
    stored("share")

    @pl.when(own)
    def _():
        stored("hid")
        stored("din")
        net.posted("own")

    pl.when(far)(lambda: net.posted("far"))
    net.posted("all")
    net.finish("all")
    pl.when(is_end)(lambda: net.finish("end"))
    pl.when(is_mid)(lambda: net.finish("mid"))


PLAN = {
    "down0": ((C, 0),),
    "down1": ((C, 1),),
    "down2": ((C, 2), (F, 0),),
    "up_back": {
        1: ((F, 1),),
    },
    "grad_up": {
        2: ((C, 3),),
        3: ((S, 0),),
        5: ((C, 4),),
        6: ((F, 2),),
        8: ((C, 5),),
        11: ((C, 6),),
    },
    "norm": ((V, 0),),
    "out": ((C, 7), (S, 1), (T, 0),),
    "datt": ((F, 3),),
    "pairs": {
        0: ((V, 1),),
        1: ((S, 2), (T, 1),),
        2: ((F, 4),),
        3: ((M, 0), (S, 3), (T, 2), (F, 5),),
        4: ((M, 1), (S, 4), (V, 2),),
        5: ((C, 8), (N, 0), (T, 3),),
    },
    "query": ((C, 9), (F, 6), (M, 2),),
    "key": ((C, 10), (T, 4), (S, 5), (F, 8), (N, 1),),
    "value": ((C, 11), (C, 12), (M, 3), (V, 3),),
    "input": ((M, 4), (T, 5), (N, 2), (F, 7), (S, 6),),
    "dxdone": (
        (N, 4), (N, 3), (S, 8), (S, 7), (M, 5), (F, 9), (T, 6), (F, 10), (T, 7), (T, 8),
        (M, 6), (N, 5),
    ),
    "tail": (
        (M, 7), (S, 9), (S, 10), (N, 6), (M, 8), (T, 9), (F, 11), (V, 4), (F, 12), (T, 10),
        (N, 7), (M, 9), (S, 11), (N, 8), (T, 11), (M, 10), (S, 12), (T, 12), (N, 9), (M, 11),
        (N, 10), (M, 12), (N, 11), (N, 12), (V, 5),
    ),
}


def scratch(reduce):
    shapes = [
        ("x", (512, 768), BF),
        ("facts", (8, 128), jnp.int32),
        ("meta", (4, 8, 128), jnp.int32),
        ("cot", (256, 768), BF),
        ("vectors", (8, 768), F32),
        ("wq", (768, 768), BF),
        ("wk", (768, 768), BF),
        ("wv", (768, 768), BF),
        ("wo", (768, 768), BF),
        ("wr", (768, 768), BF),
        ("pool", (2, 2, 2, 768, 768), BF),
        ("g", (2, 2, 2, 768, 768), BF),
        ("sine", (256, 384), F32),
        ("cosine", (256, 384), F32),
        ("feat", (512, 896), BF),
        ("q", (256, 768), BF),
        ("k", (512, 768), BF),
        ("v", (512, 768), BF),
        ("att", (256, 768), BF),
        ("relq", (512, 896), BF),
        ("score", (512, 512), F32),
        ("dlog", (512, 512), BF),
        ("probs", (PAIRS, 512, 512), BF),
        ("res", (256, 768), F32),
        ("hat", (256, 768), F32),
        ("scale", (256, 128), F32),
        ("low", (256, 768), BF),
        ("act", (256, 3072), BF),
        ("dlow", (256, 768), BF),
        ("out", (256, 768), BF),
        ("dxr", (256, 768), BF),
        ("din", (256, 768), BF),
        ("sm", (6, 8, 768), F32),
    ]
    if reduce:
        shapes += [("r1_%d" % u, (2, 2, c[2], 768), BF) for u, c in enumerate(CHUNKS)]
        shapes += [
            ("ra", (2, 624, 768), BF),
            ("rb", (2, 624, 768), BF),
            ("ra2", (624, 768), BF),
            ("rb2", (624, 768), BF),
            ("zr", (1248, 768), BF),
            ("za", (1248, 768), BF),
            ("sums", (1248, 768), BF),
            ("smr", (5, 8, 768), F32),
        ]
    return shapes


def layer(lengths, hidden_in, boxes, cotangent, vectors, weights, reduce):
    hi, lo = trig_tables(QUARTER)
    any_space = pl.BlockSpec(memory_space=pl.ANY)
    vmem = pl.BlockSpec(memory_space=pltpu.VMEM)
    ins = (
        ("lengths", lengths.reshape(-1), pl.BlockSpec(memory_space=pltpu.SMEM)),
        ("hidden_in", hidden_in, any_space),
        ("cotangent", cotangent, any_space),
        ("boxes", boxes, vmem),
        ("hi", jnp.asarray(hi), vmem),
        ("lo", jnp.asarray(lo), vmem),
    )
    ins += tuple(("vector%d" % i, v, vmem) for i, v in enumerate(vectors))
    ins += tuple((name, w, any_space) for name, w in weights)
    outs = (
        ("hidden_out", (2, 128, 768), BF),
        ("input_grad", (2, 128, 768), BF),
        ("share", (1248, 768) if reduce else (2, 2, 2, 2, 768, 768), BF),
        ("small", (8, 768), F32),
    )
    shapes = scratch(reduce)
    sems = ("send_sem", "recv_sem", "post_sem", "load_sem", "store_sem")
    names = tuple(i[0] for i in ins) + tuple(o[0] for o in outs)
    names += tuple(s[0] for s in shapes) + sems
    dma = pltpu.SemaphoreType.DMA
    return pl.pallas_call(
        functools.partial(layer_kernel, names, reduce),
        out_shape=[jax.ShapeDtypeStruct(o[1], o[2]) for o in outs],
        in_specs=[i[2] for i in ins],
        out_specs=[any_space] * len(outs),
        scratch_shapes=[pltpu.VMEM(s[1], s[2]) for s in shapes]
        + [dma((len(i),)) for i in (SENDS, SENDS, POSTS, LOADS, STORES)],
        compiler_params=pltpu.CompilerParams(
            vmem_limit_bytes=VMEM_LIMIT, collective_id=0, has_side_effects=True
        ),
        name="layer",
    )(*[i[1] for i in ins])


def finish_kernel(share, small, hid, din, hidden, dinput, dq, dk, dv, dout, drel, dup, *rest):
    dbup, ddown, vectors = rest[0], rest[1], rest[2:]
    hidden[...] = hid[...]
    dinput[...] = din[...]
    for j in range(4):
        dup[:, 768 * j : 768 * j + 768] = share[96 * j : 96 * j + 96, :].astype(F32)
    ddown[...] = share[384:768, :].astype(F32)
    for i, ref in enumerate((dout, drel, dq, dk, dv)):
        ref[...] = share[768 + 96 * i : 864 + 96 * i, :].astype(F32)
    dp = lax.axis_index("dp")
    row = small[pl.ds(dp // 2, 1), :]
    dbup[...] = jnp.where(dp % 2 == 0, row[:, 0:384], row[:, 384:768]).reshape(384)
    turned = pltpu.roll(small[...], lax.rem(768 - 96 * dp, 768), 1)
    for i, ref in enumerate(vectors):
        ref[...] = turned[4 + i : 5 + i, 0:96].reshape(96)


def finish(share, small, hidden, dinput):
    shapes = [(96, 768)] * 5 + [(96, 3072), (384,), (384, 768)] + [(96,)] * 4
    low = jax.ShapeDtypeStruct(hidden.shape, BF)
    return pl.pallas_call(
        finish_kernel,
        out_shape=[low, low] + [jax.ShapeDtypeStruct(s, F32) for s in shapes],
        name="finish",
    )(share, small, hidden, dinput)


def finish_any(g, small):
    order = g.transpose(0, 2, 3, 1, 4, 5).reshape(2, 8, 768, 768)

    def weight(which, base):
        return order[which, :, base : base + 96].reshape(768, 768)

    up = jnp.concatenate([weight(0, 96 * j) for j in range(4)], axis=1)
    down = order[0, :, 384:768].reshape(3072, 768)
    full = [weight(1, base) for base in (192, 288, 384, 0, 96)] + [up, down]
    grads = [
        lax.psum(lax.psum_scatter(w, "dp", scatter_dimension=0, tiled=True), "seq").astype(F32)
        for w in full
    ]
    small = lax.psum(small, ("dp", "seq"))
    dp, count = lax.axis_index("dp"), lax.axis_size("dp")

    def own_part(vector):
        size = vector.shape[0] // count
        return lax.dynamic_slice_in_dim(vector, dp * size, size)

    parts = [own_part(small[4 + i]) for i in range(4)]
    return grads[:6] + [own_part(small[0:4].reshape(-1)), grads[6]] + parts


def shards(
    hidden_in,
    boxes,
    lengths,
    w_query,
    w_key,
    w_value,
    w_out,
    w_rel,
    w_up,
    b_up,
    w_down,
    gain_attn,
    bias_attn,
    gain_ffn,
    bias_ffn,
    cotangent,
):
    vectors = (b_up, gain_attn, bias_attn, gain_ffn, bias_ffn)
    weights = (
        ("w_query", w_query),
        ("w_key", w_key),
        ("w_value", w_value),
        ("w_out", w_out),
        ("w_rel", w_rel),
        ("w_up", w_up),
        ("w_down", w_down),
    )
    reduce = lax.axis_size("dp") == 8
    hidden, dinput, share, small = layer(
        lengths,
        hidden_in[:, 0],
        boxes[:, :, 0],
        cotangent[:, 0],
        vectors,
        weights,
        reduce,
    )
    if reduce:
        hidden, dinput, *rest = finish(share, small, hidden, dinput)
    else:
        rest = finish_any(share, small)
    return (hidden[:, None], dinput[:, None], *rest)


def solution(mesh):
    rows = P(None, "dp", "seq", None)
    placed = (rows, P(None, None, "dp", "seq"), P(None, "dp")) + (P(),) * 12 + (rows,)
    matrix, vector = P("dp", None), P("dp")
    return jax.shard_map(
        shards,
        mesh=mesh,
        in_specs=placed,
        out_specs=(rows, rows) + (matrix,) * 6 + (vector, matrix) + (vector,) * 4,
        check_vma=False,
    )
```

```python
import functools

import jax
import jax.numpy as jnp
import numpy as np
from jax import lax
from jax.experimental import pallas as pl
from jax.experimental.pallas import tpu as pltpu
from jax.sharding import PartitionSpec as P

HEADS = 12
EPS = 1e-05
BF = jnp.bfloat16
F32 = jnp.float32
PAIRS = HEADS // 2
VMEM_LIMIT = 67043328
QUARTER = 192


def nn(a, b):
    return lax.dot_general(a, b, (((1,), (0,)), ((), ())), preferred_element_type=F32)


def nt(a, b):
    return lax.dot_general(a, b, (((1,), (1,)), ((), ())), preferred_element_type=F32)


def tn(a, b):
    return lax.dot_general(a, b, (((0,), (0,)), ((), ())), preferred_element_type=F32)


def trig_tables(quarter):
    freq = 10000.0 ** (-np.arange(quarter) / quarter)
    tables = []
    for step in (32.0, 1.0):
        angle = step * np.arange(32)[:, None] * freq[None, :]
        rest = np.concatenate([np.sin(angle), np.cos(angle)], axis=1).astype(np.float32)
        parts = []
        for _ in range(3):
            part = rest.astype(BF)
            parts.append(part)
            rest = rest - part.astype(np.float32)
        tables.append(np.concatenate(parts, axis=0))
    return tables


def features(slot, c, micro, r):
    half = 2 * QUARTER
    iota = lax.broadcasted_iota(jnp.int32, (32, 128), 0)
    hi_tab, lo_tab = r.hi[...], r.lo[...]
    block = pltpu.roll(r.meta[slot], 64 * c, 1)
    sines, cosines = [], []
    for axis in range(2):
        where = jnp.where(micro == 0, block[axis : axis + 1], block[2 + axis : 3 + axis])
        pick_hi = (iota == lax.shift_right_logical(where, 5)).astype(F32).astype(BF)
        pick_lo = (iota == (where & 31)).astype(F32).astype(BF)
        hi = tn(jnp.concatenate([pick_hi] * 3, axis=0), hi_tab)
        lo = tn(jnp.concatenate([pick_lo] * 3, axis=0), lo_tab)
        sin_hi, cos_hi = hi[:, :QUARTER], hi[:, QUARTER:]
        sin_lo, cos_lo = lo[:, :QUARTER], lo[:, QUARTER:]
        sines.append(sin_hi * cos_lo + cos_hi * sin_lo)
        cosines.append(cos_hi * cos_lo - sin_hi * sin_lo)
    sine = jnp.concatenate(sines, axis=1)
    cosine = jnp.concatenate(cosines, axis=1)
    for part in range(2):
        mine = slice(64 * part, 64 * part + 64)
        rows = pl.ds(256 * part + 64 * slot, 64)
        r.feat[rows, 0:half] = cosine[mine].astype(BF)
        r.feat[rows, half : 2 * half] = sine[mine].astype(BF)
    rows = pl.ds(64 * slot, 64)
    r.sine[rows, :] = sine[0:64]
    r.cosine[rows, :] = cosine[0:64]


def head_stack(pair):
    first = lax.broadcasted_iota(jnp.int32, pair.shape, 1) < 64
    zero = jnp.zeros_like(pair)
    return jnp.concatenate([jnp.where(first, pair, zero), jnp.where(first, zero, pair)], axis=0)


def head_join(stack):
    half = stack.shape[0] // 2
    first = lax.broadcasted_iota(jnp.int32, (half, 128), 1) < 64
    return jnp.where(first, stack[:half], stack[half:])


def attend_pair(pair, live, r):
    cols = pl.ds(pl.multiple_of(128 * pair, 128), 128)
    stack = head_stack(r.q[:, cols].astype(F32) * 0.125).astype(BF)
    for head in range(2):
        rows = slice(256 * head, 256 * head + 256)
        left = nt(stack[rows], r.wr[0:384, cols])
        right = nt(stack[rows], r.wr[384:768, cols])
        sin, cos = r.sine[...], r.cosine[...]
        r.relq[rows, 0:384] = (left * sin + right * cos).astype(BF)
        r.relq[rows, 384:768] = (right * sin - left * cos).astype(BF)
    r.relq[:, 768:896] = stack
    r.feat[:, 768:896] = r.k[:, cols]
    r.score[...] = nt(r.relq[...], r.feat[...])
    for block in range(8):
        rows = pl.ds(64 * block, 64)
        score = jnp.where(live, r.score[rows, :], -1e30)
        top = jnp.max(score, axis=-1, keepdims=True)
        weight = jnp.exp(score - top)
        total = jnp.sum(weight, axis=-1, keepdims=True)
        r.probs[pair, rows, :] = (weight * (1.0 / total)).astype(BF)
    r.att[:, cols] = head_join(nn(r.probs[pair], r.v[:, cols])).astype(BF)


def attend_pair_back(pair, r):
    cols = pl.ds(pl.multiple_of(128 * pair, 128), 128)
    given = head_stack(r.att[:, cols].astype(F32)).astype(BF)
    stack = head_stack(r.q[:, cols].astype(F32)).astype(BF)
    r.score[...] = nt(given, r.v[:, cols])
    for block in range(8):
        rows = pl.ds(64 * block, 64)
        prob = r.probs[pair, rows, :].astype(F32)
        push = prob * r.score[rows, :]
        mean = jnp.sum(push, axis=-1, keepdims=True)
        r.dlog[rows, :] = ((push - prob * mean) * 0.125).astype(BF)
    r.feat[:, 768:896] = r.k[:, cols]
    r.v[:, cols] = tn(r.probs[pair], given).astype(BF)
    r.k[:, cols] = tn(r.dlog[...], stack).astype(BF)
    for head in range(2):
        rows = slice(256 * head, 256 * head + 256)
        first = nn(r.dlog[rows, :], r.feat[:, 0:384])
        second = nn(r.dlog[rows, :], r.feat[:, 384:768])
        sin, cos = r.sine[...], r.cosine[...]
        r.relq[rows, 0:384] = (first * sin - second * cos).astype(BF)
        r.relq[rows, 384:768] = (first * cos + second * sin).astype(BF)
    dq = nn(r.dlog[...], r.feat[:, 768:896]) + nn(r.relq[:, 0:768], r.wr[:, cols])
    r.q[:, cols] = head_join(dq).astype(BF)
    part = tn(r.relq[:, 0:768], stack).astype(BF)
    for piece, share in enumerate((0, 1, 4, 5, 2, 3, 6, 7)):
        c, y, x = share % 2, share // 4, share // 2 % 2
        r.pool[c, y, x, 96:192, cols] = part[96 * piece : 96 * piece + 96]


def norm_back(given, hat, scale, gain):
    push = given * gain
    mean = jnp.mean(push, axis=-1, keepdims=True)
    lean = jnp.mean(push * hat, axis=-1, keepdims=True)
    return scale * (push - mean - hat * lean)


def put_shares(ref, base, cols, part):
    for share in range(8):
        c, y, x = share % 2, share // 4, share // 2 % 2
        ref[c, y, x, pl.ds(base, 96), cols] = part[96 * share : 96 * share + 96].astype(BF)


class Refs:
    pass


CHUNKS = (
    ("g", 384, 128, 384),
    ("g", 512, 128, 512),
    ("g", 640, 128, 640),
    ("g", 0, 96, 0),
    ("g", 96, 96, 96),
    ("g", 192, 96, 192),
    ("g", 288, 96, 288),
    ("pool", 0, 96, 768),
    ("pool", 96, 96, 864),
    ("pool", 192, 96, 960),
    ("pool", 288, 96, 1056),
    ("pool", 384, 64, 1152),
    ("pool", 448, 32, 1216),
)
C, F, S, T, M, N, V = range(7)
STAGES = ("core", "xa", "xb", "ya", "yb", "z1", "z2", "z3")
BLOCKS = ("x", "m", "c", "f", "o", "d")
SENDS = tuple(k + str(i) for k in BLOCKS for i in range(4)) + ("dx0",)
SENDS += tuple("s%d" % i for i in range(5))
SENDS += tuple("%s%d" % (s, u) for u in range(len(CHUNKS)) for s in STAGES)
LOADS = ("x", "x2", "cot", "key", "value", "query", "out")
LOADS += tuple("rel%d" % i for i in range(4)) + tuple("up%d" % i for i in range(4))
LOADS += tuple("down%d" % i for i in range(4))
STORES = ("hid", "din", "share", "small")
POSTS = tuple(k + i for k in "xmc" for i in ("a0", "a1", "b0", "b1", "p"))
POSTS += tuple(k + str(i) for k in "fod" for i in range(4)) + ("dx",)


class Net:
    def __init__(self, r):
        self.r = r
        self.made = {}
        self.order = {"all": [], "end": [], "mid": []}
        self.posts = {"all": [], "own": [], "far": []}

    def _of(self, name):
        i = SENDS.index(name)
        src, dst, peer = self.made[name]()
        return pltpu.make_async_remote_copy(
            src_ref=src,
            dst_ref=dst,
            send_sem=self.r.send_sem.at[i],
            recv_sem=self.r.recv_sem.at[i],
            device_id=peer,
            device_id_type=pl.DeviceIdType.MESH,
        )

    def start(self, name, make, role="all"):
        self.made[name] = make
        self._of(name).start()
        self.order[role].append(name)

    def got(self, name):
        self._of(name).wait_recv()

    def _post(self, name, src, dst, at, peer):
        return pltpu.make_async_remote_copy(
            src_ref=src,
            dst_ref=dst,
            send_sem=self.r.post_sem.at[POSTS.index(name)],
            recv_sem=self.r.recv_sem.at[at],
            device_id=peer,
            device_id_type=pl.DeviceIdType.MESH,
        )

    def post(self, name, kind, index, make, role="all"):
        src, dst, peer = make()
        self._post(name, src, dst, SENDS.index(kind + "0") + index, peer).start()
        self.posts[role].append((name, kind, index, make))

    def came(self, kind, index, make):
        src, dst, peer = make()
        self._post(POSTS[0], src, dst, SENDS.index(kind + "0") + index, peer).wait_recv()

    def finish(self, role):
        for name in self.order[role]:
            self._of(name).wait_send()

    def posted(self, role):
        for name, kind, index, make in self.posts[role]:
            src, dst, peer = make()
            self._post(name, src, dst, SENDS.index(kind + "0") + index, peer).wait_send()


def add_rows(count, body):
    size = 48 if count % 48 == 0 else 32 if count % 32 == 0 else 16

    def step(i, carry):
        body(pl.multiple_of(size * i, 16), size)
        return carry

    lax.fori_loop(0, count // size, step, 0)


def total(*terms):
    out = terms[0].astype(F32)
    for term in terms[1:]:
        out = out + term.astype(F32)
    return out.astype(BF)


class Reduction:
    def __init__(self, r, net, dp, z):
        self.r, self.net = r, net
        self.c, self.x, self.y = dp % 2, dp // 2 % 2, dp // 4
        self.pc = (dp + 1 - 2 * self.c, z)
        self.px = (dp + 2 - 4 * self.x, z)
        self.py = (dp + 4 - 8 * self.y, z)
        self.pz1 = (dp, z + 1 - 2 * (z % 2))
        self.pz2 = (dp, (z + 2) % 4)
        self.across = (dp, 3 - z)

    def parts(self, u):
        name, base, rows, out = CHUNKS[u]
        return getattr(self.r, name), base, rows // 2, out, self.r.r1[u], out // 2

    def core(self, u):
        g, base, half, _, r1, _ = self.parts(u)
        self.net.start(
            "core%d" % u, lambda: (g.at[1 - self.c, :, :, pl.ds(base, 2 * half)], r1, self.pc)
        )

    def first(self, u):
        g, base, half, _, r1, at = self.parts(u)
        c, x, y = self.c, self.x, self.y
        self.net.got("core%d" % u)

        def add(i, size):
            for k in range(2):
                rows, own = pl.ds(base + i, size), pl.ds(i, size)
                g[c, k, 1 - x, rows] = total(g[c, k, 1 - x, rows], r1[k, 1 - x, own])
                rows, own = pl.ds(base + half + i, size), pl.ds(half + i, size)
                g[c, 1 - y, k, rows] = total(g[c, 1 - y, k, rows], r1[1 - y, k, own])

        add_rows(half, add)
        a, b, to = pl.ds(base, half), pl.ds(base + half, half), pl.ds(at, half)
        self.net.start("xa%d" % u, lambda: (g.at[c, :, 1 - x, a], self.r.ra.at[:, to], self.px))
        self.net.start("yb%d" % u, lambda: (g.at[c, 1 - y, :, b], self.r.rb.at[:, to], self.py))

    def second(self, u):
        g, base, half, _, r1, at = self.parts(u)
        c, x, y = self.c, self.x, self.y
        ra, rb = self.r.ra, self.r.rb
        self.net.got("xa%d" % u)
        self.net.got("yb%d" % u)

        def add(i, size):
            came = pl.ds(at + i, size)
            rows, own = pl.ds(base + i, size), pl.ds(i, size)
            g[c, 1 - y, x, rows] = total(g[c, 1 - y, x, rows], r1[1 - y, x, own], ra[1 - y, came])
            rows, own = pl.ds(base + half + i, size), pl.ds(half + i, size)
            g[c, y, 1 - x, rows] = total(g[c, y, 1 - x, rows], r1[y, 1 - x, own], rb[1 - x, came])

        add_rows(half, add)
        a, b, to = pl.ds(base, half), pl.ds(base + half, half), pl.ds(at, half)
        self.net.start("ya%d" % u, lambda: (g.at[c, 1 - y, x, a], self.r.ra2.at[to], self.py))
        self.net.start("xb%d" % u, lambda: (g.at[c, y, 1 - x, b], self.r.rb2.at[to], self.px))

    def third(self, u, mid):
        g, base, half, out, r1, at = self.parts(u)
        c, x, y = self.c, self.x, self.y
        ra, rb, ra2, rb2, zr = self.r.ra, self.r.rb, self.r.ra2, self.r.rb2, self.r.zr
        self.net.got("ya%d" % u)
        self.net.got("xb%d" % u)
        if mid:
            self.net.got("z1%d" % u)

        def add(i, size):
            came = pl.ds(at + i, size)
            rows, own = pl.ds(base + i, size), pl.ds(i, size)
            more = (zr[pl.ds(out + i, size)],) if mid else ()
            g[c, y, x, rows] = total(
                g[c, y, x, rows], r1[y, x, own], ra[y, came], ra2[came], *more
            )
            rows, own = pl.ds(base + half + i, size), pl.ds(half + i, size)
            more = (zr[pl.ds(out + half + i, size)],) if mid else ()
            g[c, y, x, rows] = total(
                g[c, y, x, rows], r1[y, x, own], rb[x, came], rb2[came], *more
            )

        add_rows(half, add)
        rows, to = pl.ds(base, 2 * half), pl.ds(out, 2 * half)
        if mid:
            make = lambda: (g.at[c, y, x, rows], self.r.za.at[to], self.across)
            self.net.start("z2%d" % u, make, "mid")
        else:
            make = lambda: (g.at[c, y, x, rows], self.r.zr.at[to], self.pz1)
            self.net.start("z1%d" % u, make, "end")

    def fourth(self, u):
        g, base, half, out, _, _ = self.parts(u)
        c, x, y = self.c, self.x, self.y
        self.net.got("z2%d" % u)

        def add(i, size):
            rows, to = pl.ds(base + i, size), pl.ds(out + i, size)
            self.r.sums[to] = total(g[c, y, x, rows], self.r.za[to])

        add_rows(2 * half, add)
        to = pl.ds(out, 2 * half)
        self.net.start("z3%d" % u, lambda: (self.r.sums.at[to], self.r.sums.at[to], self.pz1), "mid")

    def small(self, i):
        if i:
            self.net.got("s%d" % (i - 1))
            self.r.sm[i] = self.r.sm[i - 1] + self.r.smr[i - 1]
        if i < 5:
            peer = (self.pc, self.px, self.py, self.pz1, self.pz2)[i]
            self.net.start("s%d" % i, lambda: (self.r.sm.at[i], self.r.smr.at[i], peer))


def layer_kernel(names, reduce, *refs):
    r = Refs()
    for name, ref in zip(names, refs):
        setattr(r, name, ref)
    dp, z = lax.axis_index("dp"), lax.axis_index("seq")
    micro, c = z // 2, dp % 2
    is_mid = lax.rem(z, 3) > 0
    is_end = lax.rem(z, 3) == 0
    own = c == z % 2
    far = c != z % 2
    base = jnp.where(own, 0, 1)
    column = dp - c
    source = column + z % 2
    pair = (dp + 1 - 2 * c, z)
    half = pl.ds(pl.multiple_of(64 * c, 64), 64)
    other = pl.ds(pl.multiple_of(64 - 64 * c, 64), 64)
    net = Net(r)
    red = None
    if reduce:
        r.r1 = tuple(getattr(r, "r1_%d" % u) for u in range(len(CHUNKS)))
        red = Reduction(r, net, dp, z)

    def kept(u):
        rows = pl.ds(CHUNKS[u][3], CHUNKS[u][2])
        return pltpu.make_async_copy(r.sums.at[rows], r.share.at[rows], r.keep_sem.at[u])

    def whole(u):
        red.fourth(u)
        kept(u).start()

    def run(*steps):
        if not reduce:
            return
        for kind, u in steps:
            if kind == C:
                red.core(u)
            elif kind == F:
                red.first(u)
            elif kind == S:
                red.second(u)
            elif kind == T:
                pl.when(is_end)(functools.partial(red.third, u, False))
            elif kind == M:
                pl.when(is_mid)(functools.partial(red.third, u, True))
            elif kind == N:
                pl.when(is_mid)(functools.partial(whole, u))
            else:
                red.small(u)

    def run_plan(place):
        run(*PLAN.get(place, ()))

    def run_at(index, place):
        for at, steps in PLAN[place].items():
            pl.when(index == at)(functools.partial(run, *steps))

    loads = {}

    def load(name, src, dst):
        loads[name] = lambda: (src(), dst(), r.load_sem.at[LOADS.index(name)])
        pltpu.make_async_copy(*loads[name]()).start()

    def loaded(name):
        pltpu.make_async_copy(*loads[name]()).wait()

    load("key", lambda: r.w_key, lambda: r.wk)
    load("value", lambda: r.w_value, lambda: r.wv)
    load("query", lambda: r.w_query, lambda: r.wq)

    greet = [pair] + [(column + h, (z + i) % 4) for i in range(1, 4) for h in range(2)]
    greet += [red.px, red.py] if reduce else []
    line = lax.broadcasted_iota(jnp.int32, (8, 128), 0)
    wide = [r.boxes[axis, m : m + 1, :] for m in range(2) for axis in range(2)]
    wide = jnp.concatenate(wide * 2, axis=0)
    wide = jnp.where(line == 4, r.lengths[0], jnp.where(line == 5, r.lengths[1], wide))
    r.facts[...] = wide
    barrier = pltpu.get_barrier_semaphore()
    for peer in greet:
        pl.semaphore_signal(barrier, 1, device_id=peer, device_id_type=pl.DeviceIdType.MESH)
    pl.semaphore_wait(barrier, len(greet))

    def spread(kind, src, dst):
        for first in (False, True):
            step = base if first else base + 2
            to = (z + 4 - step) % 4
            rows = pl.ds(pl.multiple_of(64 * step, 64), 64)
            for h in range(2):
                def make(h=h, to=to, rows=rows, step=step):
                    return src(to // 2, pl.ds(64 * h, 64)), dst(step, rows), (column + h, to)

                name = kind + ("a" if first else "b") + str(h)
                if first:
                    pl.when(far)(functools.partial(net.post, name, kind, step, make, "far"))
                else:
                    net.post(name, kind, step, make)

    def here(kind, src, dst):
        make = lambda: (src(micro, other), dst(0, pl.ds(0, 64)), pair)
        net.post(kind + "p", kind, 0, make, "own")

    hidden = lambda m, rows: r.hidden_in.at[m, rows]
    grads = lambda m, rows: r.cotangent.at[m, rows]

    x_to = lambda step, rows: r.x.at[rows]
    m_to = lambda step, rows: r.meta.at[step]
    c_to = lambda step, rows: r.cot.at[rows]
    spread("m", lambda m, rows: r.facts, m_to)
    spread("x", hidden, x_to)

    @pl.when(own)
    def _():
        here("m", lambda m, rows: r.facts, m_to)
        here("x", hidden, x_to)
        make = lambda: (hidden(micro, half), r.x.at[256:320], pair)
        net.post("f0", "f", 0, make, "own")
        load("x", lambda: hidden(micro, half), lambda: r.x.at[0:64])
        load("x2", lambda: hidden(micro, other), lambda: r.x.at[256:320])
        r.meta[0] = r.facts[...]

    for i, (dst, src) in enumerate(((0, 0), (192, 384), (384, 192), (576, 576))):
        load("rel%d" % i, lambda src=src, dst=dst: r.w_rel.at[src : src + 192], lambda src=src, dst=dst: r.wr.at[dst : dst + 192])
    load("out", lambda: r.w_out, lambda: r.wo)
    for j in range(4):
        load("up%d" % j, lambda j=j: r.w_up.at[:, 768 * j : 768 * j + 768], lambda j=j: r.pool.at[0, j // 2, j % 2])
    for j in range(4):
        load("down%d" % j, lambda j=j: r.w_down.at[768 * j : 768 * j + 768], lambda j=j: r.pool.at[1, j // 2, j % 2])
    pl.when(own)(lambda: load("cot", lambda: grads(micro, half), lambda: r.cot.at[0:64]))

    def project(start, stop):
        rows = slice(start, stop)
        for tile in range(3):
            cols = slice(256 * tile, 256 * tile + 256)
            r.k[rows, cols] = nn(r.x[rows, :], r.wk[:, cols]).astype(BF)
            r.v[rows, cols] = nn(r.x[rows, :], r.wv[:, cols]).astype(BF)
            if stop <= 256:
                r.q[rows, cols] = nn(r.x[rows, :], r.wq[:, cols]).astype(BF)

    for j in range(4):
        r.vectors[j : j + 1, :] = r.vector0[768 * j : 768 * j + 768].astype(F32).reshape(1, 768)
        row = getattr(r, "vector%d" % (j + 1))[...]
        r.vectors[4 + j : 5 + j, :] = row.astype(F32).reshape(1, 768)
    x_size = lambda: (hidden(0, pl.ds(0, 64)), r.x.at[0:64], pair)
    m_size = lambda: (r.facts, r.meta.at[0], pair)
    pl.when(far)(lambda: net.came("m", 0, m_size))
    features(0, c, micro, r)
    for slot in (1, 3, 2):
        net.came("m", slot, m_size)
        features(slot, c, micro, r)
    loaded("key")
    loaded("value")
    loaded("query")

    @pl.when(own)
    def _():
        loaded("x")
        loaded("x2")

    @pl.when(far)
    def _():
        net.came("x", 0, x_size)
        net.came("f", 0, x_size)

    project(0, 64)
    project(256, 320)
    for i in range(4):
        loaded("rel%d" % i)
    for slot in (1, 3, 2):
        net.came("x", slot, x_size)
        mine, theirs = slice(64 * slot, 64 * slot + 64), slice(256 + 64 * slot, 320 + 64 * slot)
        make = lambda mine=mine, theirs=theirs: (r.x.at[mine], r.x.at[theirs], pair)
        net.post("f%d" % slot, "f", slot, make)
    spread("c", grads, c_to)
    pl.when(own)(lambda: here("c", grads, c_to))
    project(64, 256)
    for slot in (1, 3, 2):
        net.came("f", slot, x_size)
    project(320, 512)

    place = lax.broadcasted_iota(jnp.int32, (1, 512), 1)
    turn = lax.shift_right_logical(place, 8)
    token = 128 * ((z + (lax.shift_right_logical(place, 6) & 3)) & 3) + (place & 63)
    token = token + 64 * ((c + turn) & 1)
    known = r.meta[1]
    length = jnp.where(micro == 0, known[4:5], known[5:6])
    live = token < jnp.concatenate([length] * 4, axis=1)

    def attend(pair, carry):
        attend_pair(pair, live, r)
        return carry

    lax.fori_loop(0, PAIRS, attend, 0)

    loaded("out")
    for tile in range(3):
        cols = slice(256 * tile, 256 * tile + 256)
        r.res[:, cols] = r.x[0:256, cols].astype(F32) + nn(r.att[...], r.wo[:, cols])

    gain1, bias1, gain2, bias2 = [r.vectors[4 + i : 5 + i, :] for i in range(4)]
    for block in range(4):
        rows = slice(64 * block, 64 * block + 64)
        res = r.res[rows, :]
        center = res - jnp.mean(res, axis=-1, keepdims=True)
        scale = lax.rsqrt(jnp.mean(center * center, axis=-1, keepdims=True) + EPS)
        hat = center * scale
        r.hat[rows, :] = hat
        r.scale[rows, :] = jnp.broadcast_to(scale, (64, 128))
        normed = hat * gain1 + bias1
        r.res[rows, :] = normed
        r.low[rows, :] = normed.astype(BF)

    for j in range(4):
        loaded("up%d" % j)
    for j in range(4):
        loaded("down%d" % j)

    def up_tile(tile):
        j = tile // 3
        return j // 2, j % 2, pl.ds(pl.multiple_of(256 * (tile % 3), 256), 256)

    def up(tile, carry):
        cols = pl.ds(pl.multiple_of(256 * tile, 256), 256)
        y, x, part = up_tile(tile)
        bias = r.vectors[pl.ds(tile // 3, 1), part]
        value = nn(r.low[...], r.pool[0, y, x, :, part]) + bias
        below = 0.5 * (1.0 + lax.erf(value * np.float32(np.sqrt(0.5))))
        r.act[:, cols] = (value * below).astype(BF)
        top = value.astype(BF)
        r.g[0, y, x, 0:256, part] = top
        r.g[1, y, x, 0:256, part] = (value - top.astype(F32)).astype(BF)
        return carry

    lax.fori_loop(0, 12, up, 0)
    for tile in range(3):
        cols = slice(256 * tile, 256 * tile + 256)
        r.res[:, cols] = r.res[:, cols] + sum(
            nn(r.act[:, 768 * j : 768 * j + 768], r.pool[1, j // 2, j % 2, :, cols])
            for j in range(4)
        )

    c_size = lambda: (grads(0, pl.ds(0, 64)), r.cot.at[0:64], pair)
    pl.when(own)(lambda: loaded("cot"))
    pl.when(far)(lambda: net.came("c", 0, c_size))
    for slot in (1, 2, 3):
        net.came("c", slot, c_size)
    sums = [jnp.zeros((1, 768), F32) for _ in range(4)]
    for block in range(4):
        rows = slice(64 * block, 64 * block + 64)
        res = r.res[rows, :]
        center = res - jnp.mean(res, axis=-1, keepdims=True)
        scale = lax.rsqrt(jnp.mean(center * center, axis=-1, keepdims=True) + EPS)
        hat = center * scale
        r.out[rows, :] = (hat * gain2 + bias2).astype(BF)
        given = r.cot[rows, :].astype(F32)
        sums[2] = sums[2] + jnp.sum(given * hat, axis=0, keepdims=True)
        sums[3] = sums[3] + jnp.sum(given, axis=0, keepdims=True)
        dres = norm_back(given, hat, scale, gain2)
        r.res[rows, :] = dres
        r.dlow[rows, :] = dres.astype(BF)

    def grad_down(offset):
        for quad in range(2):
            shares = range(4 * quad, 4 * quad + 4)
            starts = [384 * share + offset for share in shares]
            left = jnp.concatenate([r.act[:, at : at + 128] for at in starts], axis=1)
            part = tn(left, r.dlow[...]).astype(BF)
            for i, share in enumerate(shares):
                place = (share % 2, share // 4, share // 2 % 2, pl.ds(384 + offset, 128))
                r.g[place] = part[128 * i : 128 * i + 128]

    for third in range(3):
        grad_down(128 * third)
        run_plan("down%d" % third)
    stores = {}

    def store(name, src, dst):
        stores[name] = lambda: (src(), dst(), r.store_sem.at[STORES.index(name)])
        pltpu.make_async_copy(*stores[name]()).start()

    def stored(name):
        pltpu.make_async_copy(*stores[name]()).wait()

    def give_back(kind, src, dst):
        for slot in (3, 1, 2, 0):
            rows = slice(64 * slot, 64 * slot + 64)
            to = (source, (z + slot) % 4)
            make = lambda rows=rows, to=to: (src.at[rows], dst.at[micro, half], to)
            role = "all" if slot else "far"
            post = functools.partial(net.post, kind + str(slot), kind, 2 * micro + c, make, role)
            if slot:
                post()
            else:
                pl.when(far)(post)

    def given_back(kind, dst):
        size = lambda: (r.out.at[0:64], dst.at[0, 0:64], pair)
        for m in range(2):
            for h in range(2):
                local = own & (micro == m) & (c == h)
                pl.when(jnp.logical_not(local))(functools.partial(net.came, kind, 2 * m + h, size))

    give_back("o", r.out, r.hidden_out)
    pl.when(own)(lambda: store("hid", lambda: r.out.at[0:64], lambda: r.hidden_out.at[micro, half]))

    def up_back(tile, carry):
        cols = pl.ds(pl.multiple_of(256 * tile, 256), 256)
        y, x, part = up_tile(tile)
        value = r.g[0, y, x, 0:256, part].astype(F32) + r.g[1, y, x, 0:256, part].astype(F32)
        below = 0.5 * (1.0 + lax.erf(value * np.float32(np.sqrt(0.5))))
        dense = jnp.exp(value * value * -0.5) * np.float32(1.0 / np.sqrt(2.0 * np.pi))
        slope = below + value * dense
        push = nt(r.dlow[...], r.pool[1, y, x, part, :]) * slope
        low = push.astype(BF)
        r.act[:, cols] = low
        r.sm[0, pl.ds(tile // 3, 1), part] = jnp.sum(low.astype(F32), axis=0, keepdims=True)
        run_at(tile, "up_back")
        return carry

    lax.fori_loop(0, 12, up_back, 0)

    def grad_up(tile, carry):
        cols = pl.ds(pl.multiple_of(256 * tile, 256), 256)
        _, _, dest = up_tile(tile)
        put_shares(r.g, pl.multiple_of(96 * (tile // 3), 32), dest, tn(r.low[...], r.act[:, cols]))
        run_at(tile, "grad_up")
        return carry

    lax.fori_loop(0, 12, grad_up, 0)
    for tile in range(3):
        cols = slice(256 * tile, 256 * tile + 256)
        r.res[:, cols] = r.res[:, cols] + sum(
            nt(r.act[:, 768 * j : 768 * j + 768], r.pool[0, j // 2, j % 2, cols, :])
            for j in range(4)
        )
    for block in range(4):
        rows = slice(64 * block, 64 * block + 64)
        given, hat = r.res[rows, :], r.hat[rows, :]
        sums[0] = sums[0] + jnp.sum(given * hat, axis=0, keepdims=True)
        sums[1] = sums[1] + jnp.sum(given, axis=0, keepdims=True)
        dres = norm_back(given, hat, r.scale[rows, 0:1], gain1)
        r.res[rows, :] = dres
        r.dlow[rows, :] = dres.astype(BF)
    for row in range(4):
        r.sm[0, 4 + row : 5 + row, :] = sums[row]
    run_plan("norm")
    for tile in range(3):
        cols = slice(256 * tile, 256 * tile + 256)
        put_shares(r.pool, 0, cols, tn(r.att[...], r.dlow[:, cols]))
    run_plan("out")
    for tile in range(3):
        cols = slice(256 * tile, 256 * tile + 256)
        r.att[:, cols] = nt(r.dlow[...], r.wo[cols, :]).astype(BF)
    run_plan("datt")

    def attend_back(pair, carry):
        attend_pair_back(pair, r)
        run_at(pair, "pairs")
        return carry

    lax.fori_loop(0, PAIRS, attend_back, 0)
    for tile in range(3):
        cols = slice(256 * tile, 256 * tile + 256)
        put_shares(r.pool, 192, cols, tn(r.x[0:256, :], r.q[:, cols]))
    run_plan("query")
    for tile in range(3):
        cols = slice(256 * tile, 256 * tile + 256)
        put_shares(r.pool, 288, cols, tn(r.x[...], r.k[:, cols]))
    run_plan("key")
    for tile in range(3):
        cols = slice(256 * tile, 256 * tile + 256)
        put_shares(r.pool, 384, cols, tn(r.x[...], r.v[:, cols]))
    run_plan("value")

    for tile in range(3):
        cols = slice(256 * tile, 256 * tile + 256)
        tail = nt(r.k[...], r.wk[cols, :]) + nt(r.v[...], r.wv[cols, :])
        r.relq[256:512, cols] = tail[256:512].astype(BF)
        r.relq[0:256, cols] = (
            tail[0:256] + r.res[:, cols] + nt(r.q[...], r.wq[cols, :])
        ).astype(BF)
    net.post("dx", "dx", 0, lambda: (r.relq.at[256:512, 0:768], r.dxr, pair))
    run_plan("input")
    net.came("dx", 0, lambda: (r.relq.at[256:512, 0:768], r.dxr, pair))
    r.din[...] = (r.relq[0:256, 0:768].astype(F32) + r.dxr[...].astype(F32)).astype(BF)
    give_back("d", r.din, r.input_grad)
    pl.when(own)(lambda: store("din", lambda: r.din.at[0:64], lambda: r.input_grad.at[micro, half]))
    run_plan("dxdone")
    run_plan("tail")
    if reduce:
        store("small", lambda: r.sm.at[5], lambda: r.small)

        @pl.when(is_end)
        def _():
            for u in range(len(CHUNKS)):
                net.got("z3%d" % u)
                kept(u).start()
    else:
        store("small", lambda: r.sm.at[0], lambda: r.small)
        store("share", lambda: r.g, lambda: r.share.at[0])
        last = pltpu.make_async_copy(r.pool, r.share.at[1], r.load_sem.at[0])
        last.start()
        last.wait()
    given_back("o", r.hidden_out)
    given_back("d", r.input_grad)
    stored("small")
    if reduce:
        for u in range(len(CHUNKS)):
            kept(u).wait()
    else:
        stored("share")

    @pl.when(own)
    def _():
        stored("hid")
        stored("din")
        net.posted("own")

    pl.when(far)(lambda: net.posted("far"))
    net.posted("all")
    net.finish("all")
    pl.when(is_end)(lambda: net.finish("end"))
    pl.when(is_mid)(lambda: net.finish("mid"))


PLAN = {
    "down0": ((C, 0),),
    "down1": ((C, 1),),
    "down2": ((C, 2), (F, 0),),
    "up_back": {
        1: ((F, 1),),
    },
    "grad_up": {
        2: ((C, 3),),
        3: ((S, 0),),
        5: ((C, 4),),
        6: ((F, 2),),
        8: ((C, 5),),
        11: ((C, 6),),
    },
    "norm": ((V, 0),),
    "out": ((C, 7), (S, 1), (T, 0),),
    "datt": ((F, 3),),
    "pairs": {
        0: ((V, 1),),
        1: ((S, 2), (T, 1),),
        2: ((F, 4),),
        3: ((M, 0), (S, 3), (T, 2), (F, 5),),
        4: ((M, 1), (S, 4), (V, 2),),
        5: ((C, 8), (N, 0), (T, 3),),
    },
    "query": ((C, 9), (F, 6), (M, 2),),
    "key": ((C, 10), (T, 4), (S, 5), (F, 8), (N, 1),),
    "value": ((C, 11), (C, 12), (M, 3), (V, 3),),
    "input": ((M, 4), (T, 5), (N, 2), (F, 7), (S, 6),),
    "dxdone": (
        (N, 4), (N, 3), (S, 8), (S, 7), (M, 5), (F, 9), (T, 6), (F, 10), (T, 7), (T, 8),
        (M, 6), (N, 5),
    ),
    "tail": (
        (M, 7), (S, 9), (S, 10), (N, 6), (M, 8), (T, 9), (F, 11), (V, 4), (F, 12), (T, 10),
        (N, 7), (M, 9), (S, 11), (N, 8), (T, 11), (M, 10), (S, 12), (T, 12), (N, 9), (M, 11),
        (N, 10), (M, 12), (N, 11), (N, 12), (V, 5),
    ),
}


def scratch(reduce):
    shapes = [
        ("x", (512, 768), BF),
        ("facts", (8, 128), jnp.int32),
        ("meta", (4, 8, 128), jnp.int32),
        ("cot", (256, 768), BF),
        ("vectors", (8, 768), F32),
        ("wq", (768, 768), BF),
        ("wk", (768, 768), BF),
        ("wv", (768, 768), BF),
        ("wo", (768, 768), BF),
        ("wr", (768, 768), BF),
        ("pool", (2, 2, 2, 768, 768), BF),
        ("g", (2, 2, 2, 768, 768), BF),
        ("sine", (256, 384), F32),
        ("cosine", (256, 384), F32),
        ("feat", (512, 896), BF),
        ("q", (256, 768), BF),
        ("k", (512, 768), BF),
        ("v", (512, 768), BF),
        ("att", (256, 768), BF),
        ("relq", (512, 896), BF),
        ("score", (512, 512), F32),
        ("dlog", (512, 512), BF),
        ("probs", (PAIRS, 512, 512), BF),
        ("res", (256, 768), F32),
        ("hat", (256, 768), F32),
        ("scale", (256, 128), F32),
        ("low", (256, 768), BF),
        ("act", (256, 3072), BF),
        ("dlow", (256, 768), BF),
        ("out", (256, 768), BF),
        ("dxr", (256, 768), BF),
        ("din", (256, 768), BF),
        ("sm", (6, 8, 768), F32),
    ]
    if reduce:
        shapes += [("r1_%d" % u, (2, 2, c[2], 768), BF) for u, c in enumerate(CHUNKS)]
        shapes += [
            ("ra", (2, 624, 768), BF),
            ("rb", (2, 624, 768), BF),
            ("ra2", (624, 768), BF),
            ("rb2", (624, 768), BF),
            ("zr", (1248, 768), BF),
            ("za", (1248, 768), BF),
            ("sums", (1248, 768), BF),
            ("smr", (5, 8, 768), F32),
        ]
    return shapes


def layer(lengths, hidden_in, boxes, cotangent, vectors, weights, reduce):
    hi, lo = trig_tables(QUARTER)
    any_space = pl.BlockSpec(memory_space=pl.ANY)
    vmem = pl.BlockSpec(memory_space=pltpu.VMEM)
    ins = (
        ("lengths", lengths.reshape(-1), pl.BlockSpec(memory_space=pltpu.SMEM)),
        ("hidden_in", hidden_in, any_space),
        ("cotangent", cotangent, any_space),
        ("boxes", boxes, vmem),
        ("hi", jnp.asarray(hi), vmem),
        ("lo", jnp.asarray(lo), vmem),
    )
    ins += tuple(("vector%d" % i, v, vmem) for i, v in enumerate(vectors))
    ins += tuple((name, w, any_space) for name, w in weights)
    outs = (
        ("hidden_out", (2, 128, 768), BF),
        ("input_grad", (2, 128, 768), BF),
        ("share", (1248, 768) if reduce else (2, 2, 2, 2, 768, 768), BF),
        ("small", (8, 768), F32),
    )
    shapes = scratch(reduce)
    sems = ("send_sem", "recv_sem", "post_sem", "load_sem", "store_sem", "keep_sem")
    names = tuple(i[0] for i in ins) + tuple(o[0] for o in outs)
    names += tuple(s[0] for s in shapes) + sems
    dma = pltpu.SemaphoreType.DMA
    return pl.pallas_call(
        functools.partial(layer_kernel, names, reduce),
        out_shape=[jax.ShapeDtypeStruct(o[1], o[2]) for o in outs],
        in_specs=[i[2] for i in ins],
        out_specs=[any_space] * len(outs),
        scratch_shapes=[pltpu.VMEM(s[1], s[2]) for s in shapes]
        + [dma((len(i),)) for i in (SENDS, SENDS, POSTS, LOADS, STORES, CHUNKS)],
        compiler_params=pltpu.CompilerParams(
            vmem_limit_bytes=VMEM_LIMIT, collective_id=0, has_side_effects=True
        ),
        name="layer",
    )(*[i[1] for i in ins])


def finish_kernel(share, small, hid, din, hidden, dinput, dq, dk, dv, dout, drel, dup, *rest):
    dbup, ddown, vectors = rest[0], rest[1], rest[2:]
    hidden[...] = hid[...]
    dinput[...] = din[...]
    for j in range(4):
        dup[:, 768 * j : 768 * j + 768] = share[96 * j : 96 * j + 96, :].astype(F32)
    ddown[...] = share[384:768, :].astype(F32)
    for i, ref in enumerate((dout, drel, dq, dk, dv)):
        ref[...] = share[768 + 96 * i : 864 + 96 * i, :].astype(F32)
    dp = lax.axis_index("dp")
    row = small[pl.ds(dp // 2, 1), :]
    dbup[...] = jnp.where(dp % 2 == 0, row[:, 0:384], row[:, 384:768]).reshape(384)
    turned = pltpu.roll(small[...], lax.rem(768 - 96 * dp, 768), 1)
    for i, ref in enumerate(vectors):
        ref[...] = turned[4 + i : 5 + i, 0:96].reshape(96)


def finish(share, small, hidden, dinput):
    shapes = [(96, 768)] * 5 + [(96, 3072), (384,), (384, 768)] + [(96,)] * 4
    low = jax.ShapeDtypeStruct(hidden.shape, BF)
    return pl.pallas_call(
        finish_kernel,
        out_shape=[low, low] + [jax.ShapeDtypeStruct(s, F32) for s in shapes],
        name="finish",
    )(share, small, hidden, dinput)


def finish_any(g, small):
    order = g.transpose(0, 2, 3, 1, 4, 5).reshape(2, 8, 768, 768)

    def weight(which, base):
        return order[which, :, base : base + 96].reshape(768, 768)

    up = jnp.concatenate([weight(0, 96 * j) for j in range(4)], axis=1)
    down = order[0, :, 384:768].reshape(3072, 768)
    full = [weight(1, base) for base in (192, 288, 384, 0, 96)] + [up, down]
    grads = [
        lax.psum(lax.psum_scatter(w, "dp", scatter_dimension=0, tiled=True), "seq").astype(F32)
        for w in full
    ]
    small = lax.psum(small, ("dp", "seq"))
    dp, count = lax.axis_index("dp"), lax.axis_size("dp")

    def own_part(vector):
        size = vector.shape[0] // count
        return lax.dynamic_slice_in_dim(vector, dp * size, size)

    parts = [own_part(small[4 + i]) for i in range(4)]
    return grads[:6] + [own_part(small[0:4].reshape(-1)), grads[6]] + parts


def shards(
    hidden_in,
    boxes,
    lengths,
    w_query,
    w_key,
    w_value,
    w_out,
    w_rel,
    w_up,
    b_up,
    w_down,
    gain_attn,
    bias_attn,
    gain_ffn,
    bias_ffn,
    cotangent,
):
    vectors = (b_up, gain_attn, bias_attn, gain_ffn, bias_ffn)
    weights = (
        ("w_query", w_query),
        ("w_key", w_key),
        ("w_value", w_value),
        ("w_out", w_out),
        ("w_rel", w_rel),
        ("w_up", w_up),
        ("w_down", w_down),
    )
    reduce = lax.axis_size("dp") == 8
    hidden, dinput, share, small = layer(
        lengths,
        hidden_in[:, 0],
        boxes[:, :, 0],
        cotangent[:, 0],
        vectors,
        weights,
        reduce,
    )
    if reduce:
        hidden, dinput, *rest = finish(share, small, hidden, dinput)
    else:
        rest = finish_any(share, small)
    return (hidden[:, None], dinput[:, None], *rest)


def solution(mesh):
    rows = P(None, "dp", "seq", None)
    placed = (rows, P(None, None, "dp", "seq"), P(None, "dp")) + (P(),) * 12 + (rows,)
    matrix, vector = P("dp", None), P("dp")
    return jax.shard_map(
        shards,
        mesh=mesh,
        in_specs=placed,
        out_specs=(rows, rows) + (matrix,) * 6 + (vector, matrix) + (vector,) * 4,
        check_vma=False,
    )
```

```python
import functools

import jax
import jax.numpy as jnp
import numpy as np
from jax import lax
from jax.experimental import pallas as pl
from jax.experimental.pallas import tpu as pltpu
from jax.sharding import PartitionSpec as P

HEADS = 12
EPS = 1e-05
BF = jnp.bfloat16
F32 = jnp.float32
PAIRS = HEADS // 2
VMEM_LIMIT = 67043328
QUARTER = 192


def nn(a, b):
    return lax.dot_general(a, b, (((1,), (0,)), ((), ())), preferred_element_type=F32)


def nt(a, b):
    return lax.dot_general(a, b, (((1,), (1,)), ((), ())), preferred_element_type=F32)


def tn(a, b):
    return lax.dot_general(a, b, (((0,), (0,)), ((), ())), preferred_element_type=F32)


def trig_tables(quarter):
    freq = 10000.0 ** (-np.arange(quarter) / quarter)
    tables = []
    for step in (32.0, 1.0):
        angle = step * np.arange(32)[:, None] * freq[None, :]
        rest = np.concatenate([np.sin(angle), np.cos(angle)], axis=1).astype(np.float32)
        parts = []
        for _ in range(3):
            part = rest.astype(BF)
            parts.append(part)
            rest = rest - part.astype(np.float32)
        tables.append(np.concatenate(parts, axis=0))
    return tables


def features(slot, c, micro, r):
    half = 2 * QUARTER
    iota = lax.broadcasted_iota(jnp.int32, (32, 128), 0)
    hi_tab, lo_tab = r.hi[...], r.lo[...]
    block = pltpu.roll(r.meta[slot], 64 * c, 1)
    sines, cosines = [], []
    for axis in range(2):
        where = jnp.where(micro == 0, block[axis : axis + 1], block[2 + axis : 3 + axis])
        pick_hi = (iota == lax.shift_right_logical(where, 5)).astype(F32).astype(BF)
        pick_lo = (iota == (where & 31)).astype(F32).astype(BF)
        hi = tn(jnp.concatenate([pick_hi] * 3, axis=0), hi_tab)
        lo = tn(jnp.concatenate([pick_lo] * 3, axis=0), lo_tab)
        sin_hi, cos_hi = hi[:, :QUARTER], hi[:, QUARTER:]
        sin_lo, cos_lo = lo[:, :QUARTER], lo[:, QUARTER:]
        sines.append(sin_hi * cos_lo + cos_hi * sin_lo)
        cosines.append(cos_hi * cos_lo - sin_hi * sin_lo)
    sine = jnp.concatenate(sines, axis=1)
    cosine = jnp.concatenate(cosines, axis=1)
    for part in range(2):
        mine = slice(64 * part, 64 * part + 64)
        rows = pl.ds(256 * part + 64 * slot, 64)
        r.feat[rows, 0:half] = cosine[mine].astype(BF)
        r.feat[rows, half : 2 * half] = sine[mine].astype(BF)
    rows = pl.ds(64 * slot, 64)
    r.sine[rows, :] = sine[0:64]
    r.cosine[rows, :] = cosine[0:64]


def head_stack(pair):
    first = lax.broadcasted_iota(jnp.int32, pair.shape, 1) < 64
    zero = jnp.zeros_like(pair)
    return jnp.concatenate([jnp.where(first, pair, zero), jnp.where(first, zero, pair)], axis=0)


def head_join(stack):
    half = stack.shape[0] // 2
    first = lax.broadcasted_iota(jnp.int32, (half, 128), 1) < 64
    return jnp.where(first, stack[:half], stack[half:])


def attend_pair(pair, live, r):
    cols = pl.ds(pl.multiple_of(128 * pair, 128), 128)
    stack = head_stack(r.q[:, cols].astype(F32) * 0.125).astype(BF)
    for head in range(2):
        rows = slice(256 * head, 256 * head + 256)
        left = nt(stack[rows], r.wr[0:384, cols])
        right = nt(stack[rows], r.wr[384:768, cols])
        sin, cos = r.sine[...], r.cosine[...]
        r.relq[rows, 0:384] = (left * sin + right * cos).astype(BF)
        r.relq[rows, 384:768] = (right * sin - left * cos).astype(BF)
    r.relq[:, 768:896] = stack
    r.feat[:, 768:896] = r.k[:, cols]
    r.score[...] = nt(r.relq[...], r.feat[...])
    for block in range(8):
        rows = pl.ds(64 * block, 64)
        score = jnp.where(live, r.score[rows, :], -1e30)
        top = jnp.max(score, axis=-1, keepdims=True)
        weight = jnp.exp(score - top)
        total = jnp.sum(weight, axis=-1, keepdims=True)
        r.probs[pair, rows, :] = (weight * (1.0 / total)).astype(BF)
    r.att[:, cols] = head_join(nn(r.probs[pair], r.v[:, cols])).astype(BF)


def attend_pair_back(pair, r):
    cols = pl.ds(pl.multiple_of(128 * pair, 128), 128)
    given = head_stack(r.att[:, cols].astype(F32)).astype(BF)
    stack = head_stack(r.q[:, cols].astype(F32)).astype(BF)
    r.score[...] = nt(given, r.v[:, cols])
    for block in range(8):
        rows = pl.ds(64 * block, 64)
        prob = r.probs[pair, rows, :].astype(F32)
        push = prob * r.score[rows, :]
        mean = jnp.sum(push, axis=-1, keepdims=True)
        r.dlog[rows, :] = ((push - prob * mean) * 0.125).astype(BF)
    r.feat[:, 768:896] = r.k[:, cols]
    r.v[:, cols] = tn(r.probs[pair], given).astype(BF)
    r.k[:, cols] = tn(r.dlog[...], stack).astype(BF)
    for head in range(2):
        rows = slice(256 * head, 256 * head + 256)
        first = nn(r.dlog[rows, :], r.feat[:, 0:384])
        second = nn(r.dlog[rows, :], r.feat[:, 384:768])
        sin, cos = r.sine[...], r.cosine[...]
        r.relq[rows, 0:384] = (first * sin - second * cos).astype(BF)
        r.relq[rows, 384:768] = (first * cos + second * sin).astype(BF)
    dq = nn(r.dlog[...], r.feat[:, 768:896]) + nn(r.relq[:, 0:768], r.wr[:, cols])
    r.q[:, cols] = head_join(dq).astype(BF)
    part = tn(r.relq[:, 0:768], stack).astype(BF)
    for piece, share in enumerate((0, 1, 4, 5, 2, 3, 6, 7)):
        c, y, x = share % 2, share // 4, share // 2 % 2
        r.pool[c, y, x, 96:192, cols] = part[96 * piece : 96 * piece + 96]


def norm_back(given, hat, scale, gain):
    push = given * gain
    mean = jnp.mean(push, axis=-1, keepdims=True)
    lean = jnp.mean(push * hat, axis=-1, keepdims=True)
    return scale * (push - mean - hat * lean)


def put_shares(ref, base, cols, part):
    for share in range(8):
        c, y, x = share % 2, share // 4, share // 2 % 2
        ref[c, y, x, pl.ds(base, 96), cols] = part[96 * share : 96 * share + 96].astype(BF)


class Refs:
    pass


CHUNKS = (
    ("g", 384, 128, 384),
    ("g", 512, 128, 512),
    ("g", 640, 128, 640),
    ("g", 0, 96, 0),
    ("g", 96, 96, 96),
    ("g", 192, 96, 192),
    ("g", 288, 96, 288),
    ("pool", 0, 96, 768),
    ("pool", 96, 96, 864),
    ("pool", 192, 96, 960),
    ("pool", 288, 96, 1056),
    ("pool", 384, 64, 1152),
    ("pool", 448, 32, 1216),
)
C, F, S, T, M, N, V = range(7)
STAGES = ("core", "xa", "xb", "ya", "yb", "z1", "z2", "z3")
BLOCKS = ("x", "m", "c", "f", "o", "d")
SENDS = tuple(k + str(i) for k in BLOCKS for i in range(4)) + ("dx0",)
SENDS += tuple("s%d" % i for i in range(5))
SENDS += tuple("%s%d" % (s, u) for u in range(len(CHUNKS)) for s in STAGES)
LOADS = ("x", "x2", "cot", "key", "value", "query", "out")
LOADS += tuple("rel%d" % i for i in range(4)) + tuple("up%d" % i for i in range(4))
LOADS += tuple("down%d" % i for i in range(4))
STORES = ("hid", "din", "share", "small")
POSTS = tuple(k + i for k in "xmc" for i in ("a0", "a1", "b0", "b1", "p"))
POSTS += tuple(k + str(i) for k in "fod" for i in range(4)) + ("dx",)


class Net:
    def __init__(self, r):
        self.r = r
        self.made = {}
        self.order = {"all": [], "end": [], "mid": []}
        self.posts = {"all": [], "own": [], "far": []}

    def _of(self, name):
        i = SENDS.index(name)
        src, dst, peer = self.made[name]()
        return pltpu.make_async_remote_copy(
            src_ref=src,
            dst_ref=dst,
            send_sem=self.r.send_sem.at[i],
            recv_sem=self.r.recv_sem.at[i],
            device_id=peer,
            device_id_type=pl.DeviceIdType.MESH,
        )

    def start(self, name, make, role="all"):
        self.made[name] = make
        self._of(name).start()
        self.order[role].append(name)

    def got(self, name):
        self._of(name).wait_recv()

    def _post(self, name, src, dst, at, peer):
        return pltpu.make_async_remote_copy(
            src_ref=src,
            dst_ref=dst,
            send_sem=self.r.post_sem.at[POSTS.index(name)],
            recv_sem=self.r.recv_sem.at[at],
            device_id=peer,
            device_id_type=pl.DeviceIdType.MESH,
        )

    def post(self, name, kind, index, make, role="all"):
        src, dst, peer = make()
        self._post(name, src, dst, SENDS.index(kind + "0") + index, peer).start()
        self.posts[role].append((name, kind, index, make))

    def came(self, kind, index, make):
        src, dst, peer = make()
        self._post(POSTS[0], src, dst, SENDS.index(kind + "0") + index, peer).wait_recv()

    def finish(self, role):
        for name in self.order[role]:
            self._of(name).wait_send()

    def posted(self, role):
        for name, kind, index, make in self.posts[role]:
            src, dst, peer = make()
            self._post(name, src, dst, SENDS.index(kind + "0") + index, peer).wait_send()


def add_rows(count, body):
    size = 48 if count % 48 == 0 else 32 if count % 32 == 0 else 16

    def step(i, carry):
        body(pl.multiple_of(size * i, 16), size)
        return carry

    lax.fori_loop(0, count // size, step, 0)


def total(*terms):
    out = terms[0].astype(F32)
    for term in terms[1:]:
        out = out + term.astype(F32)
    return out.astype(BF)


class Reduction:
    def __init__(self, r, net, dp, z):
        self.r, self.net = r, net
        self.c, self.x, self.y = dp % 2, dp // 2 % 2, dp // 4
        self.pc = (dp + 1 - 2 * self.c, z)
        self.px = (dp + 2 - 4 * self.x, z)
        self.py = (dp + 4 - 8 * self.y, z)
        self.pz1 = (dp, z + 1 - 2 * (z % 2))
        self.pz2 = (dp, (z + 2) % 4)
        self.across = (dp, 3 - z)

    def parts(self, u):
        name, base, rows, out = CHUNKS[u]
        return getattr(self.r, name), base, rows // 2, out, self.r.r1[u], out // 2

    def core(self, u):
        g, base, half, _, r1, _ = self.parts(u)
        self.net.start(
            "core%d" % u, lambda: (g.at[1 - self.c, :, :, pl.ds(base, 2 * half)], r1, self.pc)
        )

    def first(self, u):
        g, base, half, _, r1, at = self.parts(u)
        c, x, y = self.c, self.x, self.y
        self.net.got("core%d" % u)

        def add(i, size):
            for k in range(2):
                rows, own = pl.ds(base + i, size), pl.ds(i, size)
                g[c, k, 1 - x, rows] = total(g[c, k, 1 - x, rows], r1[k, 1 - x, own])
                rows, own = pl.ds(base + half + i, size), pl.ds(half + i, size)
                g[c, 1 - y, k, rows] = total(g[c, 1 - y, k, rows], r1[1 - y, k, own])

        add_rows(half, add)
        a, b, to = pl.ds(base, half), pl.ds(base + half, half), pl.ds(at, half)
        self.net.start("xa%d" % u, lambda: (g.at[c, :, 1 - x, a], self.r.ra.at[:, to], self.px))
        self.net.start("yb%d" % u, lambda: (g.at[c, 1 - y, :, b], self.r.rb.at[:, to], self.py))

    def second(self, u):
        g, base, half, _, r1, at = self.parts(u)
        c, x, y = self.c, self.x, self.y
        ra, rb = self.r.ra, self.r.rb
        self.net.got("xa%d" % u)
        self.net.got("yb%d" % u)

        def add(i, size):
            came = pl.ds(at + i, size)
            rows, own = pl.ds(base + i, size), pl.ds(i, size)
            g[c, 1 - y, x, rows] = total(g[c, 1 - y, x, rows], r1[1 - y, x, own], ra[1 - y, came])
            rows, own = pl.ds(base + half + i, size), pl.ds(half + i, size)
            g[c, y, 1 - x, rows] = total(g[c, y, 1 - x, rows], r1[y, 1 - x, own], rb[1 - x, came])

        add_rows(half, add)
        a, b, to = pl.ds(base, half), pl.ds(base + half, half), pl.ds(at, half)
        self.net.start("ya%d" % u, lambda: (g.at[c, 1 - y, x, a], self.r.ra2.at[to], self.py))
        self.net.start("xb%d" % u, lambda: (g.at[c, y, 1 - x, b], self.r.rb2.at[to], self.px))

    def third(self, u, mid):
        g, base, half, out, r1, at = self.parts(u)
        c, x, y = self.c, self.x, self.y
        ra, rb, ra2, rb2, zr = self.r.ra, self.r.rb, self.r.ra2, self.r.rb2, self.r.zr
        self.net.got("ya%d" % u)
        self.net.got("xb%d" % u)
        if mid:
            self.net.got("z1%d" % u)

        def add(i, size):
            came = pl.ds(at + i, size)
            rows, own = pl.ds(base + i, size), pl.ds(i, size)
            more = (zr[pl.ds(out + i, size)],) if mid else ()
            g[c, y, x, rows] = total(
                g[c, y, x, rows], r1[y, x, own], ra[y, came], ra2[came], *more
            )
            rows, own = pl.ds(base + half + i, size), pl.ds(half + i, size)
            more = (zr[pl.ds(out + half + i, size)],) if mid else ()
            g[c, y, x, rows] = total(
                g[c, y, x, rows], r1[y, x, own], rb[x, came], rb2[came], *more
            )

        add_rows(half, add)
        rows, to = pl.ds(base, 2 * half), pl.ds(out, 2 * half)
        if mid:
            make = lambda: (g.at[c, y, x, rows], self.r.za.at[to], self.across)
            self.net.start("z2%d" % u, make, "mid")
        else:
            make = lambda: (g.at[c, y, x, rows], self.r.zr.at[to], self.pz1)
            self.net.start("z1%d" % u, make, "end")

    def fourth(self, u):
        g, base, half, out, _, _ = self.parts(u)
        c, x, y = self.c, self.x, self.y
        self.net.got("z2%d" % u)

        def add(i, size):
            rows, to = pl.ds(base + i, size), pl.ds(out + i, size)
            self.r.sums[to] = total(g[c, y, x, rows], self.r.za[to])

        add_rows(2 * half, add)
        to = pl.ds(out, 2 * half)
        self.net.start("z3%d" % u, lambda: (self.r.sums.at[to], self.r.sums.at[to], self.pz1), "mid")

    def small(self, i):
        if i:
            self.net.got("s%d" % (i - 1))
            self.r.sm[i] = self.r.sm[i - 1] + self.r.smr[i - 1]
        if i < 5:
            peer = (self.pc, self.px, self.py, self.pz1, self.pz2)[i]
            self.net.start("s%d" % i, lambda: (self.r.sm.at[i], self.r.smr.at[i], peer))


def layer_kernel(names, reduce, *refs):
    r = Refs()
    for name, ref in zip(names, refs):
        setattr(r, name, ref)
    dp, z = lax.axis_index("dp"), lax.axis_index("seq")
    micro, c = z // 2, dp % 2
    is_mid = lax.rem(z, 3) > 0
    is_end = lax.rem(z, 3) == 0
    own = c == z % 2
    far = c != z % 2
    base = jnp.where(own, 0, 1)
    column = dp - c
    source = column + z % 2
    pair = (dp + 1 - 2 * c, z)
    half = pl.ds(pl.multiple_of(64 * c, 64), 64)
    other = pl.ds(pl.multiple_of(64 - 64 * c, 64), 64)
    net = Net(r)
    red = None
    if reduce:
        r.r1 = tuple(getattr(r, "r1_%d" % u) for u in range(len(CHUNKS)))
        red = Reduction(r, net, dp, z)

    def kept(u):
        rows = pl.ds(CHUNKS[u][3], CHUNKS[u][2])
        return pltpu.make_async_copy(r.sums.at[rows], r.share.at[rows], r.keep_sem.at[u])

    def whole(u):
        red.fourth(u)
        kept(u).start()

    def run(*steps):
        if not reduce:
            return
        for kind, u in steps:
            if kind == C:
                red.core(u)
            elif kind == F:
                red.first(u)
            elif kind == S:
                red.second(u)
            elif kind == T:
                pl.when(is_end)(functools.partial(red.third, u, False))
            elif kind == M:
                pl.when(is_mid)(functools.partial(red.third, u, True))
            elif kind == N:
                pl.when(is_mid)(functools.partial(whole, u))
            else:
                red.small(u)

    def run_plan(place):
        run(*PLAN.get(place, ()))

    def run_at(index, place):
        for at, steps in PLAN[place].items():
            pl.when(index == at)(functools.partial(run, *steps))

    loads = {}

    def load(name, src, dst):
        loads[name] = lambda: (src(), dst(), r.load_sem.at[LOADS.index(name)])
        pltpu.make_async_copy(*loads[name]()).start()

    def loaded(name):
        pltpu.make_async_copy(*loads[name]()).wait()

    load("key", lambda: r.w_key, lambda: r.wk)
    load("value", lambda: r.w_value, lambda: r.wv)
    load("query", lambda: r.w_query, lambda: r.wq)

    greet = [pair] + [(column + h, (z + i) % 4) for i in range(1, 4) for h in range(2)]
    greet += [red.px, red.py] if reduce else []
    line = lax.broadcasted_iota(jnp.int32, (8, 128), 0)
    wide = [r.boxes[axis, m : m + 1, :] for m in range(2) for axis in range(2)]
    wide = jnp.concatenate(wide * 2, axis=0)
    wide = jnp.where(line == 4, r.lengths[0], jnp.where(line == 5, r.lengths[1], wide))
    r.facts[...] = wide
    barrier = pltpu.get_barrier_semaphore()
    for peer in greet:
        pl.semaphore_signal(barrier, 1, device_id=peer, device_id_type=pl.DeviceIdType.MESH)
    pl.semaphore_wait(barrier, len(greet))

    def spread(kind, src, dst):
        for first in (False, True):
            step = base if first else base + 2
            to = (z + 4 - step) % 4
            rows = pl.ds(pl.multiple_of(64 * step, 64), 64)
            for h in range(2):
                def make(h=h, to=to, rows=rows, step=step):
                    return src(to // 2, pl.ds(64 * h, 64)), dst(step, rows), (column + h, to)

                name = kind + ("a" if first else "b") + str(h)
                if first:
                    pl.when(far)(functools.partial(net.post, name, kind, step, make, "far"))
                else:
                    net.post(name, kind, step, make)

    def here(kind, src, dst):
        make = lambda: (src(micro, other), dst(0, pl.ds(0, 64)), pair)
        net.post(kind + "p", kind, 0, make, "own")

    hidden = lambda m, rows: r.hidden_in.at[m, rows]
    grads = lambda m, rows: r.cotangent.at[m, rows]

    x_to = lambda step, rows: r.x.at[rows]
    m_to = lambda step, rows: r.meta.at[step]
    c_to = lambda step, rows: r.cot.at[rows]
    spread("m", lambda m, rows: r.facts, m_to)
    spread("x", hidden, x_to)

    @pl.when(own)
    def _():
        here("m", lambda m, rows: r.facts, m_to)
        here("x", hidden, x_to)
        make = lambda: (hidden(micro, half), r.x.at[256:320], pair)
        net.post("f0", "f", 0, make, "own")
        load("x", lambda: hidden(micro, half), lambda: r.x.at[0:64])
        load("x2", lambda: hidden(micro, other), lambda: r.x.at[256:320])
        r.meta[0] = r.facts[...]

    for i, (dst, src) in enumerate(((0, 0), (192, 384), (384, 192), (576, 576))):
        load("rel%d" % i, lambda src=src, dst=dst: r.w_rel.at[src : src + 192], lambda src=src, dst=dst: r.wr.at[dst : dst + 192])
    load("out", lambda: r.w_out, lambda: r.wo)
    for j in range(4):
        load("up%d" % j, lambda j=j: r.w_up.at[:, 768 * j : 768 * j + 768], lambda j=j: r.pool.at[0, j // 2, j % 2])
    for j in range(4):
        load("down%d" % j, lambda j=j: r.w_down.at[768 * j : 768 * j + 768], lambda j=j: r.pool.at[1, j // 2, j % 2])
    pl.when(own)(lambda: load("cot", lambda: grads(micro, half), lambda: r.cot.at[0:64]))

    def project(start, stop):
        rows = slice(start, stop)
        for tile in range(3):
            cols = slice(256 * tile, 256 * tile + 256)
            r.k[rows, cols] = nn(r.x[rows, :], r.wk[:, cols]).astype(BF)
            r.v[rows, cols] = nn(r.x[rows, :], r.wv[:, cols]).astype(BF)
            if stop <= 256:
                r.q[rows, cols] = nn(r.x[rows, :], r.wq[:, cols]).astype(BF)

    for j in range(4):
        r.vectors[j : j + 1, :] = r.vector0[768 * j : 768 * j + 768].astype(F32).reshape(1, 768)
        row = getattr(r, "vector%d" % (j + 1))[...]
        r.vectors[4 + j : 5 + j, :] = row.astype(F32).reshape(1, 768)
    x_size = lambda: (hidden(0, pl.ds(0, 64)), r.x.at[0:64], pair)
    m_size = lambda: (r.facts, r.meta.at[0], pair)
    pl.when(far)(lambda: net.came("m", 0, m_size))
    features(0, c, micro, r)
    for slot in (1, 3, 2):
        net.came("m", slot, m_size)
        features(slot, c, micro, r)
    loaded("key")
    loaded("value")
    loaded("query")

    @pl.when(own)
    def _():
        loaded("x")
        loaded("x2")

    @pl.when(far)
    def _():
        net.came("x", 0, x_size)
        net.came("f", 0, x_size)

    project(0, 64)
    project(256, 320)
    for i in range(4):
        loaded("rel%d" % i)
    for slot in (1, 3, 2):
        net.came("x", slot, x_size)
        mine, theirs = slice(64 * slot, 64 * slot + 64), slice(256 + 64 * slot, 320 + 64 * slot)
        make = lambda mine=mine, theirs=theirs: (r.x.at[mine], r.x.at[theirs], pair)
        net.post("f%d" % slot, "f", slot, make)
    spread("c", grads, c_to)
    pl.when(own)(lambda: here("c", grads, c_to))
    project(64, 256)
    for slot in (1, 3, 2):
        net.came("f", slot, x_size)
    project(320, 512)

    place = lax.broadcasted_iota(jnp.int32, (1, 512), 1)
    turn = lax.shift_right_logical(place, 8)
    token = 128 * ((z + (lax.shift_right_logical(place, 6) & 3)) & 3) + (place & 63)
    token = token + 64 * ((c + turn) & 1)
    known = r.meta[1]
    length = jnp.where(micro == 0, known[4:5], known[5:6])
    live = token < jnp.concatenate([length] * 4, axis=1)

    def attend(pair, carry):
        attend_pair(pair, live, r)
        return carry

    lax.fori_loop(0, PAIRS, attend, 0, unroll=6)

    loaded("out")
    for tile in range(3):
        cols = slice(256 * tile, 256 * tile + 256)
        r.res[:, cols] = r.x[0:256, cols].astype(F32) + nn(r.att[...], r.wo[:, cols])

    gain1, bias1, gain2, bias2 = [r.vectors[4 + i : 5 + i, :] for i in range(4)]
    for block in range(4):
        rows = slice(64 * block, 64 * block + 64)
        res = r.res[rows, :]
        center = res - jnp.mean(res, axis=-1, keepdims=True)
        scale = lax.rsqrt(jnp.mean(center * center, axis=-1, keepdims=True) + EPS)
        hat = center * scale
        r.hat[rows, :] = hat
        r.scale[rows, :] = jnp.broadcast_to(scale, (64, 128))
        normed = hat * gain1 + bias1
        r.res[rows, :] = normed
        r.low[rows, :] = normed.astype(BF)

    for j in range(4):
        loaded("up%d" % j)
    for j in range(4):
        loaded("down%d" % j)

    def up_tile(tile):
        j = tile // 3
        return j // 2, j % 2, pl.ds(pl.multiple_of(256 * (tile % 3), 256), 256)

    def up(tile, carry):
        cols = pl.ds(pl.multiple_of(256 * tile, 256), 256)
        y, x, part = up_tile(tile)
        bias = r.vectors[pl.ds(tile // 3, 1), part]
        value = nn(r.low[...], r.pool[0, y, x, :, part]) + bias
        below = 0.5 * (1.0 + lax.erf(value * np.float32(np.sqrt(0.5))))
        r.act[:, cols] = (value * below).astype(BF)
        top = value.astype(BF)
        r.g[0, y, x, 0:256, part] = top
        r.g[1, y, x, 0:256, part] = (value - top.astype(F32)).astype(BF)
        return carry

    lax.fori_loop(0, 12, up, 0, unroll=12)
    for tile in range(3):
        cols = slice(256 * tile, 256 * tile + 256)
        r.res[:, cols] = r.res[:, cols] + sum(
            nn(r.act[:, 768 * j : 768 * j + 768], r.pool[1, j // 2, j % 2, :, cols])
            for j in range(4)
        )

    c_size = lambda: (grads(0, pl.ds(0, 64)), r.cot.at[0:64], pair)
    pl.when(own)(lambda: loaded("cot"))
    pl.when(far)(lambda: net.came("c", 0, c_size))
    for slot in (1, 2, 3):
        net.came("c", slot, c_size)
    sums = [jnp.zeros((1, 768), F32) for _ in range(4)]
    for block in range(4):
        rows = slice(64 * block, 64 * block + 64)
        res = r.res[rows, :]
        center = res - jnp.mean(res, axis=-1, keepdims=True)
        scale = lax.rsqrt(jnp.mean(center * center, axis=-1, keepdims=True) + EPS)
        hat = center * scale
        r.out[rows, :] = (hat * gain2 + bias2).astype(BF)
        given = r.cot[rows, :].astype(F32)
        sums[2] = sums[2] + jnp.sum(given * hat, axis=0, keepdims=True)
        sums[3] = sums[3] + jnp.sum(given, axis=0, keepdims=True)
        dres = norm_back(given, hat, scale, gain2)
        r.res[rows, :] = dres
        r.dlow[rows, :] = dres.astype(BF)

    def grad_down(offset):
        for quad in range(2):
            shares = range(4 * quad, 4 * quad + 4)
            starts = [384 * share + offset for share in shares]
            left = jnp.concatenate([r.act[:, at : at + 128] for at in starts], axis=1)
            part = tn(left, r.dlow[...]).astype(BF)
            for i, share in enumerate(shares):
                place = (share % 2, share // 4, share // 2 % 2, pl.ds(384 + offset, 128))
                r.g[place] = part[128 * i : 128 * i + 128]

    for third in range(3):
        grad_down(128 * third)
        run_plan("down%d" % third)
    stores = {}

    def store(name, src, dst):
        stores[name] = lambda: (src(), dst(), r.store_sem.at[STORES.index(name)])
        pltpu.make_async_copy(*stores[name]()).start()

    def stored(name):
        pltpu.make_async_copy(*stores[name]()).wait()

    def give_back(kind, src, dst):
        for slot in (3, 1, 2, 0):
            rows = slice(64 * slot, 64 * slot + 64)
            to = (source, (z + slot) % 4)
            make = lambda rows=rows, to=to: (src.at[rows], dst.at[micro, half], to)
            role = "all" if slot else "far"
            post = functools.partial(net.post, kind + str(slot), kind, 2 * micro + c, make, role)
            if slot:
                post()
            else:
                pl.when(far)(post)

    def given_back(kind, dst):
        size = lambda: (r.out.at[0:64], dst.at[0, 0:64], pair)
        for m in range(2):
            for h in range(2):
                local = own & (micro == m) & (c == h)
                pl.when(jnp.logical_not(local))(functools.partial(net.came, kind, 2 * m + h, size))

    give_back("o", r.out, r.hidden_out)
    pl.when(own)(lambda: store("hid", lambda: r.out.at[0:64], lambda: r.hidden_out.at[micro, half]))

    def up_back(tile, carry):
        cols = pl.ds(pl.multiple_of(256 * tile, 256), 256)
        y, x, part = up_tile(tile)
        value = r.g[0, y, x, 0:256, part].astype(F32) + r.g[1, y, x, 0:256, part].astype(F32)
        below = 0.5 * (1.0 + lax.erf(value * np.float32(np.sqrt(0.5))))
        dense = jnp.exp(value * value * -0.5) * np.float32(1.0 / np.sqrt(2.0 * np.pi))
        slope = below + value * dense
        push = nt(r.dlow[...], r.pool[1, y, x, part, :]) * slope
        low = push.astype(BF)
        r.act[:, cols] = low
        r.sm[0, pl.ds(tile // 3, 1), part] = jnp.sum(low.astype(F32), axis=0, keepdims=True)
        run_at(tile, "up_back")
        return carry

    lax.fori_loop(0, 12, up_back, 0)

    def grad_up(tile, carry):
        cols = pl.ds(pl.multiple_of(256 * tile, 256), 256)
        _, _, dest = up_tile(tile)
        put_shares(r.g, pl.multiple_of(96 * (tile // 3), 32), dest, tn(r.low[...], r.act[:, cols]))
        run_at(tile, "grad_up")
        return carry

    lax.fori_loop(0, 12, grad_up, 0)
    for tile in range(3):
        cols = slice(256 * tile, 256 * tile + 256)
        r.res[:, cols] = r.res[:, cols] + sum(
            nt(r.act[:, 768 * j : 768 * j + 768], r.pool[0, j // 2, j % 2, cols, :])
            for j in range(4)
        )
    for block in range(4):
        rows = slice(64 * block, 64 * block + 64)
        given, hat = r.res[rows, :], r.hat[rows, :]
        sums[0] = sums[0] + jnp.sum(given * hat, axis=0, keepdims=True)
        sums[1] = sums[1] + jnp.sum(given, axis=0, keepdims=True)
        dres = norm_back(given, hat, r.scale[rows, 0:1], gain1)
        r.res[rows, :] = dres
        r.dlow[rows, :] = dres.astype(BF)
    for row in range(4):
        r.sm[0, 4 + row : 5 + row, :] = sums[row]
    run_plan("norm")
    for tile in range(3):
        cols = slice(256 * tile, 256 * tile + 256)
        put_shares(r.pool, 0, cols, tn(r.att[...], r.dlow[:, cols]))
    run_plan("out")
    for tile in range(3):
        cols = slice(256 * tile, 256 * tile + 256)
        r.att[:, cols] = nt(r.dlow[...], r.wo[cols, :]).astype(BF)
    run_plan("datt")

    def attend_back(pair, carry):
        attend_pair_back(pair, r)
        run_at(pair, "pairs")
        return carry

    lax.fori_loop(0, PAIRS, attend_back, 0)
    for tile in range(3):
        cols = slice(256 * tile, 256 * tile + 256)
        put_shares(r.pool, 192, cols, tn(r.x[0:256, :], r.q[:, cols]))
    run_plan("query")
    for tile in range(3):
        cols = slice(256 * tile, 256 * tile + 256)
        put_shares(r.pool, 288, cols, tn(r.x[...], r.k[:, cols]))
    run_plan("key")
    for tile in range(3):
        cols = slice(256 * tile, 256 * tile + 256)
        put_shares(r.pool, 384, cols, tn(r.x[...], r.v[:, cols]))
    run_plan("value")

    for tile in range(3):
        cols = slice(256 * tile, 256 * tile + 256)
        tail = nt(r.k[...], r.wk[cols, :]) + nt(r.v[...], r.wv[cols, :])
        r.relq[256:512, cols] = tail[256:512].astype(BF)
        r.relq[0:256, cols] = (
            tail[0:256] + r.res[:, cols] + nt(r.q[...], r.wq[cols, :])
        ).astype(BF)
    net.post("dx", "dx", 0, lambda: (r.relq.at[256:512, 0:768], r.dxr, pair))
    run_plan("input")
    net.came("dx", 0, lambda: (r.relq.at[256:512, 0:768], r.dxr, pair))
    r.din[...] = (r.relq[0:256, 0:768].astype(F32) + r.dxr[...].astype(F32)).astype(BF)
    give_back("d", r.din, r.input_grad)
    pl.when(own)(lambda: store("din", lambda: r.din.at[0:64], lambda: r.input_grad.at[micro, half]))
    run_plan("dxdone")
    run_plan("tail")
    if reduce:
        store("small", lambda: r.sm.at[5], lambda: r.small)

        @pl.when(is_end)
        def _():
            for u in range(len(CHUNKS)):
                net.got("z3%d" % u)
                kept(u).start()
    else:
        store("small", lambda: r.sm.at[0], lambda: r.small)
        store("share", lambda: r.g, lambda: r.share.at[0])
        last = pltpu.make_async_copy(r.pool, r.share.at[1], r.load_sem.at[0])
        last.start()
        last.wait()
    given_back("o", r.hidden_out)
    given_back("d", r.input_grad)
    stored("small")
    if reduce:
        for u in range(len(CHUNKS)):
            kept(u).wait()
    else:
        stored("share")

    @pl.when(own)
    def _():
        stored("hid")
        stored("din")
        net.posted("own")

    pl.when(far)(lambda: net.posted("far"))
    net.posted("all")
    net.finish("all")
    pl.when(is_end)(lambda: net.finish("end"))
    pl.when(is_mid)(lambda: net.finish("mid"))


PLAN = {
    "down0": ((C, 0),),
    "down1": ((C, 1),),
    "down2": ((C, 2), (F, 0),),
    "up_back": {
        1: ((F, 1),),
    },
    "grad_up": {
        2: ((C, 3),),
        3: ((S, 0),),
        5: ((C, 4),),
        6: ((F, 2),),
        8: ((C, 5),),
        11: ((C, 6),),
    },
    "norm": ((V, 0),),
    "out": ((C, 7), (S, 1), (T, 0),),
    "datt": ((F, 3),),
    "pairs": {
        0: ((V, 1),),
        1: ((S, 2), (T, 1),),
        2: ((F, 4),),
        3: ((M, 0), (S, 3), (T, 2), (F, 5),),
        4: ((M, 1), (S, 4), (V, 2),),
        5: ((C, 8), (N, 0), (T, 3),),
    },
    "query": ((C, 9), (F, 6), (M, 2),),
    "key": ((C, 10), (T, 4), (S, 5), (F, 8), (N, 1),),
    "value": ((C, 11), (C, 12), (M, 3), (V, 3),),
    "input": ((M, 4), (T, 5), (N, 2), (F, 7), (S, 6),),
    "dxdone": (
        (N, 4), (N, 3), (S, 8), (S, 7), (M, 5), (F, 9), (T, 6), (F, 10), (T, 7), (T, 8),
        (M, 6), (N, 5),
    ),
    "tail": (
        (M, 7), (S, 9), (S, 10), (N, 6), (M, 8), (T, 9), (F, 11), (V, 4), (F, 12), (T, 10),
        (N, 7), (M, 9), (S, 11), (N, 8), (T, 11), (M, 10), (S, 12), (T, 12), (N, 9), (M, 11),
        (N, 10), (M, 12), (N, 11), (N, 12), (V, 5),
    ),
}


def scratch(reduce):
    shapes = [
        ("x", (512, 768), BF),
        ("facts", (8, 128), jnp.int32),
        ("meta", (4, 8, 128), jnp.int32),
        ("cot", (256, 768), BF),
        ("vectors", (8, 768), F32),
        ("wq", (768, 768), BF),
        ("wk", (768, 768), BF),
        ("wv", (768, 768), BF),
        ("wo", (768, 768), BF),
        ("wr", (768, 768), BF),
        ("pool", (2, 2, 2, 768, 768), BF),
        ("g", (2, 2, 2, 768, 768), BF),
        ("sine", (256, 384), F32),
        ("cosine", (256, 384), F32),
        ("feat", (512, 896), BF),
        ("q", (256, 768), BF),
        ("k", (512, 768), BF),
        ("v", (512, 768), BF),
        ("att", (256, 768), BF),
        ("relq", (512, 896), BF),
        ("score", (512, 512), F32),
        ("dlog", (512, 512), BF),
        ("probs", (PAIRS, 512, 512), BF),
        ("res", (256, 768), F32),
        ("hat", (256, 768), F32),
        ("scale", (256, 128), F32),
        ("low", (256, 768), BF),
        ("act", (256, 3072), BF),
        ("dlow", (256, 768), BF),
        ("out", (256, 768), BF),
        ("dxr", (256, 768), BF),
        ("din", (256, 768), BF),
        ("sm", (6, 8, 768), F32),
    ]
    if reduce:
        shapes += [("r1_%d" % u, (2, 2, c[2], 768), BF) for u, c in enumerate(CHUNKS)]
        shapes += [
            ("ra", (2, 624, 768), BF),
            ("rb", (2, 624, 768), BF),
            ("ra2", (624, 768), BF),
            ("rb2", (624, 768), BF),
            ("zr", (1248, 768), BF),
            ("za", (1248, 768), BF),
            ("sums", (1248, 768), BF),
            ("smr", (5, 8, 768), F32),
        ]
    return shapes


def layer(lengths, hidden_in, boxes, cotangent, vectors, weights, reduce):
    hi, lo = trig_tables(QUARTER)
    any_space = pl.BlockSpec(memory_space=pl.ANY)
    vmem = pl.BlockSpec(memory_space=pltpu.VMEM)
    ins = (
        ("lengths", lengths.reshape(-1), pl.BlockSpec(memory_space=pltpu.SMEM)),
        ("hidden_in", hidden_in, any_space),
        ("cotangent", cotangent, any_space),
        ("boxes", boxes, vmem),
        ("hi", jnp.asarray(hi), vmem),
        ("lo", jnp.asarray(lo), vmem),
    )
    ins += tuple(("vector%d" % i, v, vmem) for i, v in enumerate(vectors))
    ins += tuple((name, w, any_space) for name, w in weights)
    outs = (
        ("hidden_out", (2, 128, 768), BF),
        ("input_grad", (2, 128, 768), BF),
        ("share", (1248, 768) if reduce else (2, 2, 2, 2, 768, 768), BF),
        ("small", (8, 768), F32),
    )
    shapes = scratch(reduce)
    sems = ("send_sem", "recv_sem", "post_sem", "load_sem", "store_sem", "keep_sem")
    names = tuple(i[0] for i in ins) + tuple(o[0] for o in outs)
    names += tuple(s[0] for s in shapes) + sems
    dma = pltpu.SemaphoreType.DMA
    return pl.pallas_call(
        functools.partial(layer_kernel, names, reduce),
        out_shape=[jax.ShapeDtypeStruct(o[1], o[2]) for o in outs],
        in_specs=[i[2] for i in ins],
        out_specs=[any_space] * len(outs),
        scratch_shapes=[pltpu.VMEM(s[1], s[2]) for s in shapes]
        + [dma((len(i),)) for i in (SENDS, SENDS, POSTS, LOADS, STORES, CHUNKS)],
        compiler_params=pltpu.CompilerParams(
            vmem_limit_bytes=VMEM_LIMIT, collective_id=0, has_side_effects=True
        ),
        name="layer",
    )(*[i[1] for i in ins])


def finish_kernel(share, small, hid, din, hidden, dinput, dq, dk, dv, dout, drel, dup, *rest):
    dbup, ddown, vectors = rest[0], rest[1], rest[2:]
    hidden[...] = hid[...]
    dinput[...] = din[...]
    for j in range(4):
        dup[:, 768 * j : 768 * j + 768] = share[96 * j : 96 * j + 96, :].astype(F32)
    ddown[...] = share[384:768, :].astype(F32)
    for i, ref in enumerate((dout, drel, dq, dk, dv)):
        ref[...] = share[768 + 96 * i : 864 + 96 * i, :].astype(F32)
    dp = lax.axis_index("dp")
    row = small[pl.ds(dp // 2, 1), :]
    dbup[...] = jnp.where(dp % 2 == 0, row[:, 0:384], row[:, 384:768]).reshape(384)
    turned = pltpu.roll(small[...], lax.rem(768 - 96 * dp, 768), 1)
    for i, ref in enumerate(vectors):
        ref[...] = turned[4 + i : 5 + i, 0:96].reshape(96)


def finish(share, small, hidden, dinput):
    shapes = [(96, 768)] * 5 + [(96, 3072), (384,), (384, 768)] + [(96,)] * 4
    low = jax.ShapeDtypeStruct(hidden.shape, BF)
    return pl.pallas_call(
        finish_kernel,
        out_shape=[low, low] + [jax.ShapeDtypeStruct(s, F32) for s in shapes],
        name="finish",
    )(share, small, hidden, dinput)


def finish_any(g, small):
    order = g.transpose(0, 2, 3, 1, 4, 5).reshape(2, 8, 768, 768)

    def weight(which, base):
        return order[which, :, base : base + 96].reshape(768, 768)

    up = jnp.concatenate([weight(0, 96 * j) for j in range(4)], axis=1)
    down = order[0, :, 384:768].reshape(3072, 768)
    full = [weight(1, base) for base in (192, 288, 384, 0, 96)] + [up, down]
    grads = [
        lax.psum(lax.psum_scatter(w, "dp", scatter_dimension=0, tiled=True), "seq").astype(F32)
        for w in full
    ]
    small = lax.psum(small, ("dp", "seq"))
    dp, count = lax.axis_index("dp"), lax.axis_size("dp")

    def own_part(vector):
        size = vector.shape[0] // count
        return lax.dynamic_slice_in_dim(vector, dp * size, size)

    parts = [own_part(small[4 + i]) for i in range(4)]
    return grads[:6] + [own_part(small[0:4].reshape(-1)), grads[6]] + parts


def shards(
    hidden_in,
    boxes,
    lengths,
    w_query,
    w_key,
    w_value,
    w_out,
    w_rel,
    w_up,
    b_up,
    w_down,
    gain_attn,
    bias_attn,
    gain_ffn,
    bias_ffn,
    cotangent,
):
    vectors = (b_up, gain_attn, bias_attn, gain_ffn, bias_ffn)
    weights = (
        ("w_query", w_query),
        ("w_key", w_key),
        ("w_value", w_value),
        ("w_out", w_out),
        ("w_rel", w_rel),
        ("w_up", w_up),
        ("w_down", w_down),
    )
    reduce = lax.axis_size("dp") == 8
    hidden, dinput, share, small = layer(
        lengths,
        hidden_in[:, 0],
        boxes[:, :, 0],
        cotangent[:, 0],
        vectors,
        weights,
        reduce,
    )
    if reduce:
        hidden, dinput, *rest = finish(share, small, hidden, dinput)
    else:
        rest = finish_any(share, small)
    return (hidden[:, None], dinput[:, None], *rest)


def solution(mesh):
    rows = P(None, "dp", "seq", None)
    placed = (rows, P(None, None, "dp", "seq"), P(None, "dp")) + (P(),) * 12 + (rows,)
    matrix, vector = P("dp", None), P("dp")
    return jax.shard_map(
        shards,
        mesh=mesh,
        in_specs=placed,
        out_specs=(rows, rows) + (matrix,) * 6 + (vector, matrix) + (vector,) * 4,
        check_vma=False,
    )
```

```python
import functools

import jax
import jax.numpy as jnp
import numpy as np
from jax import lax
from jax.experimental import pallas as pl
from jax.experimental.pallas import tpu as pltpu
from jax.sharding import PartitionSpec as P

HEADS = 12
EPS = 1e-05
BF = jnp.bfloat16
F32 = jnp.float32
PAIRS = HEADS // 2
VMEM_LIMIT = 67043328
QUARTER = 192


def nn(a, b):
    return lax.dot_general(a, b, (((1,), (0,)), ((), ())), preferred_element_type=F32)


def nt(a, b):
    return lax.dot_general(a, b, (((1,), (1,)), ((), ())), preferred_element_type=F32)


def tn(a, b):
    return lax.dot_general(a, b, (((0,), (0,)), ((), ())), preferred_element_type=F32)


def trig_tables(quarter):
    freq = 10000.0 ** (-np.arange(quarter) / quarter)
    tables = []
    for step in (32.0, 1.0):
        angle = step * np.arange(32)[:, None] * freq[None, :]
        rest = np.concatenate([np.sin(angle), np.cos(angle)], axis=1).astype(np.float32)
        parts = []
        for _ in range(3):
            part = rest.astype(BF)
            parts.append(part)
            rest = rest - part.astype(np.float32)
        tables.append(np.concatenate(parts, axis=0))
    return tables


def features(slot, c, micro, r):
    half = 2 * QUARTER
    iota = lax.broadcasted_iota(jnp.int32, (32, 128), 0)
    hi_tab, lo_tab = r.hi[...], r.lo[...]
    block = pltpu.roll(r.meta[slot], 64 * c, 1)
    sines, cosines = [], []
    for axis in range(2):
        where = jnp.where(micro == 0, block[axis : axis + 1], block[2 + axis : 3 + axis])
        pick_hi = (iota == lax.shift_right_logical(where, 5)).astype(F32).astype(BF)
        pick_lo = (iota == (where & 31)).astype(F32).astype(BF)
        hi = tn(jnp.concatenate([pick_hi] * 3, axis=0), hi_tab)
        lo = tn(jnp.concatenate([pick_lo] * 3, axis=0), lo_tab)
        sin_hi, cos_hi = hi[:, :QUARTER], hi[:, QUARTER:]
        sin_lo, cos_lo = lo[:, :QUARTER], lo[:, QUARTER:]
        sines.append(sin_hi * cos_lo + cos_hi * sin_lo)
        cosines.append(cos_hi * cos_lo - sin_hi * sin_lo)
    sine = jnp.concatenate(sines, axis=1)
    cosine = jnp.concatenate(cosines, axis=1)
    for part in range(2):
        mine = slice(64 * part, 64 * part + 64)
        rows = pl.ds(256 * part + 64 * slot, 64)
        r.feat[rows, 0:half] = cosine[mine].astype(BF)
        r.feat[rows, half : 2 * half] = sine[mine].astype(BF)
    rows = pl.ds(64 * slot, 64)
    r.sine[rows, :] = sine[0:64]
    r.cosine[rows, :] = cosine[0:64]


def head_stack(pair):
    first = lax.broadcasted_iota(jnp.int32, pair.shape, 1) < 64
    zero = jnp.zeros_like(pair)
    return jnp.concatenate([jnp.where(first, pair, zero), jnp.where(first, zero, pair)], axis=0)


def head_join(stack):
    half = stack.shape[0] // 2
    first = lax.broadcasted_iota(jnp.int32, (half, 128), 1) < 64
    return jnp.where(first, stack[:half], stack[half:])


def attend_pair(pair, live, r):
    cols = pl.ds(pl.multiple_of(128 * pair, 128), 128)
    stack = head_stack(r.q[:, cols].astype(F32) * 0.125).astype(BF)
    both_left = nt(stack, r.wr[0:384, cols])
    both_right = nt(stack, r.wr[384:768, cols])
    for head in range(2):
        rows = slice(256 * head, 256 * head + 256)
        left, right = both_left[rows], both_right[rows]
        sin, cos = r.sine[...], r.cosine[...]
        r.relq[rows, 0:384] = (left * sin + right * cos).astype(BF)
        r.relq[rows, 384:768] = (right * sin - left * cos).astype(BF)
    r.relq[:, 768:896] = stack
    r.feat[:, 768:896] = r.k[:, cols]
    r.score[...] = nt(r.relq[...], r.feat[...])
    for block in range(8):
        rows = pl.ds(64 * block, 64)
        score = jnp.where(live, r.score[rows, :], -1e30)
        top = jnp.max(score, axis=-1, keepdims=True)
        weight = jnp.exp(score - top)
        total = jnp.sum(weight, axis=-1, keepdims=True)
        r.probs[pair, rows, :] = (weight * (1.0 / total)).astype(BF)
    r.att[:, cols] = head_join(nn(r.probs[pair], r.v[:, cols])).astype(BF)


def attend_pair_back(pair, r):
    cols = pl.ds(pl.multiple_of(128 * pair, 128), 128)
    given = head_stack(r.att[:, cols].astype(F32)).astype(BF)
    stack = head_stack(r.q[:, cols].astype(F32)).astype(BF)
    r.score[...] = nt(given, r.v[:, cols])
    for block in range(8):
        rows = pl.ds(64 * block, 64)
        prob = r.probs[pair, rows, :].astype(F32)
        push = prob * r.score[rows, :]
        mean = jnp.sum(push, axis=-1, keepdims=True)
        r.dlog[rows, :] = ((push - prob * mean) * 0.125).astype(BF)
    r.feat[:, 768:896] = r.k[:, cols]
    r.v[:, cols] = tn(r.probs[pair], given).astype(BF)
    r.k[:, cols] = tn(r.dlog[...], stack).astype(BF)
    for head in range(2):
        rows = slice(256 * head, 256 * head + 256)
        first = nn(r.dlog[rows, :], r.feat[:, 0:384])
        second = nn(r.dlog[rows, :], r.feat[:, 384:768])
        sin, cos = r.sine[...], r.cosine[...]
        r.relq[rows, 0:384] = (first * sin - second * cos).astype(BF)
        r.relq[rows, 384:768] = (first * cos + second * sin).astype(BF)
    dq = nn(r.dlog[...], r.feat[:, 768:896]) + nn(r.relq[:, 0:768], r.wr[:, cols])
    r.q[:, cols] = head_join(dq).astype(BF)
    part = tn(r.relq[:, 0:768], stack).astype(BF)
    for piece, share in enumerate((0, 1, 4, 5, 2, 3, 6, 7)):
        c, y, x = share % 2, share // 4, share // 2 % 2
        r.pool[c, y, x, 96:192, cols] = part[96 * piece : 96 * piece + 96]


def norm_back(given, hat, scale, gain):
    push = given * gain
    mean = jnp.mean(push, axis=-1, keepdims=True)
    lean = jnp.mean(push * hat, axis=-1, keepdims=True)
    return scale * (push - mean - hat * lean)


def put_shares(ref, base, cols, part):
    for share in range(8):
        c, y, x = share % 2, share // 4, share // 2 % 2
        ref[c, y, x, pl.ds(base, 96), cols] = part[96 * share : 96 * share + 96].astype(BF)


class Refs:
    pass


CHUNKS = (
    ("g", 384, 128, 384),
    ("g", 512, 128, 512),
    ("g", 640, 128, 640),
    ("g", 0, 96, 0),
    ("g", 96, 96, 96),
    ("g", 192, 96, 192),
    ("g", 288, 96, 288),
    ("pool", 0, 96, 768),
    ("pool", 96, 96, 864),
    ("pool", 192, 96, 960),
    ("pool", 288, 96, 1056),
    ("pool", 384, 64, 1152),
    ("pool", 448, 32, 1216),
)
C, F, S, T, M, N, V = range(7)
STAGES = ("core", "xa", "xb", "ya", "yb", "z1", "z2", "z3")
BLOCKS = ("x", "m", "c", "f", "o", "d")
SENDS = tuple(k + str(i) for k in BLOCKS for i in range(4)) + ("dx0",)
SENDS += tuple("s%d" % i for i in range(5))
SENDS += tuple("%s%d" % (s, u) for u in range(len(CHUNKS)) for s in STAGES)
LOADS = ("x", "x2", "cot", "key", "value", "query", "out")
LOADS += tuple("rel%d" % i for i in range(4)) + tuple("up%d" % i for i in range(4))
LOADS += tuple("down%d" % i for i in range(4))
STORES = ("hid", "din", "share", "small")
POSTS = tuple(k + i for k in "xmc" for i in ("a0", "a1", "b0", "b1", "p"))
POSTS += tuple(k + str(i) for k in "fod" for i in range(4)) + ("dx",)


class Net:
    def __init__(self, r):
        self.r = r
        self.made = {}
        self.order = {"all": [], "end": [], "mid": []}
        self.posts = {"all": [], "own": [], "far": []}

    def _of(self, name):
        i = SENDS.index(name)
        src, dst, peer = self.made[name]()
        return pltpu.make_async_remote_copy(
            src_ref=src,
            dst_ref=dst,
            send_sem=self.r.send_sem.at[i],
            recv_sem=self.r.recv_sem.at[i],
            device_id=peer,
            device_id_type=pl.DeviceIdType.MESH,
        )

    def start(self, name, make, role="all"):
        self.made[name] = make
        self._of(name).start()
        self.order[role].append(name)

    def got(self, name):
        self._of(name).wait_recv()

    def _post(self, name, src, dst, at, peer):
        return pltpu.make_async_remote_copy(
            src_ref=src,
            dst_ref=dst,
            send_sem=self.r.post_sem.at[POSTS.index(name)],
            recv_sem=self.r.recv_sem.at[at],
            device_id=peer,
            device_id_type=pl.DeviceIdType.MESH,
        )

    def post(self, name, kind, index, make, role="all"):
        src, dst, peer = make()
        self._post(name, src, dst, SENDS.index(kind + "0") + index, peer).start()
        self.posts[role].append((name, kind, index, make))

    def came(self, kind, index, make):
        src, dst, peer = make()
        self._post(POSTS[0], src, dst, SENDS.index(kind + "0") + index, peer).wait_recv()

    def finish(self, role):
        for name in self.order[role]:
            self._of(name).wait_send()

    def posted(self, role):
        for name, kind, index, make in self.posts[role]:
            src, dst, peer = make()
            self._post(name, src, dst, SENDS.index(kind + "0") + index, peer).wait_send()


def add_rows(count, body):
    size = 48 if count % 48 == 0 else 32 if count % 32 == 0 else 16

    def step(i, carry):
        body(pl.multiple_of(size * i, 16), size)
        return carry

    lax.fori_loop(0, count // size, step, 0)


def total(*terms):
    out = terms[0].astype(F32)
    for term in terms[1:]:
        out = out + term.astype(F32)
    return out.astype(BF)


class Reduction:
    def __init__(self, r, net, dp, z):
        self.r, self.net = r, net
        self.c, self.x, self.y = dp % 2, dp // 2 % 2, dp // 4
        self.pc = (dp + 1 - 2 * self.c, z)
        self.px = (dp + 2 - 4 * self.x, z)
        self.py = (dp + 4 - 8 * self.y, z)
        self.pz1 = (dp, z + 1 - 2 * (z % 2))
        self.pz2 = (dp, (z + 2) % 4)
        self.across = (dp, 3 - z)

    def parts(self, u):
        name, base, rows, out = CHUNKS[u]
        return getattr(self.r, name), base, rows // 2, out, self.r.r1[u], out // 2

    def core(self, u):
        g, base, half, _, r1, _ = self.parts(u)
        self.net.start(
            "core%d" % u, lambda: (g.at[1 - self.c, :, :, pl.ds(base, 2 * half)], r1, self.pc)
        )

    def first(self, u):
        g, base, half, _, r1, at = self.parts(u)
        c, x, y = self.c, self.x, self.y
        self.net.got("core%d" % u)

        def add(i, size):
            for k in range(2):
                rows, own = pl.ds(base + i, size), pl.ds(i, size)
                g[c, k, 1 - x, rows] = total(g[c, k, 1 - x, rows], r1[k, 1 - x, own])
                rows, own = pl.ds(base + half + i, size), pl.ds(half + i, size)
                g[c, 1 - y, k, rows] = total(g[c, 1 - y, k, rows], r1[1 - y, k, own])

        add_rows(half, add)
        a, b, to = pl.ds(base, half), pl.ds(base + half, half), pl.ds(at, half)
        self.net.start("xa%d" % u, lambda: (g.at[c, :, 1 - x, a], self.r.ra.at[:, to], self.px))
        self.net.start("yb%d" % u, lambda: (g.at[c, 1 - y, :, b], self.r.rb.at[:, to], self.py))

    def second(self, u):
        g, base, half, _, r1, at = self.parts(u)
        c, x, y = self.c, self.x, self.y
        ra, rb = self.r.ra, self.r.rb
        self.net.got("xa%d" % u)
        self.net.got("yb%d" % u)

        def add(i, size):
            came = pl.ds(at + i, size)
            rows, own = pl.ds(base + i, size), pl.ds(i, size)
            g[c, 1 - y, x, rows] = total(g[c, 1 - y, x, rows], r1[1 - y, x, own], ra[1 - y, came])
            rows, own = pl.ds(base + half + i, size), pl.ds(half + i, size)
            g[c, y, 1 - x, rows] = total(g[c, y, 1 - x, rows], r1[y, 1 - x, own], rb[1 - x, came])

        add_rows(half, add)
        a, b, to = pl.ds(base, half), pl.ds(base + half, half), pl.ds(at, half)
        self.net.start("ya%d" % u, lambda: (g.at[c, 1 - y, x, a], self.r.ra2.at[to], self.py))
        self.net.start("xb%d" % u, lambda: (g.at[c, y, 1 - x, b], self.r.rb2.at[to], self.px))

    def third(self, u, mid):
        g, base, half, out, r1, at = self.parts(u)
        c, x, y = self.c, self.x, self.y
        ra, rb, ra2, rb2, zr = self.r.ra, self.r.rb, self.r.ra2, self.r.rb2, self.r.zr
        self.net.got("ya%d" % u)
        self.net.got("xb%d" % u)
        if mid:
            self.net.got("z1%d" % u)

        def add(i, size):
            came = pl.ds(at + i, size)
            rows, own = pl.ds(base + i, size), pl.ds(i, size)
            more = (zr[pl.ds(out + i, size)],) if mid else ()
            g[c, y, x, rows] = total(
                g[c, y, x, rows], r1[y, x, own], ra[y, came], ra2[came], *more
            )
            rows, own = pl.ds(base + half + i, size), pl.ds(half + i, size)
            more = (zr[pl.ds(out + half + i, size)],) if mid else ()
            g[c, y, x, rows] = total(
                g[c, y, x, rows], r1[y, x, own], rb[x, came], rb2[came], *more
            )

        add_rows(half, add)
        rows, to = pl.ds(base, 2 * half), pl.ds(out, 2 * half)
        if mid:
            make = lambda: (g.at[c, y, x, rows], self.r.za.at[to], self.across)
            self.net.start("z2%d" % u, make, "mid")
        else:
            make = lambda: (g.at[c, y, x, rows], self.r.zr.at[to], self.pz1)
            self.net.start("z1%d" % u, make, "end")

    def fourth(self, u):
        g, base, half, out, _, _ = self.parts(u)
        c, x, y = self.c, self.x, self.y
        self.net.got("z2%d" % u)

        def add(i, size):
            rows, to = pl.ds(base + i, size), pl.ds(out + i, size)
            self.r.sums[to] = total(g[c, y, x, rows], self.r.za[to])

        add_rows(2 * half, add)
        to = pl.ds(out, 2 * half)
        self.net.start("z3%d" % u, lambda: (self.r.sums.at[to], self.r.sums.at[to], self.pz1), "mid")

    def small(self, i):
        if i:
            self.net.got("s%d" % (i - 1))
            self.r.sm[i] = self.r.sm[i - 1] + self.r.smr[i - 1]
        if i < 5:
            peer = (self.pc, self.px, self.py, self.pz1, self.pz2)[i]
            self.net.start("s%d" % i, lambda: (self.r.sm.at[i], self.r.smr.at[i], peer))


def layer_kernel(names, reduce, *refs):
    r = Refs()
    for name, ref in zip(names, refs):
        setattr(r, name, ref)
    dp, z = lax.axis_index("dp"), lax.axis_index("seq")
    micro, c = z // 2, dp % 2
    is_mid = lax.rem(z, 3) > 0
    is_end = lax.rem(z, 3) == 0
    own = c == z % 2
    far = c != z % 2
    base = jnp.where(own, 0, 1)
    column = dp - c
    source = column + z % 2
    pair = (dp + 1 - 2 * c, z)
    half = pl.ds(pl.multiple_of(64 * c, 64), 64)
    other = pl.ds(pl.multiple_of(64 - 64 * c, 64), 64)
    net = Net(r)
    red = None
    if reduce:
        r.r1 = tuple(getattr(r, "r1_%d" % u) for u in range(len(CHUNKS)))
        red = Reduction(r, net, dp, z)

    def kept(u):
        rows = pl.ds(CHUNKS[u][3], CHUNKS[u][2])
        return pltpu.make_async_copy(r.sums.at[rows], r.share.at[rows], r.keep_sem.at[u])

    def whole(u):
        red.fourth(u)
        kept(u).start()

    def run(*steps):
        if not reduce:
            return
        for kind, u in steps:
            if kind == C:
                red.core(u)
            elif kind == F:
                red.first(u)
            elif kind == S:
                red.second(u)
            elif kind == T:
                pl.when(is_end)(functools.partial(red.third, u, False))
            elif kind == M:
                pl.when(is_mid)(functools.partial(red.third, u, True))
            elif kind == N:
                pl.when(is_mid)(functools.partial(whole, u))
            else:
                red.small(u)

    def run_plan(place):
        run(*PLAN.get(place, ()))

    def run_at(index, place):
        for at, steps in PLAN[place].items():
            pl.when(index == at)(functools.partial(run, *steps))

    loads = {}

    def load(name, src, dst):
        loads[name] = lambda: (src(), dst(), r.load_sem.at[LOADS.index(name)])
        pltpu.make_async_copy(*loads[name]()).start()

    def loaded(name):
        pltpu.make_async_copy(*loads[name]()).wait()

    load("key", lambda: r.w_key, lambda: r.wk)
    load("value", lambda: r.w_value, lambda: r.wv)
    load("query", lambda: r.w_query, lambda: r.wq)

    greet = [pair] + [(column + h, (z + i) % 4) for i in range(1, 4) for h in range(2)]
    greet += [red.px, red.py] if reduce else []
    line = lax.broadcasted_iota(jnp.int32, (8, 128), 0)
    wide = [r.boxes[axis, m : m + 1, :] for m in range(2) for axis in range(2)]
    wide = jnp.concatenate(wide * 2, axis=0)
    wide = jnp.where(line == 4, r.lengths[0], jnp.where(line == 5, r.lengths[1], wide))
    r.facts[...] = wide
    barrier = pltpu.get_barrier_semaphore()
    for peer in greet:
        pl.semaphore_signal(barrier, 1, device_id=peer, device_id_type=pl.DeviceIdType.MESH)
    pl.semaphore_wait(barrier, len(greet))

    def spread(kind, src, dst):
        for first in (False, True):
            step = base if first else base + 2
            to = (z + 4 - step) % 4
            rows = pl.ds(pl.multiple_of(64 * step, 64), 64)
            for h in range(2):
                def make(h=h, to=to, rows=rows, step=step):
                    return src(to // 2, pl.ds(64 * h, 64)), dst(step, rows), (column + h, to)

                name = kind + ("a" if first else "b") + str(h)
                if first:
                    pl.when(far)(functools.partial(net.post, name, kind, step, make, "far"))
                else:
                    net.post(name, kind, step, make)

    def here(kind, src, dst):
        make = lambda: (src(micro, other), dst(0, pl.ds(0, 64)), pair)
        net.post(kind + "p", kind, 0, make, "own")

    hidden = lambda m, rows: r.hidden_in.at[m, rows]
    grads = lambda m, rows: r.cotangent.at[m, rows]

    x_to = lambda step, rows: r.x.at[rows]
    m_to = lambda step, rows: r.meta.at[step]
    c_to = lambda step, rows: r.cot.at[rows]
    spread("m", lambda m, rows: r.facts, m_to)
    spread("x", hidden, x_to)

    @pl.when(own)
    def _():
        here("m", lambda m, rows: r.facts, m_to)
        here("x", hidden, x_to)
        make = lambda: (hidden(micro, half), r.x.at[256:320], pair)
        net.post("f0", "f", 0, make, "own")
        load("x", lambda: hidden(micro, half), lambda: r.x.at[0:64])
        load("x2", lambda: hidden(micro, other), lambda: r.x.at[256:320])
        r.meta[0] = r.facts[...]

    for i, (dst, src) in enumerate(((0, 0), (192, 384), (384, 192), (576, 576))):
        load("rel%d" % i, lambda src=src, dst=dst: r.w_rel.at[src : src + 192], lambda src=src, dst=dst: r.wr.at[dst : dst + 192])
    load("out", lambda: r.w_out, lambda: r.wo)
    for j in range(4):
        load("up%d" % j, lambda j=j: r.w_up.at[:, 768 * j : 768 * j + 768], lambda j=j: r.pool.at[0, j // 2, j % 2])
    for j in range(4):
        load("down%d" % j, lambda j=j: r.w_down.at[768 * j : 768 * j + 768], lambda j=j: r.pool.at[1, j // 2, j % 2])
    pl.when(own)(lambda: load("cot", lambda: grads(micro, half), lambda: r.cot.at[0:64]))

    def project(start, stop):
        rows = slice(start, stop)
        for tile in range(3):
            cols = slice(256 * tile, 256 * tile + 256)
            r.k[rows, cols] = nn(r.x[rows, :], r.wk[:, cols]).astype(BF)
            r.v[rows, cols] = nn(r.x[rows, :], r.wv[:, cols]).astype(BF)
            if stop <= 256:
                r.q[rows, cols] = nn(r.x[rows, :], r.wq[:, cols]).astype(BF)

    for j in range(4):
        r.vectors[j : j + 1, :] = r.vector0[768 * j : 768 * j + 768].astype(F32).reshape(1, 768)
        row = getattr(r, "vector%d" % (j + 1))[...]
        r.vectors[4 + j : 5 + j, :] = row.astype(F32).reshape(1, 768)
    x_size = lambda: (hidden(0, pl.ds(0, 64)), r.x.at[0:64], pair)
    m_size = lambda: (r.facts, r.meta.at[0], pair)
    pl.when(far)(lambda: net.came("m", 0, m_size))
    features(0, c, micro, r)
    for slot in (1, 3, 2):
        net.came("m", slot, m_size)
        features(slot, c, micro, r)
    loaded("key")
    loaded("value")
    loaded("query")

    @pl.when(own)
    def _():
        loaded("x")
        loaded("x2")

    @pl.when(far)
    def _():
        net.came("x", 0, x_size)
        net.came("f", 0, x_size)

    project(0, 64)
    project(256, 320)
    for i in range(4):
        loaded("rel%d" % i)
    for slot in (1, 3, 2):
        net.came("x", slot, x_size)
        mine, theirs = slice(64 * slot, 64 * slot + 64), slice(256 + 64 * slot, 320 + 64 * slot)
        make = lambda mine=mine, theirs=theirs: (r.x.at[mine], r.x.at[theirs], pair)
        net.post("f%d" % slot, "f", slot, make)
    spread("c", grads, c_to)
    pl.when(own)(lambda: here("c", grads, c_to))
    project(64, 256)
    for slot in (1, 3, 2):
        net.came("f", slot, x_size)
    project(320, 512)

    place = lax.broadcasted_iota(jnp.int32, (1, 512), 1)
    turn = lax.shift_right_logical(place, 8)
    token = 128 * ((z + (lax.shift_right_logical(place, 6) & 3)) & 3) + (place & 63)
    token = token + 64 * ((c + turn) & 1)
    known = r.meta[1]
    length = jnp.where(micro == 0, known[4:5], known[5:6])
    live = token < jnp.concatenate([length] * 4, axis=1)

    def attend(pair, carry):
        attend_pair(pair, live, r)
        return carry

    lax.fori_loop(0, PAIRS, attend, 0, unroll=6)

    loaded("out")
    for tile in range(3):
        cols = slice(256 * tile, 256 * tile + 256)
        r.res[:, cols] = r.x[0:256, cols].astype(F32) + nn(r.att[...], r.wo[:, cols])

    gain1, bias1, gain2, bias2 = [r.vectors[4 + i : 5 + i, :] for i in range(4)]
    for block in range(4):
        rows = slice(64 * block, 64 * block + 64)
        res = r.res[rows, :]
        center = res - jnp.mean(res, axis=-1, keepdims=True)
        scale = lax.rsqrt(jnp.mean(center * center, axis=-1, keepdims=True) + EPS)
        hat = center * scale
        r.hat[rows, :] = hat
        r.scale[rows, :] = jnp.broadcast_to(scale, (64, 128))
        normed = hat * gain1 + bias1
        r.res[rows, :] = normed
        r.low[rows, :] = normed.astype(BF)

    for j in range(4):
        loaded("up%d" % j)
    for j in range(4):
        loaded("down%d" % j)

    def up_tile(tile):
        j = tile // 3
        return j // 2, j % 2, pl.ds(pl.multiple_of(256 * (tile % 3), 256), 256)

    def up(tile, carry):
        cols = pl.ds(pl.multiple_of(256 * tile, 256), 256)
        y, x, part = up_tile(tile)
        bias = r.vectors[pl.ds(tile // 3, 1), part]
        value = nn(r.low[...], r.pool[0, y, x, :, part]) + bias
        below = 0.5 * (1.0 + lax.erf(value * np.float32(np.sqrt(0.5))))
        r.act[:, cols] = (value * below).astype(BF)
        top = value.astype(BF)
        r.g[0, y, x, 0:256, part] = top
        r.g[1, y, x, 0:256, part] = (value - top.astype(F32)).astype(BF)
        return carry

    lax.fori_loop(0, 12, up, 0, unroll=12)
    for tile in range(3):
        cols = slice(256 * tile, 256 * tile + 256)
        r.res[:, cols] = r.res[:, cols] + sum(
            nn(r.act[:, 768 * j : 768 * j + 768], r.pool[1, j // 2, j % 2, :, cols])
            for j in range(4)
        )

    c_size = lambda: (grads(0, pl.ds(0, 64)), r.cot.at[0:64], pair)
    pl.when(own)(lambda: loaded("cot"))
    pl.when(far)(lambda: net.came("c", 0, c_size))
    for slot in (1, 2, 3):
        net.came("c", slot, c_size)
    sums = [jnp.zeros((1, 768), F32) for _ in range(4)]
    for block in range(4):
        rows = slice(64 * block, 64 * block + 64)
        res = r.res[rows, :]
        center = res - jnp.mean(res, axis=-1, keepdims=True)
        scale = lax.rsqrt(jnp.mean(center * center, axis=-1, keepdims=True) + EPS)
        hat = center * scale
        r.out[rows, :] = (hat * gain2 + bias2).astype(BF)
        given = r.cot[rows, :].astype(F32)
        sums[2] = sums[2] + jnp.sum(given * hat, axis=0, keepdims=True)
        sums[3] = sums[3] + jnp.sum(given, axis=0, keepdims=True)
        dres = norm_back(given, hat, scale, gain2)
        r.res[rows, :] = dres
        r.dlow[rows, :] = dres.astype(BF)

    def grad_down(offset):
        for quad in range(2):
            shares = range(4 * quad, 4 * quad + 4)
            starts = [384 * share + offset for share in shares]
            left = jnp.concatenate([r.act[:, at : at + 128] for at in starts], axis=1)
            part = tn(left, r.dlow[...]).astype(BF)
            for i, share in enumerate(shares):
                place = (share % 2, share // 4, share // 2 % 2, pl.ds(384 + offset, 128))
                r.g[place] = part[128 * i : 128 * i + 128]

    for third in range(3):
        grad_down(128 * third)
        run_plan("down%d" % third)
    stores = {}

    def store(name, src, dst):
        stores[name] = lambda: (src(), dst(), r.store_sem.at[STORES.index(name)])
        pltpu.make_async_copy(*stores[name]()).start()

    def stored(name):
        pltpu.make_async_copy(*stores[name]()).wait()

    def give_back(kind, src, dst):
        for slot in (3, 1, 2, 0):
            rows = slice(64 * slot, 64 * slot + 64)
            to = (source, (z + slot) % 4)
            make = lambda rows=rows, to=to: (src.at[rows], dst.at[micro, half], to)
            role = "all" if slot else "far"
            post = functools.partial(net.post, kind + str(slot), kind, 2 * micro + c, make, role)
            if slot:
                post()
            else:
                pl.when(far)(post)

    def given_back(kind, dst):
        size = lambda: (r.out.at[0:64], dst.at[0, 0:64], pair)
        for m in range(2):
            for h in range(2):
                local = own & (micro == m) & (c == h)
                pl.when(jnp.logical_not(local))(functools.partial(net.came, kind, 2 * m + h, size))

    give_back("o", r.out, r.hidden_out)
    pl.when(own)(lambda: store("hid", lambda: r.out.at[0:64], lambda: r.hidden_out.at[micro, half]))

    def up_back(tile, carry):
        cols = pl.ds(pl.multiple_of(256 * tile, 256), 256)
        y, x, part = up_tile(tile)
        value = r.g[0, y, x, 0:256, part].astype(F32) + r.g[1, y, x, 0:256, part].astype(F32)
        below = 0.5 * (1.0 + lax.erf(value * np.float32(np.sqrt(0.5))))
        dense = jnp.exp(value * value * -0.5) * np.float32(1.0 / np.sqrt(2.0 * np.pi))
        slope = below + value * dense
        push = nt(r.dlow[...], r.pool[1, y, x, part, :]) * slope
        low = push.astype(BF)
        r.act[:, cols] = low
        r.sm[0, pl.ds(tile // 3, 1), part] = jnp.sum(low.astype(F32), axis=0, keepdims=True)
        run_at(tile, "up_back")
        return carry

    lax.fori_loop(0, 12, up_back, 0)

    def grad_up(tile, carry):
        cols = pl.ds(pl.multiple_of(256 * tile, 256), 256)
        _, _, dest = up_tile(tile)
        put_shares(r.g, pl.multiple_of(96 * (tile // 3), 32), dest, tn(r.low[...], r.act[:, cols]))
        run_at(tile, "grad_up")
        return carry

    lax.fori_loop(0, 12, grad_up, 0)
    for tile in range(3):
        cols = slice(256 * tile, 256 * tile + 256)
        r.res[:, cols] = r.res[:, cols] + sum(
            nt(r.act[:, 768 * j : 768 * j + 768], r.pool[0, j // 2, j % 2, cols, :])
            for j in range(4)
        )
    for block in range(4):
        rows = slice(64 * block, 64 * block + 64)
        given, hat = r.res[rows, :], r.hat[rows, :]
        sums[0] = sums[0] + jnp.sum(given * hat, axis=0, keepdims=True)
        sums[1] = sums[1] + jnp.sum(given, axis=0, keepdims=True)
        dres = norm_back(given, hat, r.scale[rows, 0:1], gain1)
        r.res[rows, :] = dres
        r.dlow[rows, :] = dres.astype(BF)
    for row in range(4):
        r.sm[0, 4 + row : 5 + row, :] = sums[row]
    run_plan("norm")
    for tile in range(3):
        cols = slice(256 * tile, 256 * tile + 256)
        put_shares(r.pool, 0, cols, tn(r.att[...], r.dlow[:, cols]))
    run_plan("out")
    for tile in range(3):
        cols = slice(256 * tile, 256 * tile + 256)
        r.att[:, cols] = nt(r.dlow[...], r.wo[cols, :]).astype(BF)
    run_plan("datt")

    def attend_back(pair, carry):
        attend_pair_back(pair, r)
        run_at(pair, "pairs")
        return carry

    lax.fori_loop(0, PAIRS, attend_back, 0)
    for tile in range(3):
        cols = slice(256 * tile, 256 * tile + 256)
        put_shares(r.pool, 192, cols, tn(r.x[0:256, :], r.q[:, cols]))
    run_plan("query")
    for tile in range(3):
        cols = slice(256 * tile, 256 * tile + 256)
        put_shares(r.pool, 288, cols, tn(r.x[...], r.k[:, cols]))
    run_plan("key")
    for tile in range(3):
        cols = slice(256 * tile, 256 * tile + 256)
        put_shares(r.pool, 384, cols, tn(r.x[...], r.v[:, cols]))
    run_plan("value")

    for tile in range(3):
        cols = slice(256 * tile, 256 * tile + 256)
        tail = nt(r.k[...], r.wk[cols, :]) + nt(r.v[...], r.wv[cols, :])
        r.relq[256:512, cols] = tail[256:512].astype(BF)
        r.relq[0:256, cols] = (
            tail[0:256] + r.res[:, cols] + nt(r.q[...], r.wq[cols, :])
        ).astype(BF)
    net.post("dx", "dx", 0, lambda: (r.relq.at[256:512, 0:768], r.dxr, pair))
    run_plan("input")
    net.came("dx", 0, lambda: (r.relq.at[256:512, 0:768], r.dxr, pair))
    r.din[...] = (r.relq[0:256, 0:768].astype(F32) + r.dxr[...].astype(F32)).astype(BF)
    give_back("d", r.din, r.input_grad)
    pl.when(own)(lambda: store("din", lambda: r.din.at[0:64], lambda: r.input_grad.at[micro, half]))
    run_plan("dxdone")
    run_plan("tail")
    if reduce:
        store("small", lambda: r.sm.at[5], lambda: r.small)

        @pl.when(is_end)
        def _():
            for u in range(len(CHUNKS)):
                net.got("z3%d" % u)
                kept(u).start()
    else:
        store("small", lambda: r.sm.at[0], lambda: r.small)
        store("share", lambda: r.g, lambda: r.share.at[0])
        last = pltpu.make_async_copy(r.pool, r.share.at[1], r.load_sem.at[0])
        last.start()
        last.wait()
    given_back("o", r.hidden_out)
    given_back("d", r.input_grad)
    stored("small")
    if reduce:
        for u in range(len(CHUNKS)):
            kept(u).wait()
    else:
        stored("share")

    @pl.when(own)
    def _():
        stored("hid")
        stored("din")
        net.posted("own")

    pl.when(far)(lambda: net.posted("far"))
    net.posted("all")
    net.finish("all")
    pl.when(is_end)(lambda: net.finish("end"))
    pl.when(is_mid)(lambda: net.finish("mid"))


PLAN = {
    "down0": ((C, 0),),
    "down1": ((C, 1),),
    "down2": ((C, 2), (F, 0),),
    "up_back": {
        1: ((F, 1),),
    },
    "grad_up": {
        2: ((C, 3),),
        3: ((S, 0),),
        5: ((C, 4),),
        6: ((F, 2),),
        8: ((C, 5),),
        11: ((C, 6),),
    },
    "norm": ((V, 0),),
    "out": ((C, 7), (S, 1), (T, 0),),
    "datt": ((F, 3),),
    "pairs": {
        0: ((V, 1),),
        1: ((S, 2), (T, 1),),
        2: ((F, 4),),
        3: ((M, 0), (S, 3), (T, 2), (F, 5),),
        4: ((M, 1), (S, 4), (V, 2),),
        5: ((C, 8), (N, 0), (T, 3),),
    },
    "query": ((C, 9), (F, 6), (M, 2),),
    "key": ((C, 10), (T, 4), (S, 5), (F, 8), (N, 1),),
    "value": ((C, 11), (C, 12), (M, 3), (V, 3),),
    "input": ((M, 4), (T, 5), (N, 2), (F, 7), (S, 6),),
    "dxdone": (
        (N, 4), (N, 3), (S, 8), (S, 7), (M, 5), (F, 9), (T, 6), (F, 10), (T, 7), (T, 8),
        (M, 6), (N, 5),
    ),
    "tail": (
        (M, 7), (S, 9), (S, 10), (N, 6), (M, 8), (T, 9), (F, 11), (V, 4), (F, 12), (T, 10),
        (N, 7), (M, 9), (S, 11), (N, 8), (T, 11), (M, 10), (S, 12), (T, 12), (N, 9), (M, 11),
        (N, 10), (M, 12), (N, 11), (N, 12), (V, 5),
    ),
}


def scratch(reduce):
    shapes = [
        ("x", (512, 768), BF),
        ("facts", (8, 128), jnp.int32),
        ("meta", (4, 8, 128), jnp.int32),
        ("cot", (256, 768), BF),
        ("vectors", (8, 768), F32),
        ("wq", (768, 768), BF),
        ("wk", (768, 768), BF),
        ("wv", (768, 768), BF),
        ("wo", (768, 768), BF),
        ("wr", (768, 768), BF),
        ("pool", (2, 2, 2, 768, 768), BF),
        ("g", (2, 2, 2, 768, 768), BF),
        ("sine", (256, 384), F32),
        ("cosine", (256, 384), F32),
        ("feat", (512, 896), BF),
        ("q", (256, 768), BF),
        ("k", (512, 768), BF),
        ("v", (512, 768), BF),
        ("att", (256, 768), BF),
        ("relq", (512, 896), BF),
        ("score", (512, 512), F32),
        ("dlog", (512, 512), BF),
        ("probs", (PAIRS, 512, 512), BF),
        ("res", (256, 768), F32),
        ("hat", (256, 768), F32),
        ("scale", (256, 128), F32),
        ("low", (256, 768), BF),
        ("act", (256, 3072), BF),
        ("dlow", (256, 768), BF),
        ("out", (256, 768), BF),
        ("dxr", (256, 768), BF),
        ("din", (256, 768), BF),
        ("sm", (6, 8, 768), F32),
    ]
    if reduce:
        shapes += [("r1_%d" % u, (2, 2, c[2], 768), BF) for u, c in enumerate(CHUNKS)]
        shapes += [
            ("ra", (2, 624, 768), BF),
            ("rb", (2, 624, 768), BF),
            ("ra2", (624, 768), BF),
            ("rb2", (624, 768), BF),
            ("zr", (1248, 768), BF),
            ("za", (1248, 768), BF),
            ("sums", (1248, 768), BF),
            ("smr", (5, 8, 768), F32),
        ]
    return shapes


def layer(lengths, hidden_in, boxes, cotangent, vectors, weights, reduce):
    hi, lo = trig_tables(QUARTER)
    any_space = pl.BlockSpec(memory_space=pl.ANY)
    vmem = pl.BlockSpec(memory_space=pltpu.VMEM)
    ins = (
        ("lengths", lengths.reshape(-1), pl.BlockSpec(memory_space=pltpu.SMEM)),
        ("hidden_in", hidden_in, any_space),
        ("cotangent", cotangent, any_space),
        ("boxes", boxes, vmem),
        ("hi", jnp.asarray(hi), vmem),
        ("lo", jnp.asarray(lo), vmem),
    )
    ins += tuple(("vector%d" % i, v, vmem) for i, v in enumerate(vectors))
    ins += tuple((name, w, any_space) for name, w in weights)
    outs = (
        ("hidden_out", (2, 128, 768), BF),
        ("input_grad", (2, 128, 768), BF),
        ("share", (1248, 768) if reduce else (2, 2, 2, 2, 768, 768), BF),
        ("small", (8, 768), F32),
    )
    shapes = scratch(reduce)
    sems = ("send_sem", "recv_sem", "post_sem", "load_sem", "store_sem", "keep_sem")
    names = tuple(i[0] for i in ins) + tuple(o[0] for o in outs)
    names += tuple(s[0] for s in shapes) + sems
    dma = pltpu.SemaphoreType.DMA
    return pl.pallas_call(
        functools.partial(layer_kernel, names, reduce),
        out_shape=[jax.ShapeDtypeStruct(o[1], o[2]) for o in outs],
        in_specs=[i[2] for i in ins],
        out_specs=[any_space] * len(outs),
        scratch_shapes=[pltpu.VMEM(s[1], s[2]) for s in shapes]
        + [dma((len(i),)) for i in (SENDS, SENDS, POSTS, LOADS, STORES, CHUNKS)],
        compiler_params=pltpu.CompilerParams(
            vmem_limit_bytes=VMEM_LIMIT, collective_id=0, has_side_effects=True
        ),
        name="layer",
    )(*[i[1] for i in ins])


def finish_kernel(share, small, hid, din, hidden, dinput, dq, dk, dv, dout, drel, dup, *rest):
    dbup, ddown, vectors = rest[0], rest[1], rest[2:]
    hidden[...] = hid[...]
    dinput[...] = din[...]
    for j in range(4):
        dup[:, 768 * j : 768 * j + 768] = share[96 * j : 96 * j + 96, :].astype(F32)
    ddown[...] = share[384:768, :].astype(F32)
    for i, ref in enumerate((dout, drel, dq, dk, dv)):
        ref[...] = share[768 + 96 * i : 864 + 96 * i, :].astype(F32)
    dp = lax.axis_index("dp")
    row = small[pl.ds(dp // 2, 1), :]
    dbup[...] = jnp.where(dp % 2 == 0, row[:, 0:384], row[:, 384:768]).reshape(384)
    turned = pltpu.roll(small[...], lax.rem(768 - 96 * dp, 768), 1)
    for i, ref in enumerate(vectors):
        ref[...] = turned[4 + i : 5 + i, 0:96].reshape(96)


def finish(share, small, hidden, dinput):
    shapes = [(96, 768)] * 5 + [(96, 3072), (384,), (384, 768)] + [(96,)] * 4
    low = jax.ShapeDtypeStruct(hidden.shape, BF)
    return pl.pallas_call(
        finish_kernel,
        out_shape=[low, low] + [jax.ShapeDtypeStruct(s, F32) for s in shapes],
        name="finish",
    )(share, small, hidden, dinput)


def finish_any(g, small):
    order = g.transpose(0, 2, 3, 1, 4, 5).reshape(2, 8, 768, 768)

    def weight(which, base):
        return order[which, :, base : base + 96].reshape(768, 768)

    up = jnp.concatenate([weight(0, 96 * j) for j in range(4)], axis=1)
    down = order[0, :, 384:768].reshape(3072, 768)
    full = [weight(1, base) for base in (192, 288, 384, 0, 96)] + [up, down]
    grads = [
        lax.psum(lax.psum_scatter(w, "dp", scatter_dimension=0, tiled=True), "seq").astype(F32)
        for w in full
    ]
    small = lax.psum(small, ("dp", "seq"))
    dp, count = lax.axis_index("dp"), lax.axis_size("dp")

    def own_part(vector):
        size = vector.shape[0] // count
        return lax.dynamic_slice_in_dim(vector, dp * size, size)

    parts = [own_part(small[4 + i]) for i in range(4)]
    return grads[:6] + [own_part(small[0:4].reshape(-1)), grads[6]] + parts


def shards(
    hidden_in,
    boxes,
    lengths,
    w_query,
    w_key,
    w_value,
    w_out,
    w_rel,
    w_up,
    b_up,
    w_down,
    gain_attn,
    bias_attn,
    gain_ffn,
    bias_ffn,
    cotangent,
):
    vectors = (b_up, gain_attn, bias_attn, gain_ffn, bias_ffn)
    weights = (
        ("w_query", w_query),
        ("w_key", w_key),
        ("w_value", w_value),
        ("w_out", w_out),
        ("w_rel", w_rel),
        ("w_up", w_up),
        ("w_down", w_down),
    )
    reduce = lax.axis_size("dp") == 8
    hidden, dinput, share, small = layer(
        lengths,
        hidden_in[:, 0],
        boxes[:, :, 0],
        cotangent[:, 0],
        vectors,
        weights,
        reduce,
    )
    if reduce:
        hidden, dinput, *rest = finish(share, small, hidden, dinput)
    else:
        rest = finish_any(share, small)
    return (hidden[:, None], dinput[:, None], *rest)


def solution(mesh):
    rows = P(None, "dp", "seq", None)
    placed = (rows, P(None, None, "dp", "seq"), P(None, "dp")) + (P(),) * 12 + (rows,)
    matrix, vector = P("dp", None), P("dp")
    return jax.shard_map(
        shards,
        mesh=mesh,
        in_specs=placed,
        out_specs=(rows, rows) + (matrix,) * 6 + (vector, matrix) + (vector,) * 4,
        check_vma=False,
    )
```
